32 devices in a mesh: head: 4 (over y, x), row: 8 (over z, core).
Axes of the slice: x: 2, y: 2, z: 4, core: 2. Of those that a mesh axis runs over, the one named last changes fastest.
Arguments:
- tokens: bfloat16 [48, 512, 1024], P('row', 'head'), may hold values from -6 to 6
- prev_logits: bfloat16 [48, 16, 512, 512], P('row', 'head'), may hold values from -6 to 6
- segment_ids: int32 [48, 512], P('row'), may hold values from 0 to 3, never falling along the last dimension, each value on 1 to 320 neighbouring positions
- w_qkv: bfloat16 [1024, 3, 1024], P(None, None, 'head'), may hold values from -0.1875 to 0.1875
- b_qv: bfloat16 [2, 1024], P(None, 'head'), may hold values from -3 to 3
- w_out: bfloat16 [1024, 1024], P('head'), may hold values from -1.5 to 1.5
- b_out: bfloat16 [1024], replicated, may hold values from -3 to 3
- ln1_gain: float32 [1024], replicated, may hold values from 0.5 to 1.5
- ln1_shift: float32 [1024], replicated, may hold values from -2 to 2
- w_in: bfloat16 [1024, 4096], P(None, ('head', 'row')), may hold values from -0.1875 to 0.1875
- b_in: bfloat16 [4096], P(('head', 'row')), may hold values from -3 to 3
- w_down: bfloat16 [4096, 1024], P(('head', 'row')), may hold values from -0.1875 to 0.1875
- b_down: bfloat16 [1024], replicated, may hold values from -2 to 2
- ln2_gain: float32 [1024], replicated, may hold values from 0.5 to 1.5
- ln2_shift: float32 [1024], replicated, may hold values from -2 to 2
- out_grad: bfloat16 [48, 512, 1024], P('row', 'head'), may hold values from -6 to 6
- logit_grad: bfloat16 [48, 16, 512, 512], P('row', 'head'), may hold values from -3 to 3
Outputs:
- layer_out: bfloat16 [48, 512, 1024], P('row', 'head')
- raw_logits: bfloat16 [48, 16, 512, 512], P('row', 'head')
- tokens_grad: float32 [48, 512, 1024], P('row', 'head')
- prev_grad: bfloat16 [48, 16, 512, 512], P('row', 'head')
- grad_w_qkv: float32 [1024, 3, 1024], P(None, None, 'head')
- grad_b_qv: float32 [2, 1024], P(None, 'head')
- grad_w_out: float32 [1024, 1024], P('head')
- grad_b_out: float32 [1024], replicated
- grad_ln1_gain: float32 [1024], replicated
- grad_ln1_shift: float32 [1024], replicated
- grad_w_in: float32 [1024, 4096], P(None, ('head', 'row'))
- grad_b_in: float32 [4096], P(('head', 'row'))
- grad_w_down: float32 [4096, 1024], P(('head', 'row'))
- grad_b_down: float32 [1024], replicated
- grad_ln2_gain: float32 [1024], replicated
- grad_ln2_shift: float32 [1024], replicated
The draws below stay inside these ranges and needn't reach their ends.
Inputs may be any that keep to these rules, and one draw needn't show every extreme that they name: `segment_ids`: in each row of 512 slots the ids never fall and each id covers 1 to 320 slots.
All inputs are finite; a program needn't handle non-finite values.
Results may differ from the reference program's by a relative error of at most 0.015.
Values may be sent and summed in bfloat16 or wider, within the bound.
No kernel may reach another device: no remote copies, remote signals or barrier semaphores. Data moves between devices by JAX's collectives and lax.ppermute only.
A program may use at most 256 MiB of HBM per device.

```python
import math
import jax
import jax.numpy as jnp
import numpy as np
from jax import lax

D = 1024
HEADS = 16
DH = 64
FF = 4096
SLOTS = 512
DOCS = 4
DOC_MOST = 320
ROWS = 48


def shard_levels(rng, shape, cuts, low, largest):
    level = 1.0
    for dim, parts in cuts:
        heights = jax.random.uniform(jax.random.fold_in(jax.random.fold_in(rng, 6), dim), (parts,), jnp.float32, low / len(cuts), largest / len(cuts))
        level = level * jnp.repeat(jnp.exp(heights), shape[dim] // parts).reshape((-1,) + (1,) * (len(shape) - 1 - dim))
    return level


def length_profile(count, total, bound, slope):
    weights = [(1 << 20) // math.isqrt(standing ** slope) + 1 for standing in range(2, count + 1)]
    rest, holding = total - bound - (count - 1), [1] * (count - 1)
    while rest > 0:
        free = [i for i in range(count - 1) if holding[i] < bound]
        pool, left = sum([weights[i] for i in free]), rest
        for i in free:
            extra = min(bound - holding[i], max(1, left * weights[i] // pool), rest)
            holding[i] = holding[i] + extra
            rest = rest - extra
    return np.array([bound] + holding)


def uneven_parts(rng, number_of, total, most, skew):
    if number_of == 2:
        one = jax.random.randint(rng, (), max(1, total - most), min(most, total - 1) + 1)
        return jnp.stack([one, total - one])
    tallies = jnp.asarray(length_profile(number_of, total, most, skew), jnp.int32)
    pairs = (number_of - 1) // 2
    giver, taker = tallies[1:1 + 2 * pairs:2], tallies[2:2 + 2 * pairs:2]
    slack = jnp.minimum(giver - 1, most - taker)
    moved = jax.random.randint(jax.random.fold_in(rng, 1), (pairs,), 0, 1 << 20) % (slack + 1)
    tallies = tallies.at[1:1 + 2 * pairs:2].set(giver - moved).at[2:2 + 2 * pairs:2].set(taker + moved)
    return tallies[jax.random.permutation(jax.random.fold_in(rng, 2), number_of)]


def scatter_about(stream_key, extent, scale, bound, cuts=(), kind=jnp.bfloat16):
    array = jax.random.normal(stream_key, extent, jnp.float32) * scale
    if len(cuts) > 0:
        array = shard_levels(stream_key, extent, cuts, -0.22, 0.18) * array
    return jnp.clip(array, min=-bound, max=bound).astype(kind)


def setup_inputs(seed: int = 0) -> dict:
    arg_keys = jax.random.split(jax.random.key(seed), 18)
    tokens = scatter_about(arg_keys[0], (ROWS, SLOTS, D), 1.0, 6.0, ((0, 8), (1, 4)))
    prev_logits = scatter_about(arg_keys[1], (ROWS, HEADS, SLOTS, SLOTS), 1.0, 6.0, ((0, 8), (1, 4)))
    segment_ids = jax.vmap(lambda own: jnp.searchsorted(jnp.cumsum(uneven_parts(own, DOCS, SLOTS, DOC_MOST, 2)), jnp.arange(SLOTS), side="right"))(jax.random.split(arg_keys[2], ROWS)).reshape((ROWS, SLOTS)).astype(jnp.int32)
    w_qkv = scatter_about(arg_keys[3], (D, 3, HEADS * DH), D ** -0.5, 0.1875, ((2, 4),))
    b_qv = scatter_about(arg_keys[4], (2, HEADS * DH), 0.5, 3.0, ((1, 4),))
    w_out = scatter_about(arg_keys[5], (HEADS * DH, D), (HEADS * DH // 64) ** -0.5, 1.5, ((0, 4),))
    b_out = scatter_about(arg_keys[6], (D,), 0.5, 3.0)
    ln1_gain = jnp.clip(1.0 + 0.1 * jax.random.normal(arg_keys[7], (D,), jnp.float32), 0.5, 1.5)
    ln1_shift = scatter_about(arg_keys[8], (D,), 0.3, 2.0, (), jnp.float32)
    w_in = scatter_about(arg_keys[9], (D, FF), D ** -0.5, 0.1875, ((1, 32),))
    b_in = scatter_about(arg_keys[10], (FF,), 0.5, 3.0, ((0, 32),))
    w_down = scatter_about(arg_keys[11], (FF, D), (FF // 4) ** -0.5, 0.1875, ((0, 32),))
    b_down = scatter_about(arg_keys[12], (D,), 0.3, 2.0)
    ln2_gain = jnp.clip(1.0 + 0.1 * jax.random.normal(arg_keys[13], (D,), jnp.float32), 0.5, 1.5)
    ln2_shift = scatter_about(arg_keys[14], (D,), 0.3, 2.0, (), jnp.float32)
    out_grad = scatter_about(arg_keys[15], (ROWS, SLOTS, D), 1.0, 6.0, ((0, 8), (1, 4)))
    logit_grad = scatter_about(arg_keys[16], (ROWS, HEADS, SLOTS, SLOTS), 0.5, 3.0, ((0, 8), (1, 4)))
    return {"tokens": tokens, "prev_logits": prev_logits, "segment_ids": segment_ids, "w_qkv": w_qkv, "b_qv": b_qv, "w_out": w_out, "b_out": b_out, "ln1_gain": ln1_gain, "ln1_shift": ln1_shift, "w_in": w_in, "b_in": b_in, "w_down": w_down, "b_down": b_down, "ln2_gain": ln2_gain, "ln2_shift": ln2_shift, "out_grad": out_grad, "logit_grad": logit_grad}


@jax.custom_vjp
def low(v):
    return lax.optimization_barrier(v.astype(jnp.bfloat16)).astype(jnp.float32)

@jax.custom_vjp
def low_back(v):
    return v

def low_keep(v):
    return (low(v), None)

def low_pass(kept, grad):
    return (grad,)

def back_keep(v):
    return (v, None)

def back_low(kept, grad):
    return (low(grad),)
low.defvjp(low_keep, low_pass)
low_back.defvjp(back_keep, back_low)
norm_eps = 1e-12
masked_fill = -1000000000.0
highest = lax.Precision.HIGHEST

def layer_norm(values_in, gain_vec, shift_vec):
    center = lax.optimization_barrier(jnp.mean(values_in, axis=-1, keepdims=True))
    offset = values_in - center
    spread = lax.optimization_barrier(jnp.mean(offset * offset, axis=-1, keepdims=True))
    return offset * lax.rsqrt(spread + norm_eps) * gain_vec + shift_vec

def layer_block(tok_blk, prev_blk, seg_blk, weights):
    w_qkv, b_qv, w_out, b_out, ln1_gain, ln1_shift, w_in, b_in, w_down, b_down, ln2_gain, ln2_shift = weights
    rows_blk = tok_blk.shape[0]
    token_flat = tok_blk.reshape(rows_blk * SLOTS, D)
    bias_full = jnp.concatenate([b_qv[0:1], jnp.zeros((1, HEADS * DH), jnp.float32), b_qv[1:2]], axis=0)
    projected = jnp.einsum('td,dcf->tcf', token_flat, w_qkv, precision=highest) + bias_full[None]
    projected = low(low_back(projected)).reshape(rows_blk, SLOTS, 3, HEADS, DH)
    queries = projected[:, :, 0]
    key_rows = projected[:, :, 1]
    value_rows = projected[:, :, 2]
    raw_scores = jnp.einsum('rihe,rjhe->rhij', queries, key_rows, precision=highest) * DH ** (-0.5) + prev_blk
    raw_scores = low_back(raw_scores)
    same_doc = seg_blk[:, :, None] == seg_blk[:, None, :]
    masked = jnp.where(same_doc[:, None], raw_scores, masked_fill)
    row_top = lax.optimization_barrier(jnp.max(masked, axis=-1, keepdims=True))
    shifted = jnp.exp(masked - row_top)
    attn_probs = low(shifted / lax.optimization_barrier(jnp.sum(shifted, axis=-1, keepdims=True)))
    context = jnp.einsum('rhij,rjhe->rihe', attn_probs, value_rows, precision=highest)
    context = low(low_back(context.reshape(rows_blk * SLOTS, HEADS * DH)))
    branch = low_back(jnp.dot(context, w_out, precision=highest) + b_out)
    normed_one = layer_norm(token_flat + branch, ln1_gain, ln1_shift)
    hidden_pre = low_back(jnp.dot(low(normed_one), w_in, precision=highest) + b_in)
    active = low(jax.nn.gelu(hidden_pre, approximate=False))
    ffn_out = low_back(jnp.dot(active, w_down, precision=highest) + b_down)
    result = layer_norm(normed_one + ffn_out, ln2_gain, ln2_shift)
    return (result.reshape(rows_blk, SLOTS, D), raw_scores)

def reference(tokens, prev_logits, segment_ids, w_qkv, b_qv, w_out, b_out, ln1_gain, ln1_shift, w_in, b_in, w_down, b_down, ln2_gain, ln2_shift, out_grad, logit_grad):
    params = tuple((member.astype(jnp.float32) for member in (w_qkv, b_qv, w_out, b_out, ln1_gain, ln1_shift, w_in, b_in, w_down, b_down, ln2_gain, ln2_shift)))
    group = math.gcd(ROWS, 8)
    blocks = ROWS // group
    tok_f = tokens.astype(jnp.float32).reshape(blocks, group, SLOTS, D)
    prev_f = prev_logits.astype(jnp.float32).reshape(blocks, group, HEADS, SLOTS, SLOTS)
    seg_blocks = segment_ids.reshape(blocks, group, SLOTS)

    def forward(tok_in, prev_in, weights):

        def one_block(pieces):
            return layer_block(pieces[0], pieces[1], pieces[2], weights)
        return lax.map(jax.checkpoint(one_block), (tok_in, prev_in, seg_blocks))
    (out_f, raw_f), pullback = jax.vjp(forward, tok_f, prev_f, params)
    grad_tok, grad_prev, grad_params = pullback((out_grad.astype(jnp.float32).reshape(blocks, group, SLOTS, D), logit_grad.astype(jnp.float32).reshape(blocks, group, HEADS, SLOTS, SLOTS)))
    return (out_f.reshape(ROWS, SLOTS, D).astype(jnp.bfloat16), raw_f.reshape(ROWS, HEADS, SLOTS, SLOTS).astype(jnp.bfloat16), grad_tok.reshape(ROWS, SLOTS, D), grad_prev.reshape(ROWS, HEADS, SLOTS, SLOTS).astype(jnp.bfloat16), grad_params[0], grad_params[1], grad_params[2], grad_params[3], grad_params[4], grad_params[5], grad_params[6], grad_params[7], grad_params[8], grad_params[9], grad_params[10], grad_params[11])
```

```python
import functools

import jax
import jax.numpy as jnp
from jax import lax
from jax.experimental import pallas as pl
from jax.experimental.pallas import tpu as pltpu
from jax.sharding import PartitionSpec as P

norm_eps = 1e-12
masked_fill = -1000000000.0
head_dim = 64
hidden_block = 512
bf16 = jnp.bfloat16
f32 = jnp.float32


def dot_nn(a, b):
    return lax.dot_general(a, b, (((1,), (0,)), ((), ())), preferred_element_type=f32)


def dot_nt(a, b):
    return lax.dot_general(a, b, (((1,), (1,)), ((), ())), preferred_element_type=f32)


def dot_tn(a, b):
    return lax.dot_general(a, b, (((0,), (0,)), ((), ())), preferred_element_type=f32)


def params(limit_mib=60):
    return pltpu.CompilerParams(
        dimension_semantics=("arbitrary",), vmem_limit_bytes=limit_mib * 1024 * 1024
    )


def whole(shape):
    return pl.BlockSpec(shape, lambda *_: (0,) * len(shape))


def by_step(shape, axis=0):
    return pl.BlockSpec(shape, lambda t, *_: tuple(t if d == axis else 0 for d in range(len(shape))))


def norm_parts(values):
    center = jnp.mean(values, axis=-1, keepdims=True)
    offset = values - center
    inverse = lax.rsqrt(jnp.mean(offset * offset, axis=-1, keepdims=True) + norm_eps)
    return offset * inverse, inverse


def norm_back(grad_in, unit_vals, inverse, gain_vec):
    scaled = grad_in * gain_vec
    return inverse * (
        scaled
        - jnp.mean(scaled, axis=-1, keepdims=True)
        - unit_vals * jnp.mean(scaled * unit_vals, axis=-1, keepdims=True)
    )


def lane_halves():
    lane = lax.broadcasted_iota(jnp.int32, (1, 2 * head_dim), 1)
    return lane < head_dim


def attend(me, tok_pieces, w_flat, bias_row, seg_row, seg_col, prev):
    rows, heads, slots, _ = prev.shape
    nh = len(tok_pieces)
    _, part, width = tok_pieces[0].shape
    cols = heads * head_dim
    step = 128
    scale = head_dim ** (-0.5)

    def body(me_ref, *refs):
        toks = refs[:nh]
        w_ref, b_ref, sr_ref, sc_ref, prev_ref = refs[nh : nh + 5]
        qkv_ref, raw_ref, ctx_ref, lse_ref, tok_all, ctx_all = refs[nh + 5 :]
        mine = me_ref[0]
        for k in range(nh):
            tok_all[pl.ds(pl.multiple_of((mine ^ k) * part, part), part), :] = toks[k][0]
        qkv_ref[0] = (dot_nn(tok_all[...], w_ref[...]) + b_ref[...]).astype(bf16)
        low_half = lane_halves()
        keep = [jnp.where(low_half, scale, 0.0).astype(bf16), jnp.where(low_half, 0.0, scale).astype(bf16)]
        lane = lax.broadcasted_iota(jnp.int32, (step, 128), 1)

        def block(i, carry):
            at = pl.ds(pl.multiple_of(i * step, step), step)
            same = sc_ref[0, at, :] == sr_ref[0]
            lse_tile = jnp.zeros((step, 128), f32)
            for pair in range(heads // 2):
                span = slice(pair * 128, pair * 128 + 128)
                q_pair = qkv_ref[0, at, span]
                k_pair = qkv_ref[0, :, cols + pair * 128 : cols + pair * 128 + 128]
                v_pair = qkv_ref[0, :, 2 * cols + pair * 128 : 2 * cols + pair * 128 + 128]
                outs = []
                for half in range(2):
                    h = 2 * pair + half
                    raw = dot_nt(q_pair * keep[half], k_pair) + prev_ref[0, h, at, :].astype(f32)
                    raw_ref[0, h, at, :] = raw.astype(bf16)
                    masked = jnp.where(same, raw, masked_fill)
                    top = jnp.max(masked, axis=-1, keepdims=True)
                    grown = jnp.exp(masked - top)
                    total = jnp.sum(grown, axis=-1, keepdims=True)
                    probs = (grown * (1.0 / total)).astype(bf16)
                    outs.append(dot_nn(probs, v_pair))
                    lse_tile = jnp.where(lane == h, top + jnp.log(total), lse_tile)
                ctx_all[at, span] = jnp.where(low_half, outs[0], outs[1]).astype(bf16)
            lse_ref[0, at, :] = lse_tile
            return carry

        lax.fori_loop(0, slots // step, block, 0)
        for k in range(nh):
            ctx_ref[k, 0] = ctx_all[pl.ds(pl.multiple_of((mine ^ k) * part, part), part), :]

    return pl.pallas_call(
        body,
        grid_spec=pltpu.PrefetchScalarGridSpec(
            num_scalar_prefetch=1,
            grid=(rows,),
            in_specs=[by_step((1, part, width))] * nh
            + [
                whole((width, 3 * cols)),
                whole((1, 3 * cols)),
                by_step((1, 1, slots)),
                by_step((1, slots, 1)),
                by_step((1, heads, slots, slots)),
            ],
            out_specs=[
                by_step((1, slots, 3 * cols)),
                by_step((1, heads, slots, slots)),
                by_step((nh, 1, part, cols), 1),
                by_step((1, slots, 128)),
            ],
            scratch_shapes=[pltpu.VMEM((slots, width), bf16), pltpu.VMEM((slots, cols), bf16)],
        ),
        out_shape=[
            jax.ShapeDtypeStruct((rows, slots, 3 * cols), bf16),
            jax.ShapeDtypeStruct((rows, heads, slots, slots), bf16),
            jax.ShapeDtypeStruct((nh, rows, part, cols), bf16),
            jax.ShapeDtypeStruct((rows, slots, 128), f32),
        ],
        compiler_params=params(),
        name="attend",
    )(me, *tok_pieces, w_flat, bias_row, seg_row, seg_col, prev)


def attend_back(me, tok_pieces, ctx_grads, qkv, prev, logit_grad, seg_row, seg_col, lse, w_flat):
    rows, heads, slots, _ = prev.shape
    nh = len(tok_pieces)
    _, part, width = tok_pieces[0].shape
    cols = heads * head_dim
    step = 128
    scale = head_dim ** (-0.5)

    def body(me_ref, *refs):
        toks, grads = refs[:nh], refs[nh : 2 * nh]
        qkv_ref, prev_ref, lg_ref, sr_ref, sc_ref, lse_ref, w_ref = refs[2 * nh : 2 * nh + 7]
        pg_ref, in_ref, gw_ref, gb_ref, tok_all, go_all, p_all, dt_all, in_all = refs[2 * nh + 7 :]
        mine = me_ref[0]
        for k in range(nh):
            at = pl.ds(pl.multiple_of((mine ^ k) * part, part), part)
            tok_all[at, :] = toks[k][0]
            go_all[at, :] = grads[k][0]
        low_half = lane_halves()
        keep_q = [jnp.where(low_half, scale, 0.0).astype(bf16), jnp.where(low_half, 0.0, scale).astype(bf16)]
        keep_g = [jnp.where(low_half, 1.0, 0.0).astype(bf16), jnp.where(low_half, 0.0, 1.0).astype(bf16)]

        def block(i, carry):
            at = pl.ds(pl.multiple_of(i * step, step), step)
            same = sc_ref[0, at, :] == sr_ref[0]
            lse_tile = lse_ref[0, at, :]
            for pair in range(heads // 2):
                span = slice(pair * 128, pair * 128 + 128)
                q_pair = qkv_ref[0, at, span]
                g_pair = go_all[at, span]
                k_pair = qkv_ref[0, :, cols + pair * 128 : cols + pair * 128 + 128]
                v_pair = qkv_ref[0, :, 2 * cols + pair * 128 : 2 * cols + pair * 128 + 128]
                for half in range(2):
                    h = 2 * pair + half
                    raw = dot_nt(q_pair * keep_q[half], k_pair) + prev_ref[0, h, at, :].astype(f32)
                    probs = jnp.exp(jnp.where(same, raw, masked_fill) - lse_tile[:, h : h + 1])
                    p_all[h, at, :] = probs.astype(bf16)
                    pulled = probs * dot_nt(g_pair * keep_g[half], v_pair)
                    inner = jnp.sum(pulled, axis=-1, keepdims=True)
                    pg_ref[0, h, at, :] = (pulled - probs * inner + lg_ref[0, h, at, :].astype(f32)).astype(bf16)
            return carry

        lax.fori_loop(0, slots // step, block, 0)
        q_t = qkv_ref[0, :, :cols].T
        k_t = qkv_ref[0, :, cols : 2 * cols].T
        g_t = go_all[...].T
        for h in range(heads):
            span = slice(h * head_dim, h * head_dim + head_dim)
            grad_raw = pg_ref[0, h]
            dt_all[h * head_dim : (h + 1) * head_dim, :] = (dot_nt(k_t[span], grad_raw) * scale).astype(bf16)
            dt_all[cols + h * head_dim : cols + (h + 1) * head_dim, :] = (dot_nn(q_t[span], grad_raw) * scale).astype(bf16)
            dt_all[2 * cols + h * head_dim : 2 * cols + (h + 1) * head_dim, :] = dot_nn(g_t[span], p_all[h]).astype(bf16)
        grad_qkv = dt_all[...].T
        in_all[...] = dot_nt(grad_qkv, w_ref[...]).astype(bf16)
        for k in range(nh):
            in_ref[k, 0] = in_all[pl.ds(pl.multiple_of((mine ^ k) * part, part), part), :]
        gw = dot_nn(dt_all[...], tok_all[...])
        gb = dot_nn(jnp.ones((8, slots), bf16), grad_qkv)

        @pl.when(pl.program_id(0) == 0)
        def _():
            gw_ref[...] = gw
            gb_ref[...] = gb

        @pl.when(pl.program_id(0) > 0)
        def _():
            gw_ref[...] += gw
            gb_ref[...] += gb

    return pl.pallas_call(
        body,
        grid_spec=pltpu.PrefetchScalarGridSpec(
            num_scalar_prefetch=1,
            grid=(rows,),
            in_specs=[by_step((1, part, width))] * nh
            + [by_step((1, part, cols))] * nh
            + [
                by_step((1, slots, 3 * cols)),
                by_step((1, heads, slots, slots)),
                by_step((1, heads, slots, slots)),
                by_step((1, 1, slots)),
                by_step((1, slots, 1)),
                by_step((1, slots, 128)),
                whole((width, 3 * cols)),
            ],
            out_specs=[
                by_step((1, heads, slots, slots)),
                by_step((nh, 1, part, width), 1),
                whole((3 * cols, width)),
                whole((8, 3 * cols)),
            ],
            scratch_shapes=[
                pltpu.VMEM((slots, width), bf16),
                pltpu.VMEM((slots, cols), bf16),
                pltpu.VMEM((heads, slots, slots), bf16),
                pltpu.VMEM((3 * cols, slots), bf16),
                pltpu.VMEM((slots, width), bf16),
            ],
        ),
        out_shape=[
            jax.ShapeDtypeStruct((rows, heads, slots, slots), bf16),
            jax.ShapeDtypeStruct((nh, rows, part, width), bf16),
            jax.ShapeDtypeStruct((3 * cols, width), f32),
            jax.ShapeDtypeStruct((8, 3 * cols), f32),
        ],
        compiler_params=params(),
        name="attend_back",
    )(me, *tok_pieces, *ctx_grads, qkv, prev, logit_grad, seg_row, seg_col, lse, w_flat)


def weight_stream(refs, counts, per_block, buf, sem):
    total = sum(counts)
    t = pl.program_id(0)

    def start(which):
        low = 0
        for ref, count in zip(refs, counts):

            @pl.when((which >= low) & (which < low + count))
            def _(ref=ref, low=low):
                pltpu.make_async_copy(
                    ref.at[pl.ds((which - low) * per_block, per_block)], buf.at[which % 2], sem.at[which % 2]
                ).start()

            low += count

    @pl.when(t == 0)
    def _():
        start(t)

    pltpu.make_async_copy(refs[0].at[pl.ds(0, per_block)], buf.at[t % 2], sem.at[t % 2]).wait()

    @pl.when(t + 1 < total)
    def _():
        start(t + 1)

    return t % 2


def feed_forward(ctx_pieces, out_pieces, tokens, vectors, bias_blocks, weights, out_grad):
    count, width = tokens.shape
    nh = len(ctx_pieces)
    cols = ctx_pieces[0].shape[1]
    shard = weights[0].shape[2]
    per_block = hidden_block // shard
    counts = [w.shape[0] // per_block for w in weights]
    blocks = sum(counts)
    hidden = blocks * hidden_block
    tile = count // 3
    nw = len(weights)

    def body(*refs):
        ctx, outs = refs[:nh], refs[nh : 2 * nh]
        tok_ref, vec_ref, bias_ref, og_ref = refs[2 * nh : 2 * nh + 4]
        w_refs = refs[2 * nh + 4 : 2 * nh + 4 + nw]
        res_ref, x_ref, unit_ref, inv_ref, g2_ref, gf_ref, act_ref, slope_ref, sum_ref = refs[
            2 * nh + 4 + nw : 2 * nh + 13 + nw
        ]
        nrm, acc, buf, sem = refs[2 * nh + 13 + nw :]
        t = pl.program_id(0)
        slot = weight_stream(w_refs, counts, per_block, buf, sem)

        @pl.when(t == 0)
        def _():
            branch = vec_ref[0:1, :] + dot_nn(ctx[0][...], outs[0][...])
            for k in range(1, nh):
                branch = branch + dot_nn(ctx[k][...], outs[k][...])
            unit_one, inverse = norm_parts(tok_ref[...].astype(f32) + branch)
            unit_ref[...] = unit_one
            inv_ref[...] = jnp.broadcast_to(inverse, (count, 128))
            normed = unit_one * vec_ref[1:2, :] + vec_ref[2:3, :]
            nrm[...] = normed
            x_ref[...] = normed.astype(bf16)
            acc[...] = jnp.zeros_like(acc)

        w_in = buf[slot, :, 0].reshape(hidden_block, width)
        w_down = buf[slot, :, 1].reshape(hidden_block, width)
        for m in range(3):
            at = slice(m * tile, m * tile + tile)
            pre = dot_nt(x_ref[at, :], w_in) + bias_ref[0]
            below = 0.5 * (1.0 + lax.erf(pre * (0.5**0.5)))
            active = (pre * below).astype(bf16)
            act_ref[at, :] = active
            slope_ref[at, :] = (below + pre * (jnp.exp(-0.5 * pre * pre) * 0.3989422804014327)).astype(bf16)
            acc[at, :] += dot_nn(active, w_down)

        @pl.when(t == blocks - 1)
        def _():
            unit_two, inverse = norm_parts(nrm[...] + acc[...] + vec_ref[3:4, :])
            res_ref[...] = (unit_two * vec_ref[4:5, :] + vec_ref[5:6, :]).astype(bf16)
            top = og_ref[...].astype(f32)
            grad_two = norm_back(top, unit_two, inverse, vec_ref[4:5, :])
            g2_ref[...] = grad_two
            low = grad_two.astype(bf16)
            gf_ref[...] = low
            sum_ref[0:1, :] = jnp.sum(top * unit_two, axis=0, keepdims=True)
            sum_ref[1:2, :] = jnp.sum(top, axis=0, keepdims=True)
            sum_ref[2:3, :] = jnp.sum(low.astype(f32), axis=0, keepdims=True)
            sum_ref[3:8, :] = jnp.zeros((5, width), f32)

    return pl.pallas_call(
        body,
        grid=(blocks,),
        in_specs=[whole((count, cols))] * nh
        + [whole((cols, width))] * nh
        + [whole((count, width)), whole((8, width)), by_step((1, 1, hidden_block)), whole((count, width))]
        + [pl.BlockSpec(memory_space=pl.ANY)] * nw,
        out_specs=[
            whole((count, width)),
            whole((count, width)),
            whole((count, width)),
            whole((count, 128)),
            whole((count, width)),
            whole((count, width)),
            by_step((count, hidden_block), 1),
            by_step((count, hidden_block), 1),
            whole((8, width)),
        ],
        out_shape=[
            jax.ShapeDtypeStruct((count, width), bf16),
            jax.ShapeDtypeStruct((count, width), bf16),
            jax.ShapeDtypeStruct((count, width), f32),
            jax.ShapeDtypeStruct((count, 128), f32),
            jax.ShapeDtypeStruct((count, width), f32),
            jax.ShapeDtypeStruct((count, width), bf16),
            jax.ShapeDtypeStruct((count, hidden), bf16),
            jax.ShapeDtypeStruct((count, hidden), bf16),
            jax.ShapeDtypeStruct((8, width), f32),
        ],
        scratch_shapes=[
            pltpu.VMEM((count, width), f32),
            pltpu.VMEM((count, width), f32),
            pltpu.VMEM((2, per_block, 2, shard, width), bf16),
            pltpu.SemaphoreType.DMA((2,)),
        ],
        compiler_params=params(),
        name="feed_forward",
    )(*ctx_pieces, *out_pieces, tokens, vectors, bias_blocks, out_grad, *weights)


def feed_back(ctx_pieces, out_pieces, grad_two, grad_ffn, slope, unit_one, inv_one, vectors, weights):
    count, width = grad_two.shape
    nh = len(ctx_pieces)
    cols = ctx_pieces[0].shape[1]
    shard = weights[0].shape[2]
    per_block = hidden_block // shard
    counts = [w.shape[0] // per_block for w in weights]
    blocks = sum(counts)
    hidden = blocks * hidden_block
    tile = count // 3
    nw = len(weights)

    def body(*refs):
        ctx, outs = refs[:nh], refs[nh : 2 * nh]
        g2_ref, gf_ref, slope_ref, unit_ref, inv_ref, vec_ref = refs[2 * nh : 2 * nh + 6]
        w_refs = refs[2 * nh + 6 : 2 * nh + 6 + nw]
        res_ref, gc_ref, gwo_ref, gh_ref, gb_ref, sum_ref, acc, buf, sem = refs[2 * nh + 6 + nw :]
        t = pl.program_id(0)
        slot = weight_stream(w_refs, counts, per_block, buf, sem)

        @pl.when(t == 0)
        def _():
            acc[...] = g2_ref[...]

        w_in = buf[slot, :, 0].reshape(hidden_block, width)
        w_down = buf[slot, :, 1].reshape(hidden_block, width)
        total = jnp.zeros((1, hidden_block), f32)
        for m in range(3):
            at = slice(m * tile, m * tile + tile)
            grad_hidden = (dot_nt(gf_ref[at, :], w_down) * slope_ref[at, :].astype(f32)).astype(bf16)
            gh_ref[at, :] = grad_hidden
            total = total + jnp.sum(grad_hidden.astype(f32), axis=0, keepdims=True)
            acc[at, :] += dot_nn(grad_hidden, w_in)
        gb_ref[0] = total

        @pl.when(t == blocks - 1)
        def _():
            grad_one = acc[...]
            unit_one = unit_ref[...]
            grad_res = norm_back(grad_one, unit_one, inv_ref[:, 0:1], vec_ref[1:2, :])
            res_ref[...] = grad_res
            low = grad_res.astype(bf16)
            sum_ref[0:1, :] = jnp.sum(grad_one * unit_one, axis=0, keepdims=True)
            sum_ref[1:2, :] = jnp.sum(grad_one, axis=0, keepdims=True)
            sum_ref[2:3, :] = jnp.sum(low.astype(f32), axis=0, keepdims=True)
            sum_ref[3:8, :] = jnp.zeros((5, width), f32)
            for k in range(nh):
                gc_ref[k] = dot_nt(low, outs[k][...]).astype(bf16)
                gwo_ref[k] = dot_tn(ctx[k][...], low).astype(bf16)

    return pl.pallas_call(
        body,
        grid=(blocks,),
        in_specs=[whole((count, cols))] * nh
        + [whole((cols, width))] * nh
        + [
            whole((count, width)),
            whole((count, width)),
            by_step((count, hidden_block), 1),
            whole((count, width)),
            whole((count, 128)),
            whole((8, width)),
        ]
        + [pl.BlockSpec(memory_space=pl.ANY)] * nw,
        out_specs=[
            whole((count, width)),
            whole((nh, count, cols)),
            whole((nh, cols, width)),
            by_step((count, hidden_block), 1),
            by_step((1, 1, hidden_block)),
            whole((8, width)),
        ],
        out_shape=[
            jax.ShapeDtypeStruct((count, width), f32),
            jax.ShapeDtypeStruct((nh, count, cols), bf16),
            jax.ShapeDtypeStruct((nh, cols, width), bf16),
            jax.ShapeDtypeStruct((count, hidden), bf16),
            jax.ShapeDtypeStruct((blocks, 1, hidden_block), f32),
            jax.ShapeDtypeStruct((8, width), f32),
        ],
        scratch_shapes=[
            pltpu.VMEM((count, width), f32),
            pltpu.VMEM((2, per_block, 2, shard, width), bf16),
            pltpu.SemaphoreType.DMA((2,)),
        ],
        compiler_params=params(),
        name="feed_back",
    )(*ctx_pieces, *out_pieces, grad_two, grad_ffn, slope, unit_one, inv_one, vectors, *weights)


def weight_grads(x_low, grad_ffn, grad_hidden, active, first, blocks, shard):
    count, width = x_low.shape
    per_block = hidden_block // shard

    def body(x_ref, gf_ref, gh_ref, act_ref, out_ref):
        out_ref[:, 0] = dot_tn(gh_ref[...], x_ref[...]).astype(bf16).reshape(per_block, shard, width)
        out_ref[:, 1] = dot_tn(act_ref[...], gf_ref[...]).astype(bf16).reshape(per_block, shard, width)

    return pl.pallas_call(
        body,
        grid=(blocks,),
        in_specs=[
            whole((count, width)),
            whole((count, width)),
            pl.BlockSpec((count, hidden_block), lambda t: (0, first + t)),
            pl.BlockSpec((count, hidden_block), lambda t: (0, first + t)),
        ],
        out_specs=by_step((per_block, 2, shard, width)),
        out_shape=jax.ShapeDtypeStruct((blocks * per_block, 2, shard, width), bf16),
        compiler_params=params(),
        name="weight_grads",
    )(x_low, grad_ffn, grad_hidden, active)


def per_device(
    nh,
    tokens,
    prev_logits,
    segment_ids,
    w_qkv,
    b_qv,
    w_out,
    b_out,
    ln1_gain,
    ln1_shift,
    w_in,
    b_in,
    w_down,
    b_down,
    ln2_gain,
    ln2_shift,
    out_grad,
    logit_grad,
):
    rows, part, width = tokens.shape
    heads = prev_logits.shape[1]
    slots = prev_logits.shape[2]
    cols = heads * head_dim
    shard = w_in.shape[1]
    count = rows * part
    me = lax.axis_index("head").astype(jnp.int32).reshape(1)

    def swap(value, k):
        return lax.ppermute(value, "head", [(i, i ^ k) for i in range(nh)])

    tok_pieces = [tokens] + [swap(tokens, k) for k in range(1, nh)]
    out_pieces = [w_out] + [swap(w_out, k) for k in range(1, nh)]
    weights = lax.all_gather(jnp.stack([w_in.T, w_down])[None], ("head", "row"), axis=0, tiled=True)
    bias_all = lax.all_gather(b_in.astype(f32), ("head", "row"), axis=0, tiled=True)
    bias_blocks = bias_all.reshape(-1, 1, hidden_block)
    blocks = bias_blocks.shape[0]
    vectors = jnp.stack(
        [
            b_out.astype(f32),
            ln1_gain,
            ln1_shift,
            b_down.astype(f32),
            ln2_gain,
            ln2_shift,
            jnp.zeros_like(ln1_gain),
            jnp.zeros_like(ln1_gain),
        ]
    )
    bias_qv = b_qv.astype(f32)
    bias_row = jnp.concatenate([bias_qv[0], jnp.zeros_like(bias_qv[0]), bias_qv[1]])[None]
    w_flat = w_qkv.reshape(width, 3 * cols)
    seg_row = segment_ids[:, None, :]
    seg_col = segment_ids[:, :, None]

    qkv, raw_logits, ctx, lse = attend(me, tok_pieces, w_flat, bias_row, seg_row, seg_col, prev_logits)
    ctx = ctx.reshape(nh, count, cols)
    ctx_pieces = [ctx[0]] + [swap(ctx[k], k) for k in range(1, nh)]
    flat_tokens = tokens.reshape(count, width)
    layer_out, x_low, unit_one, inv_one, grad_two, grad_ffn, active, slope, sums_two = feed_forward(
        ctx_pieces, out_pieces, flat_tokens, vectors, bias_blocks, [weights], out_grad.reshape(count, width)
    )
    grad_res, ctx_grad, gwo, grad_hidden, gb_in, sums_one = feed_back(
        ctx_pieces, out_pieces, grad_two, grad_ffn, slope, unit_one, inv_one, vectors, [weights]
    )
    ctx_grad = ctx_grad.reshape(nh, rows, part, cols)
    ctx_grads = [ctx_grad[0]] + [swap(ctx_grad[k], k) for k in range(1, nh)]
    ffn_grads = weight_grads(x_low, grad_ffn, grad_hidden, active, 0, blocks, shard)
    own_grads = lax.psum_scatter(ffn_grads, ("head", "row"), scatter_dimension=0, tiled=True)

    prev_grad, input_part, gw, gb = attend_back(
        me, tok_pieces, ctx_grads, qkv, prev_logits, logit_grad, seg_row, seg_col, lse, w_flat
    )
    received = [swap(input_part[k], k).astype(f32) for k in range(1, nh)]
    tokens_grad = grad_res.reshape(rows, part, width) + input_part[0].astype(f32)
    for piece in received:
        tokens_grad = tokens_grad + piece
    gwo_sum = gwo[0].astype(f32)
    for k in range(1, nh):
        gwo_sum = gwo_sum + swap(gwo[k], k).astype(f32)
    grad_w_qkv, grad_w_out = lax.psum((gw.T.astype(bf16), gwo_sum.astype(bf16)), "row")
    grad_w_qkv = grad_w_qkv.astype(f32).reshape(width, 3, cols)
    grad_b_qv = lax.psum(jnp.stack([gb[0, :cols], gb[0, 2 * cols :]]), "row")
    totals, grad_b_in = lax.psum(
        (jnp.concatenate([sums_two[:3], sums_one[:3]]), gb_in.reshape(-1)), ("head", "row")
    )
    place = lax.axis_index(("head", "row"))
    grad_b_in = lax.dynamic_slice_in_dim(grad_b_in, place * shard, shard)
    return (
        layer_out.reshape(rows, part, width),
        raw_logits,
        tokens_grad,
        prev_grad,
        grad_w_qkv,
        grad_b_qv,
        grad_w_out.astype(f32),
        totals[5],
        totals[3],
        totals[4],
        own_grads[0, 0].astype(f32).T,
        grad_b_in,
        own_grads[0, 1].astype(f32),
        totals[2],
        totals[0],
        totals[1],
    )


def solution(mesh):
    placed = (
        P("row", "head", None),
        P("row", "head", None, None),
        P("row", None),
        P(None, None, "head"),
        P(None, "head"),
        P("head", None),
        P(),
        P(),
        P(),
        P(None, ("head", "row")),
        P(("head", "row")),
        P(("head", "row"), None),
        P(),
        P(),
        P(),
        P("row", "head", None),
        P("row", "head", None, None),
    )
    return jax.shard_map(
        functools.partial(per_device, mesh.shape["head"]),
        mesh=mesh,
        in_specs=placed,
        out_specs=(
            P("row", "head", None),
            P("row", "head", None, None),
            P("row", "head", None),
            P("row", "head", None, None),
            P(None, None, "head"),
            P(None, "head"),
            P("head", None),
            P(),
            P(),
            P(),
            P(None, ("head", "row")),
            P(("head", "row")),
            P(("head", "row"), None),
            P(),
            P(),
            P(),
        ),
        check_vma=False,
    )
```

```python
import functools

import jax
import jax.numpy as jnp
from jax import lax
from jax.experimental import pallas as pl
from jax.experimental.pallas import tpu as pltpu
from jax.sharding import Mesh
from jax.sharding import PartitionSpec as P

norm_eps = 1e-12
masked_fill = -1000000000.0
head_dim = 64
hidden_block = 512
bf16 = jnp.bfloat16
f32 = jnp.float32


def dot_nn(a, b):
    return lax.dot_general(a, b, (((1,), (0,)), ((), ())), preferred_element_type=f32)


def dot_nt(a, b):
    return lax.dot_general(a, b, (((1,), (1,)), ((), ())), preferred_element_type=f32)


def dot_tn(a, b):
    return lax.dot_general(a, b, (((0,), (0,)), ((), ())), preferred_element_type=f32)


def params(limit_mib=60):
    return pltpu.CompilerParams(
        dimension_semantics=("arbitrary",), vmem_limit_bytes=limit_mib * 1024 * 1024
    )


def cost(flops, nbytes, exps=0):
    return pl.CostEstimate(flops=int(flops), bytes_accessed=int(nbytes), transcendentals=int(exps))


def whole(shape):
    return pl.BlockSpec(shape, lambda *_: (0,) * len(shape))


def by_step(shape, axis=0):
    return pl.BlockSpec(shape, lambda t, *_: tuple(t if d == axis else 0 for d in range(len(shape))))


def norm_parts(values):
    center = jnp.mean(values, axis=-1, keepdims=True)
    offset = values - center
    inverse = lax.rsqrt(jnp.mean(offset * offset, axis=-1, keepdims=True) + norm_eps)
    return offset * inverse, inverse


def norm_back(grad_in, unit_vals, inverse, gain_vec):
    scaled = grad_in * gain_vec
    return inverse * (
        scaled
        - jnp.mean(scaled, axis=-1, keepdims=True)
        - unit_vals * jnp.mean(scaled * unit_vals, axis=-1, keepdims=True)
    )


def lane_halves():
    lane = lax.broadcasted_iota(jnp.int32, (1, 2 * head_dim), 1)
    return lane < head_dim


def attend(me, first, pieces, w_flat, bias_row, seg_row, seg_col, prev, raw_so_far):
    total_rows, heads, slots, _ = prev.shape
    rows, _, width = pieces[0][2].shape
    cols = heads * head_dim
    nh = len({k for k, _, _ in pieces})
    part = slots // nh
    step = 128
    scale = head_dim ** (-0.5)
    np_ = len(pieces)
    places = [(k, off, p.shape[1]) for k, off, p in pieces]
    chained = raw_so_far is not None

    def body(me_ref, *refs):
        toks = refs[:np_]
        w_ref, b_ref, sr_ref, sc_ref, prev_ref = refs[np_ : np_ + 5]
        outs = refs[np_ + 5 + chained :]
        qkv_ref, raw_ref, tok_all, lse_ref = outs[:4]
        ctx_refs = outs[4 : 4 + nh]
        ctx_all = outs[4 + nh]
        mine = me_ref[0]
        for ref, (k, off, size) in zip(toks, places):
            tok_all[0, pl.ds(pl.multiple_of((mine ^ k) * part + off, size), size), :] = ref[0]
        qkv_ref[0] = (dot_nn(tok_all[0], w_ref[...]) + b_ref[...]).astype(bf16)
        low_half = lane_halves()
        keep = [jnp.where(low_half, scale, 0.0).astype(bf16), jnp.where(low_half, 0.0, scale).astype(bf16)]
        lane = lax.broadcasted_iota(jnp.int32, (step, 128), 1)

        def block(i, carry):
            at = pl.ds(pl.multiple_of(i * step, step), step)
            same = sc_ref[0, at, :] == sr_ref[0]
            lse_tile = jnp.zeros((step, 128), f32)
            for pair in range(heads // 2):
                span = slice(pair * 128, pair * 128 + 128)
                q_pair = qkv_ref[0, at, span]
                k_pair = qkv_ref[0, :, cols + pair * 128 : cols + pair * 128 + 128]
                v_pair = qkv_ref[0, :, 2 * cols + pair * 128 : 2 * cols + pair * 128 + 128]
                outs = []
                for half in range(2):
                    h = 2 * pair + half
                    raw = dot_nt(q_pair * keep[half], k_pair) + prev_ref[0, h, at, :].astype(f32)
                    raw_ref[0, h, at, :] = raw.astype(bf16)
                    masked = jnp.where(same, raw, masked_fill)
                    top = jnp.max(masked, axis=-1, keepdims=True)
                    grown = jnp.exp(masked - top)
                    total = jnp.sum(grown, axis=-1, keepdims=True)
                    probs = (grown * (1.0 / total)).astype(bf16)
                    outs.append(dot_nn(probs, v_pair))
                    lse_tile = jnp.where(lane == h, top + jnp.log(total), lse_tile)
                ctx_all[at, span] = jnp.where(low_half, outs[0], outs[1]).astype(bf16)
            lse_ref[0, at, :] = lse_tile
            return carry

        lax.fori_loop(0, slots // step, block, 0)
        for k in range(nh):
            ctx_refs[k][0] = ctx_all[pl.ds(pl.multiple_of((mine ^ k) * part, part), part), :]

    def shifted(shape):
        return pl.BlockSpec(shape, lambda r, *_: (first + r,) + (0,) * (len(shape) - 1))

    return pl.pallas_call(
        body,
        grid_spec=pltpu.PrefetchScalarGridSpec(
            num_scalar_prefetch=1,
            grid=(rows,),
            in_specs=[by_step((1,) + p.shape[1:]) for _, _, p in pieces]
            + [
                whole((width, 3 * cols)),
                whole((1, 3 * cols)),
                shifted((1, 1, slots)),
                shifted((1, slots, 1)),
                shifted((1, heads, slots, slots)),
            ]
            + [pl.BlockSpec(memory_space=pl.ANY)] * chained,
            out_specs=[
                by_step((1, slots, 3 * cols)),
                shifted((1, heads, slots, slots)),
                by_step((1, slots, width)),
                by_step((1, slots, 128)),
            ]
            + [by_step((1, part, cols))] * nh,
            scratch_shapes=[pltpu.VMEM((slots, cols), bf16)],
        ),
        out_shape=[
            jax.ShapeDtypeStruct((rows, slots, 3 * cols), bf16),
            jax.ShapeDtypeStruct((total_rows, heads, slots, slots), bf16),
            jax.ShapeDtypeStruct((rows, slots, width), bf16),
            jax.ShapeDtypeStruct((rows, slots, 128), f32),
        ]
        + [jax.ShapeDtypeStruct((rows, part, cols), bf16)] * nh,
        input_output_aliases={np_ + 6: 1} if chained else {},
        compiler_params=params(),
        cost_estimate=cost(
            2 * rows * slots * cols * (3 * width + 2 * slots), 5 * rows * heads * slots * slots, rows * heads * slots * slots
        ),
        name="attend",
    )(me, *[p for _, _, p in pieces], w_flat, bias_row, seg_row, seg_col, prev, *([raw_so_far] if chained else []))


def attend_back(me, first, tok, ctx_grads, qkv, prev, logit_grad, seg_row, seg_col, lse, w_flat, so_far):
    total_rows, heads, slots, _ = prev.shape
    nh = len(ctx_grads)
    rows, _, width = tok.shape
    part = slots // nh
    cols = heads * head_dim
    step = 128
    scale = head_dim ** (-0.5)
    chained = so_far is not None

    def body(me_ref, *refs):
        grads = refs[:nh]
        tok_ref, qkv_ref, prev_ref, lg_ref, sr_ref, sc_ref, lse_ref, w_ref = refs[nh : nh + 8]
        rest = refs[nh + 8 :]
        if chained:
            _, gw_before, gb_before = rest[:3]
            rest = rest[3:]
        pg_ref, gw_ref, gb_ref = rest[:3]
        in_refs = rest[3 : 3 + nh]
        go_all, p_all, dt_all, in_all = rest[3 + nh :]
        mine = me_ref[0]
        for k in range(nh):
            go_all[pl.ds(pl.multiple_of((mine ^ k) * part, part), part), :] = grads[k][0]
        low_half = lane_halves()
        keep_q = [jnp.where(low_half, scale, 0.0).astype(bf16), jnp.where(low_half, 0.0, scale).astype(bf16)]
        keep_g = [jnp.where(low_half, 1.0, 0.0).astype(bf16), jnp.where(low_half, 0.0, 1.0).astype(bf16)]

        def block(i, carry):
            at = pl.ds(pl.multiple_of(i * step, step), step)
            same = sc_ref[0, at, :] == sr_ref[0]
            lse_tile = lse_ref[0, at, :]
            for pair in range(heads // 2):
                span = slice(pair * 128, pair * 128 + 128)
                q_pair = qkv_ref[0, at, span]
                g_pair = go_all[at, span]
                k_pair = qkv_ref[0, :, cols + pair * 128 : cols + pair * 128 + 128]
                v_pair = qkv_ref[0, :, 2 * cols + pair * 128 : 2 * cols + pair * 128 + 128]
                for half in range(2):
                    h = 2 * pair + half
                    raw = dot_nt(q_pair * keep_q[half], k_pair) + prev_ref[0, h, at, :].astype(f32)
                    probs = jnp.exp(jnp.where(same, raw, masked_fill) - lse_tile[:, h : h + 1])
                    p_all[h, at, :] = probs.astype(bf16)
                    pulled = probs * dot_nt(g_pair * keep_g[half], v_pair)
                    inner = jnp.sum(pulled, axis=-1, keepdims=True)
                    pg_ref[0, h, at, :] = (pulled - probs * inner + lg_ref[0, h, at, :].astype(f32)).astype(bf16)
            return carry

        lax.fori_loop(0, slots // step, block, 0)
        q_t = qkv_ref[0, :, :cols].T
        k_t = qkv_ref[0, :, cols : 2 * cols].T
        g_t = go_all[...].T
        for h in range(heads):
            span = slice(h * head_dim, h * head_dim + head_dim)
            grad_raw = pg_ref[0, h]
            dt_all[h * head_dim : (h + 1) * head_dim, :] = (dot_nt(k_t[span], grad_raw) * scale).astype(bf16)
            dt_all[cols + h * head_dim : cols + (h + 1) * head_dim, :] = (dot_nn(q_t[span], grad_raw) * scale).astype(bf16)
            dt_all[2 * cols + h * head_dim : 2 * cols + (h + 1) * head_dim, :] = dot_nn(g_t[span], p_all[h]).astype(bf16)
        grad_qkv = dt_all[...].T
        in_all[...] = dot_nt(grad_qkv, w_ref[...]).astype(bf16)
        for k in range(nh):
            in_refs[k][0] = in_all[pl.ds(pl.multiple_of((mine ^ k) * part, part), part), :]
        gw = dot_nn(dt_all[...], tok_ref[0])
        gb = dot_nn(jnp.ones((8, slots), bf16), grad_qkv)

        @pl.when(pl.program_id(0) == 0)
        def _():
            gw_ref[...] = gw_before[...] + gw if chained else gw
            gb_ref[...] = gb_before[...] + gb if chained else gb

        @pl.when(pl.program_id(0) > 0)
        def _():
            gw_ref[...] += gw
            gb_ref[...] += gb

    def shifted(shape):
        return pl.BlockSpec(shape, lambda r, *_: (first + r,) + (0,) * (len(shape) - 1))

    sums = [whole((3 * cols, width)), whole((8, 3 * cols))]
    return pl.pallas_call(
        body,
        grid_spec=pltpu.PrefetchScalarGridSpec(
            num_scalar_prefetch=1,
            grid=(rows,),
            in_specs=[by_step((1, part, cols))] * nh
            + [
                by_step((1, slots, width)),
                by_step((1, slots, 3 * cols)),
                shifted((1, heads, slots, slots)),
                shifted((1, heads, slots, slots)),
                shifted((1, 1, slots)),
                shifted((1, slots, 1)),
                by_step((1, slots, 128)),
                whole((width, 3 * cols)),
            ]
            + ([pl.BlockSpec(memory_space=pl.ANY)] + sums if chained else []),
            out_specs=[shifted((1, heads, slots, slots))] + sums + [by_step((1, part, width))] * nh,
            scratch_shapes=[
                pltpu.VMEM((slots, cols), bf16),
                pltpu.VMEM((heads, slots, slots), bf16),
                pltpu.VMEM((3 * cols, slots), bf16),
                pltpu.VMEM((slots, width), bf16),
            ],
        ),
        out_shape=[
            jax.ShapeDtypeStruct((total_rows, heads, slots, slots), bf16),
            jax.ShapeDtypeStruct((3 * cols, width), f32),
            jax.ShapeDtypeStruct((8, 3 * cols), f32),
        ]
        + [jax.ShapeDtypeStruct((rows, part, width), bf16)] * nh,
        input_output_aliases={nh + 9: 0} if chained else {},
        compiler_params=params(),
        cost_estimate=cost(
            2 * rows * slots * cols * (6 * width + 5 * slots), 7 * rows * heads * slots * slots, rows * heads * slots * slots
        ),
        name="attend_back",
    )(me, *ctx_grads, tok, qkv, prev, logit_grad, seg_row, seg_col, lse, w_flat, *(so_far if chained else []))


def weight_stream(refs, plan, buf, sem):
    t = pl.program_id(0)

    def start(which):
        for block, copies in enumerate(plan):

            @pl.when(which == block)
            def _(copies=copies, slot=block % 2):
                for array, low, size, side, to in copies:
                    pltpu.make_async_copy(
                        refs[array].at[pl.ds(low, size)], buf.at[slot, side, pl.ds(to, size)], sem.at[slot]
                    ).start()

    @pl.when(t == 0)
    def _():
        start(t)

    pltpu.make_async_copy(buf.at[t % 2], buf.at[t % 2], sem.at[t % 2]).wait()

    @pl.when(t + 1 < len(plan))
    def _():
        start(t + 1)

    return t % 2


def feed_forward(me, ctx_pieces, w_out, tokens, vectors, bias_blocks, weights, plan, out_grad):
    count, width = tokens.shape
    nh, nc = len(ctx_pieces), len(ctx_pieces[0])
    cols = ctx_pieces[0][0].shape[1]
    shard = weights[0].shape[1]
    per_block = hidden_block // shard
    blocks = len(plan)
    hidden = blocks * hidden_block
    tile = count // 3
    nw = len(weights)
    n_in = nh * nc + 5 + nw

    def body(me_ref, *refs):
        ctx = refs[: nh * nc]
        wo_ref, tok_ref, vec_ref, bias_ref, og_ref = refs[nh * nc : nh * nc + 5]
        w_refs = refs[nh * nc + 5 : n_in]
        res_ref, x_ref, unit_ref, inv_ref, g2_ref, gf_ref, act_ref, slope_ref, sum_ref = refs[n_in : n_in + 9]
        nrm, acc, buf, sem = refs[n_in + 9 :]
        t = pl.program_id(0)
        slot = weight_stream(w_refs, plan, buf, sem)

        @pl.when(t == 0)
        def _():
            low = 0
            for c in range(nc):
                size = ctx[c].shape[0]
                at = slice(low, low + size)
                low += size
                branch = vec_ref[0:1, :]
                for k in range(nh):
                    rows_of = slice(k * cols, k * cols + cols)
                    branch = branch + dot_nn(ctx[k * nc + c][...], wo_ref[rows_of, :])
                unit_one, inverse = norm_parts(tok_ref[at, :].astype(f32) + branch)
                unit_ref[at, :] = unit_one
                inv_ref[at, :] = jnp.broadcast_to(inverse, (size, 128))
                normed = unit_one * vec_ref[1:2, :] + vec_ref[2:3, :]
                nrm[at, :] = normed
                x_ref[at, :] = normed.astype(bf16)
            acc[...] = jnp.zeros_like(acc)

        w_in = buf[slot, 0].reshape(hidden_block, width)
        w_down = buf[slot, 1].reshape(hidden_block, width)
        for m in range(3):
            at = slice(m * tile, m * tile + tile)
            pre = dot_nt(x_ref[at, :], w_in) + bias_ref[0]
            below = 0.5 * (1.0 + lax.erf(pre * (0.5**0.5)))
            active = (pre * below).astype(bf16)
            act_ref[at, :] = active
            slope_ref[at, :] = (below + pre * (jnp.exp(-0.5 * pre * pre) * 0.3989422804014327)).astype(bf16)
            acc[at, :] += dot_nn(active, w_down)

        @pl.when(t == blocks - 1)
        def _():
            unit_two, inverse = norm_parts(nrm[...] + acc[...] + vec_ref[3:4, :])
            res_ref[...] = (unit_two * vec_ref[4:5, :] + vec_ref[5:6, :]).astype(bf16)
            top = og_ref[...].astype(f32)
            grad_two = norm_back(top, unit_two, inverse, vec_ref[4:5, :])
            g2_ref[...] = grad_two
            low = grad_two.astype(bf16)
            gf_ref[...] = low
            sum_ref[0:1, :] = jnp.sum(top * unit_two, axis=0, keepdims=True)
            sum_ref[1:2, :] = jnp.sum(top, axis=0, keepdims=True)
            sum_ref[2:3, :] = jnp.sum(low.astype(f32), axis=0, keepdims=True)
            sum_ref[3:8, :] = jnp.zeros((5, width), f32)

    return pl.pallas_call(
        body,
        grid_spec=pltpu.PrefetchScalarGridSpec(
            num_scalar_prefetch=1,
            grid=(blocks,),
            in_specs=[whole(p.shape) for k in ctx_pieces for p in k]
            + [
                whole(w_out.shape),
                whole((count, width)),
                whole((8, width)),
                by_step((1, 1, hidden_block)),
                whole((count, width)),
            ]
            + [pl.BlockSpec(memory_space=pl.ANY)] * nw,
            out_specs=[
                whole((count, width)),
                whole((count, width)),
                whole((count, width)),
                whole((count, 128)),
                whole((count, width)),
                whole((count, width)),
                by_step((count, hidden_block), 1),
                by_step((count, hidden_block), 1),
                whole((8, width)),
            ],
            scratch_shapes=[
                pltpu.VMEM((count, width), f32),
                pltpu.VMEM((count, width), f32),
                pltpu.VMEM((2, 2, per_block, shard, width), bf16),
                pltpu.SemaphoreType.DMA((2,)),
            ],
        ),
        out_shape=[
            jax.ShapeDtypeStruct((count, width), bf16),
            jax.ShapeDtypeStruct((count, width), bf16),
            jax.ShapeDtypeStruct((count, width), f32),
            jax.ShapeDtypeStruct((count, 128), f32),
            jax.ShapeDtypeStruct((count, width), f32),
            jax.ShapeDtypeStruct((count, width), bf16),
            jax.ShapeDtypeStruct((count, hidden), bf16),
            jax.ShapeDtypeStruct((count, hidden), bf16),
            jax.ShapeDtypeStruct((8, width), f32),
        ],
        compiler_params=params(),
        cost_estimate=cost(2 * count * width * (2 * hidden + width), 4 * hidden * (width + count), count * hidden),
        name="feed_forward",
    )(me, *[p for k in ctx_pieces for p in k], w_out, tokens, vectors, bias_blocks, out_grad, *weights)


def feed_back(me, w_out, grad_two, grad_ffn, slope, unit_one, inv_one, vectors, weights, plan, cols, chunk_sizes):
    count, width = grad_two.shape
    nh = w_out.shape[0] // cols
    nc = len(chunk_sizes)
    shard = weights[0].shape[1]
    per_block = hidden_block // shard
    blocks = len(plan)
    hidden = blocks * hidden_block
    tile = count // 3
    nw = len(weights)

    def body(me_ref, *refs):
        wo_ref, g2_ref, gf_ref, slope_ref, unit_ref, inv_ref, vec_ref = refs[:7]
        w_refs = refs[7 : 7 + nw]
        res_ref, low_ref, gh_ref, gb_ref, sum_ref = refs[7 + nw : 12 + nw]
        gc_refs = refs[12 + nw : 12 + nw + nh * nc]
        acc, buf, sem = refs[12 + nw + nh * nc :]
        t = pl.program_id(0)
        slot = weight_stream(w_refs, plan, buf, sem)

        @pl.when(t == 0)
        def _():
            acc[...] = g2_ref[...]

        w_in = buf[slot, 0].reshape(hidden_block, width)
        w_down = buf[slot, 1].reshape(hidden_block, width)
        total = jnp.zeros((1, hidden_block), f32)
        for m in range(3):
            at = slice(m * tile, m * tile + tile)
            grad_hidden = (dot_nt(gf_ref[at, :], w_down) * slope_ref[at, :].astype(f32)).astype(bf16)
            gh_ref[at, :] = grad_hidden
            total = total + jnp.sum(grad_hidden.astype(f32), axis=0, keepdims=True)
            acc[at, :] += dot_nn(grad_hidden, w_in)
        gb_ref[0] = total

        @pl.when(t == blocks - 1)
        def _():
            grad_one = acc[...]
            unit_one = unit_ref[...]
            grad_res = norm_back(grad_one, unit_one, inv_ref[:, 0:1], vec_ref[1:2, :])
            res_ref[...] = grad_res
            low = grad_res.astype(bf16)
            low_ref[...] = low
            sum_ref[0:1, :] = jnp.sum(grad_one * unit_one, axis=0, keepdims=True)
            sum_ref[1:2, :] = jnp.sum(grad_one, axis=0, keepdims=True)
            sum_ref[2:3, :] = jnp.sum(low.astype(f32), axis=0, keepdims=True)
            sum_ref[3:8, :] = jnp.zeros((5, width), f32)
            for k in range(nh):
                rows_of = slice(k * cols, k * cols + cols)
                grad_ctx = dot_nt(low_ref[...], wo_ref[rows_of, :]).astype(bf16)
                start = 0
                for c in range(nc):
                    gc_refs[k * nc + c][...] = grad_ctx[start : start + chunk_sizes[c]]
                    start += chunk_sizes[c]

    return pl.pallas_call(
        body,
        grid_spec=pltpu.PrefetchScalarGridSpec(
            num_scalar_prefetch=1,
            grid=(blocks,),
            in_specs=[
                whole(w_out.shape),
                whole((count, width)),
                whole((count, width)),
                by_step((count, hidden_block), 1),
                whole((count, width)),
                whole((count, 128)),
                whole((8, width)),
            ]
            + [pl.BlockSpec(memory_space=pl.ANY)] * nw,
            out_specs=[
                whole((count, width)),
                whole((count, width)),
                by_step((count, hidden_block), 1),
                by_step((1, 1, hidden_block)),
                whole((8, width)),
            ]
            + [whole((n, cols)) for _ in range(nh) for n in chunk_sizes],
            scratch_shapes=[
                pltpu.VMEM((count, width), f32),
                pltpu.VMEM((2, 2, per_block, shard, width), bf16),
                pltpu.SemaphoreType.DMA((2,)),
            ],
        ),
        out_shape=[
            jax.ShapeDtypeStruct((count, width), f32),
            jax.ShapeDtypeStruct((count, width), bf16),
            jax.ShapeDtypeStruct((count, hidden), bf16),
            jax.ShapeDtypeStruct((blocks, 1, hidden_block), f32),
            jax.ShapeDtypeStruct((8, width), f32),
        ]
        + [jax.ShapeDtypeStruct((n, cols), bf16) for _ in range(nh) for n in chunk_sizes],
        compiler_params=params(),
        cost_estimate=cost(2 * count * width * (2 * hidden + width), 4 * hidden * (width + count)),
        name="feed_back",
    )(me, w_out, grad_two, grad_ffn, slope, unit_one, inv_one, vectors, *weights)


def weight_grads(x_low, grad_ffn, grad_hidden, active, blocks, stride, first, shard, addends):
    count, width = x_low.shape
    per_block = hidden_block // shard
    adding = addends is not None
    specs = [
        pl.BlockSpec((per_block, None, shard, width), lambda t: (0, t, 0, 0)),
        pl.BlockSpec((None, per_block, shard, width), lambda t: (t, 0, 0, 0)),
    ]

    def body(x_ref, gf_ref, gh_ref, act_ref, *refs):
        for side, (left, right) in enumerate(((gh_ref, x_ref), (act_ref, gf_ref))):
            value = dot_tn(left[...], right[...]).reshape(per_block, shard, width)
            if adding:
                value = value + refs[side][...].astype(f32)
            refs[2 * adding + side][...] = value.astype(bf16)

    moving = pl.BlockSpec((count, hidden_block), lambda t: (0, first + stride * t))
    return pl.pallas_call(
        body,
        grid=(blocks,),
        in_specs=[whole((count, width)), whole((count, width)), moving, moving] + specs * adding,
        out_specs=specs,
        out_shape=[
            jax.ShapeDtypeStruct((per_block, blocks, shard, width), bf16),
            jax.ShapeDtypeStruct((blocks, per_block, shard, width), bf16),
        ],
        compiler_params=params(),
        cost_estimate=cost(4 * count * width * hidden_block * blocks, 8 * hidden_block * blocks * (width + count)),
        name="weight_grads",
    )(x_low, grad_ffn, grad_hidden, active, *(addends if adding else ()))


def out_grads(me, ctx_pieces, low, nh):
    nc = len(ctx_pieces[0])
    cols = ctx_pieces[0][0].shape[1]
    count, width = low.shape

    def body(*refs):
        low_ref, out_ref = refs[nh * nc : nh * nc + 2]
        for k in range(nh):
            start, value = 0, None
            for c in range(nc):
                size = refs[k * nc + c].shape[0]
                piece = dot_tn(refs[k * nc + c][...], low_ref[start : start + size, :])
                value = piece if value is None else value + piece
                start += size
            out_ref[k] = value.astype(bf16)

    return pl.pallas_call(
        body,
        grid=(1,),
        in_specs=[whole(p.shape) for k in ctx_pieces for p in k] + [whole((count, width))],
        out_specs=whole((nh, cols, width)),
        out_shape=jax.ShapeDtypeStruct((nh, cols, width), bf16),
        compiler_params=params(),
        cost_estimate=cost(2 * count * width * nh * cols, 2 * nh * cols * (width + count)),
        name="out_grads",
    )(*[p for k in ctx_pieces for p in k], low)


class Links:
    def __init__(self, head_axes, row_axes, nh, nr):
        self.head_axes, self.row_axes, self.nh, self.nr = head_axes, row_axes, nh, nr
        self.axes = head_axes + row_axes
        self.factored = len(row_axes) == 2

    def swap(self, value, head_bits=0, row_bits=0):
        mask = head_bits * self.nr + row_bits
        return lax.ppermute(value, self.axes, [(i, i ^ mask) for i in range(self.nh * self.nr)])

    def sum_rows(self, value):
        bit = 1
        while bit < self.nr:
            value = value + self.swap(value, 0, bit)
            bit *= 2
        return value

    def sum_heads(self, value):
        bit = 1
        while bit < self.nh:
            value = value + self.swap(value, bit, 0)
            bit *= 2
        return value

    def sum_all(self, value):
        return self.sum_heads(self.sum_rows(value))


def after(value, *others):
    return lax.optimization_barrier((value, *others))[0]


def gather_tokens(links, tokens, chunks, small, early):
    own = [tokens[low : low + size] for low, size in chunks]
    if links.nh != 4:
        return [[(0, 0, t)] + [(k, 0, links.swap(t, k)) for k in range(1, links.nh)] for t in own], None
    result, others, gate = [], None, ()
    for mine in own:
        mine = after(mine, *gate)
        half = mine.shape[1] // 2
        beside, across = links.swap(mine, 1), links.swap(mine, 2)
        if others is None:
            others = exchange(links, small)
            beside, across = hold((beside, across), *early)
        else:
            beside, across = hold((beside, across), *far)
        far = links.swap(across[:, :half], 1), links.swap(beside[:, half:], 2)
        gate = (beside, across, *others)
        result.append([(0, 0, mine), (1, 0, beside), (2, 0, across), (3, 0, far[0]), (3, half, far[1])])
    return result, others


def exchange_first(links, mine):
    return mine, links.swap(mine, 1), links.swap(mine, 2)


def exchange_second(links, mine, beside, across):
    half = mine.shape[0] // 2
    return mine, beside, across, links.swap(across[:half], 1), links.swap(beside[half:], 2)


def exchange(links, mine):
    return exchange_second(links, *exchange_first(links, mine))


def hold(values, *others):
    flat, tree = jax.tree.flatten(values)
    return jax.tree.unflatten(tree, lax.optimization_barrier((*flat, *others))[: len(flat)])


def all_weights(links, in_all, column, beside, across, low, high):
    mine = [in_all, column, beside, across, low, high]
    arrays = mine + [links.swap(a, 0, 1) for a in mine]
    plan = []
    for k in range(4):
        for base in (0, 6):
            copies = [(base, z * 4 + k, 1, 0, z) for z in range(4)]
            if k < 3:
                copies.append((base + 1 + k, 0, 4, 1, 0))
            else:
                copies += [(base + 4, 0, 2, 1, 0), (base + 5, 0, 2, 1, 2)]
            plan.append(copies)
    return arrays, plan


def by_core(first, second, core):
    return jnp.where(core == 0, first, second)


def add_low(a, b):
    return (a.astype(f32) + b.astype(f32)).astype(bf16)


def scatter_first(links, own, beside, across, far):
    half = far.shape[0] // 2
    return own, beside, across, links.swap(far[:half], 1), links.swap(far[half:], 2)


def scatter_second(links, own, beside, across, for_across, for_beside):
    half = for_across.shape[0]
    across = jnp.concatenate([add_low(across[:half], for_across), across[half:]])
    beside = jnp.concatenate([beside[:half], add_low(beside[half:], for_beside)])
    return own, links.swap(beside, 1), links.swap(across, 2)


def scatter_sum(own, beside, across):
    return own.astype(f32) + beside.astype(f32) + across.astype(f32)


def scatter_places(links, total):
    here = lax.axis_index("z")
    pieces = [lax.dynamic_index_in_dim(total, here ^ k, keepdims=False) for k in range(4)]
    return [pieces[0]] + [links.swap(pieces[k], 0, 2 * k) for k in range(1, 4)]


def sum_of(pieces):
    total = pieces[0].astype(f32)
    for piece in pieces[1:]:
        total = total + piece.astype(f32)
    return total


def core_half(links, value, axis):
    core = lax.axis_index("core")
    size = value.shape[axis] // 2
    keep = lax.dynamic_slice_in_dim(value, core * size, size, axis)
    give = lax.dynamic_slice_in_dim(value, (1 - core) * size, size, axis)
    return keep.astype(f32) + links.swap(give.astype(bf16), 0, 1).astype(f32)


def reduce_weights(links, gwo, gw):
    if not links.factored:
        return lax.psum((gwo, gw), links.row_axes)
    core = lax.axis_index("core")
    sums = lax.psum((gwo, gw), "z")
    others = [links.swap(v, 0, 1) for v in sums]
    return [jnp.concatenate([by_core(v, o, core), by_core(o, v, core)]) for v, o in zip(sums, others)]


def per_device(
    links,
    tokens,
    prev_logits,
    segment_ids,
    w_qkv,
    b_qv,
    w_out,
    b_out,
    ln1_gain,
    ln1_shift,
    w_in,
    b_in,
    w_down,
    b_down,
    ln2_gain,
    ln2_shift,
    out_grad,
    logit_grad,
):
    rows, part, width = tokens.shape
    heads = prev_logits.shape[1]
    cols = heads * head_dim
    shard = w_in.shape[1]
    count = rows * part
    nh, nr = links.nh, links.nr
    me = lax.axis_index(links.head_axes).astype(jnp.int32).reshape(1)
    place = lax.axis_index(links.axes)
    chunks = [(0, rows // 2), (rows // 2, rows - rows // 2)]
    chunk_sizes = [size * part for _, size in chunks]

    bias_qv = b_qv.astype(f32)
    bias_row = jnp.concatenate([bias_qv[0], jnp.zeros_like(bias_qv[0]), bias_qv[1]])[None]
    w_flat = w_qkv.reshape(width, 3 * cols)
    seg_row = segment_ids[:, None, :]
    seg_col = segment_ids[:, :, None]
    shards = nh * nr
    mine = lax.broadcasted_iota(jnp.int32, (shards, 1), 0) == place
    bias_all = links.sum_all(jnp.where(mine, b_in.astype(f32)[None], 0.0))
    core = lax.axis_index("core") if links.factored else 0
    if links.factored:
        here_h = lax.axis_index(links.head_axes)
        order = jnp.stack(
            [(here_h ^ k) * nr + z * 2 + (core ^ c) for k in range(4) for c in range(2) for z in range(4)]
        )
        bias_blocks = bias_all[order].reshape(-1, 1, hidden_block)
        column = lax.all_gather(w_down[None], "z", axis=0, tiled=True)
        out_half = lax.dynamic_slice_in_dim(w_out, core * (cols // 2), cols // 2)
        small = jnp.concatenate([w_in.T, out_half])
    else:
        bias_blocks = bias_all.reshape(-1, 1, hidden_block)
        small = None
    blocks = bias_blocks.shape[0]
    vectors = jnp.stack(
        [
            b_out.astype(f32),
            ln1_gain,
            ln1_shift,
            b_down.astype(f32),
            ln2_gain,
            ln2_shift,
            jnp.zeros_like(ln1_gain),
            jnp.zeros_like(ln1_gain),
        ]
    )

    early = (bias_row, w_flat, seg_row, seg_col, vectors, bias_blocks)
    tok_pieces, others = gather_tokens(links, tokens, chunks, small, early)
    if links.factored:
        rows_in = [others[0][:shard], others[1][:shard], others[2][:shard], others[3]]
        in_all = lax.all_gather(
            after(jnp.stack(rows_in), column, *(p for _, _, p in tok_pieces[0][1:3])), "z", axis=0, tiled=True
        )
        arrived = [p for _, _, p in tok_pieces[1][1:3]]
        tok_pieces[0] = hold(tok_pieces[0], *arrived)
        tok_pieces[0] = [(k, off, p) for (k, off, _), (_, _, p) in zip(tok_pieces[1], tok_pieces[0])]
        weight_pieces = exchange_first(links, after(column, *arrived))

    raw_logits, saved, ctx_pieces = None, [], [[] for _ in range(nh)]
    for c, ((low, size), pieces) in enumerate(zip(chunks, tok_pieces)):
        if c and links.factored:
            weight_pieces = hold(weight_pieces, raw_logits_gate)
            weight_pieces = exchange_second(links, *weight_pieces)
            near = weight_pieces[1:3]
            pieces = [(k, off, after(p, *near) if k == 3 else p) for k, off, p in pieces]
        qkv, raw_logits, tok_all, lse, *ctx = attend(
            me, low, pieces, w_flat, bias_row, seg_row, seg_col, prev_logits, raw_logits
        )
        raw_logits_gate = ctx[0]
        saved.append((qkv, tok_all, lse))
        if c and links.factored:
            ctx = hold(ctx, *(p[0] for p in ctx_pieces))
        for k in range(nh):
            piece = links.swap(ctx[k], k) if k else ctx[k]
            ctx_pieces[k].append(piece.reshape(size * part, cols))
    if links.factored:
        weights, plan = all_weights(links, *hold([in_all, *weight_pieces], raw_logits_gate))
        rows_out = jnp.stack([others[0][shard:], others[1][shard:], others[2][shard:], others[4]])
        rows_out = after(rows_out, raw_logits_gate)
        theirs = links.swap(rows_out, 0, 1)
        w_out_all = jnp.stack([by_core(rows_out, theirs, core), by_core(theirs, rows_out, core)], axis=1)
        w_out_all = w_out_all.reshape(nh * cols, width)
    else:
        weights = [lax.all_gather(a[None], links.axes, axis=0, tiled=True) for a in (w_in.T, w_down)]
        per_block = hidden_block // shard
        plan = [[(side, t * per_block, per_block, side, 0) for side in range(2)] for t in range(blocks)]
        w_out_all = jnp.concatenate([w_out] + [links.swap(w_out, k) for k in range(1, nh)])
    layer_out, x_low, unit_one, inv_one, grad_two, grad_ffn, active, slope, sums_two = feed_forward(
        me,
        ctx_pieces,
        w_out_all,
        tokens.reshape(count, width),
        vectors,
        bias_blocks,
        weights,
        plan,
        out_grad.reshape(count, width),
    )
    grad_res, grad_low, grad_hidden, gb_in, sums_one, *ctx_grad = feed_back(
        me, w_out_all, grad_two, grad_ffn, slope, unit_one, inv_one, vectors, weights, plan, cols, chunk_sizes
    )
    nc = len(chunks)
    if links.factored:
        theirs = weight_grads(x_low, grad_ffn, grad_hidden, active, blocks // 2, 2, 1, shard, None)
        gwo = out_grads(me, ctx_pieces, after(grad_low, theirs[0]), nh)
        theirs = [links.swap(g.reshape(-1, shard, width), 0, 1).reshape(g.shape) for g in theirs]
    else:
        gwo = out_grads(me, ctx_pieces, grad_low, nh)
    ctx_grads = [
        [
            (links.swap(after(ctx_grad[k * nc + c], gwo) if c else ctx_grad[k * nc], k) if k else ctx_grad[c]).reshape(size, part, cols)
            for k in range(nh)
        ]
        for c, (_, size) in enumerate(chunks)
    ]
    if links.factored:
        own = weight_grads(x_low, grad_ffn, after(grad_hidden, gwo, *ctx_grads[0]), active, blocks // 2, 2, 0, shard, theirs)
        in_sum = lax.psum_scatter(own[0].reshape(-1, shard, width), "z", scatter_dimension=0, tiled=True)
        down_state = scatter_first(links, *(own[1][k] for k in range(4)))
        gwo = core_half(links, after(gwo, own[0]), 1).astype(bf16)
        ctx_grads[0] = hold(ctx_grads[0], own[0], *ctx_grads[1], gwo)
    else:
        own = weight_grads(x_low, grad_ffn, grad_hidden, active, blocks, 1, 0, shard, None)
        own = [own[0].transpose(1, 0, 2, 3), own[1]]
        own_in, own_down = (
            lax.psum_scatter(g.reshape(-1, shard, width), links.axes, scatter_dimension=0, tiled=True)[0] for g in own
        )
    gwo_parts = [gwo[0]] + [links.swap(gwo[k], k) for k in range(1, nh)]

    so_far, returned = None, []
    for c, (low, size) in enumerate(chunks):
        qkv, tok_all, lse = saved[c]
        if links.factored and c:
            down_state, gwo_parts = hold((down_state, gwo_parts), gb)
            ctx_grads[c] = hold(ctx_grads[c], *down_state[3:], *gwo_parts)
            down_state = scatter_second(links, *down_state)
        prev_grad, gw, gb, *input_part = attend_back(
            me, low, tok_all, ctx_grads[c], qkv, prev_logits, logit_grad, seg_row, seg_col, lse, w_flat, so_far
        )
        so_far = (prev_grad, gw, gb)
        if links.factored and c:
            gw = core_half(links, after(gw, in_sum), 0).astype(bf16)
            input_part = hold(input_part, gw, *returned[-1])
        returned.append([input_part[0]] + [links.swap(input_part[k], k) for k in range(1, nh)])
    gwo_total = sum_of(gwo_parts)
    if links.factored:
        down_state = hold(down_state, gb)
        down_parts = scatter_places(links, scatter_sum(*down_state).astype(bf16))
        in_sum = after(in_sum, gb)
        in_state = scatter_first(links, *(in_sum[k] for k in range(4)))
        own_in = scatter_sum(*scatter_second(links, *in_state))
        own_down = sum_of(down_parts)
    grad_w_out, grad_w_qkv = reduce_weights(links, gwo_total.astype(bf16), gw.astype(bf16))
    parts = []
    for (low, size), pieces in zip(chunks, returned):
        total = grad_res.reshape(rows, part, width)[low : low + size]
        for piece in pieces:
            total = total + piece.astype(f32)
        parts.append(total)
    tokens_grad = jnp.concatenate(parts)
    gb_in = gb_in.reshape(shards, shard)
    if links.factored:
        seq = jnp.arange(shards)
        gb_in = gb_in[((seq // nr) ^ here_h) * 8 + ((seq % 2) ^ core) * 4 + (seq % nr) // 2]
    sums = jnp.concatenate([sums_two[:3], sums_one[:3], gb_in.reshape(-1, width), jnp.pad(gb[:1], ((0, 0), (0, width - 3 * cols)))])
    sums = links.sum_rows(after(sums, gw, *returned[0]))
    grad_b_qv = jnp.stack([sums[-1, :cols], sums[-1, 2 * cols : 3 * cols]])
    totals = links.sum_heads(sums)
    grad_b_in = lax.dynamic_slice_in_dim(totals[6:-1].reshape(-1), place * shard, shard)
    return (
        layer_out.reshape(rows, part, width),
        raw_logits,
        tokens_grad,
        prev_grad,
        grad_w_qkv.astype(f32).T.reshape(width, 3, cols),
        grad_b_qv,
        grad_w_out.astype(f32),
        totals[5],
        totals[3],
        totals[4],
        own_in.astype(f32).T,
        grad_b_in,
        own_down.astype(f32),
        totals[2],
        totals[0],
        totals[1],
    )


def solution(mesh):
    nh, nr = mesh.shape["head"], mesh.shape["row"]
    if (nh, nr) == (4, 8):
        head, row = ("y", "x"), ("z", "core")
        mesh = Mesh(mesh.devices.reshape(2, 2, 4, 2), head + row)
    else:
        head, row = ("head",), ("row",)
    every = head + row
    placed = (
        P(row, head, None),
        P(row, head, None, None),
        P(row, None),
        P(None, None, head),
        P(None, head),
        P(head, None),
        P(),
        P(),
        P(),
        P(None, every),
        P(every),
        P(every, None),
        P(),
        P(),
        P(),
        P(row, head, None),
        P(row, head, None, None),
    )
    return jax.shard_map(
        functools.partial(per_device, Links(head, row, nh, nr)),
        mesh=mesh,
        in_specs=placed,
        out_specs=(
            P(row, head, None),
            P(row, head, None, None),
            P(row, head, None),
            P(row, head, None, None),
            P(None, None, head),
            P(None, head),
            P(head, None),
            P(),
            P(),
            P(),
            P(None, every),
            P(every),
            P(every, None),
            P(),
            P(),
            P(),
        ),
        check_vma=False,
    )
```

```python
import functools

import jax
import jax.numpy as jnp
from jax import lax
from jax.experimental import pallas as pl
from jax.experimental.pallas import tpu as pltpu
from jax.sharding import Mesh
from jax.sharding import PartitionSpec as P

norm_eps = 1e-12
masked_fill = -1000000000.0
head_dim = 64
hidden_block = 512
bias_rows = 16
bf16 = jnp.bfloat16
f32 = jnp.float32


def dot_nn(a, b):
    return lax.dot_general(a, b, (((1,), (0,)), ((), ())), preferred_element_type=f32)


def dot_nt(a, b):
    return lax.dot_general(a, b, (((1,), (1,)), ((), ())), preferred_element_type=f32)


def dot_tn(a, b):
    return lax.dot_general(a, b, (((0,), (0,)), ((), ())), preferred_element_type=f32)


def params(limit_mib=60):
    return pltpu.CompilerParams(
        dimension_semantics=("arbitrary",), vmem_limit_bytes=limit_mib * 1024 * 1024
    )


def cost(flops, nbytes, exps=0):
    return pl.CostEstimate(flops=int(flops), bytes_accessed=int(nbytes), transcendentals=int(exps))


def whole(shape):
    return pl.BlockSpec(shape, lambda *_: (0,) * len(shape))


def by_step(shape, axis=0):
    return pl.BlockSpec(shape, lambda t, *_: tuple(t if d == axis else 0 for d in range(len(shape))))


def norm_parts(values):
    center = jnp.mean(values, axis=-1, keepdims=True)
    offset = values - center
    inverse = lax.rsqrt(jnp.mean(offset * offset, axis=-1, keepdims=True) + norm_eps)
    return offset * inverse, inverse


def norm_back(grad_in, unit_vals, inverse, gain_vec):
    scaled = grad_in * gain_vec
    return inverse * (
        scaled
        - jnp.mean(scaled, axis=-1, keepdims=True)
        - unit_vals * jnp.mean(scaled * unit_vals, axis=-1, keepdims=True)
    )


def lane_halves():
    lane = lax.broadcasted_iota(jnp.int32, (1, 2 * head_dim), 1)
    return lane < head_dim


def attend(me, first, pieces, w_flat, bias_row, seg_row, seg_col, prev, raw_so_far):
    total_rows, heads, slots, _ = prev.shape
    rows, _, width = pieces[0][2].shape
    cols = heads * head_dim
    nh = len({k for k, _, _ in pieces})
    part = slots // nh
    scale = head_dim ** (-0.5)
    np_ = len(pieces)
    places = [(k, off, p.shape[1]) for k, off, p in pieces]
    chained = raw_so_far is not None

    def body(me_ref, *refs):
        toks = refs[:np_]
        w_ref, b_ref, sr_ref, sc_ref, prev_ref = refs[np_ : np_ + 5]
        outs = refs[np_ + 5 + chained :]
        qkv_ref, raw_ref, tok_all, lse_ref = outs[:4]
        ctx_refs = outs[4 : 4 + nh]
        ctx_all = outs[4 + nh]
        mine = me_ref[0]
        for ref, (k, off, size) in zip(toks, places):
            tok_all[0, pl.ds(pl.multiple_of((mine ^ k) * part + off, size), size), :] = ref[0]
        qkv_ref[0] = (dot_nn(tok_all[0], w_ref[...]) + b_ref[...]).astype(bf16)
        low_half = lane_halves()
        keep = [jnp.where(low_half, scale, 0.0).astype(bf16), jnp.where(low_half, 0.0, scale).astype(bf16)]
        lane = lax.broadcasted_iota(jnp.int32, (1, 128), 1)
        same = sc_ref[0] == sr_ref[0]
        lse_tile = jnp.zeros((slots, 128), f32)
        for pair in range(heads // 2):
            span = slice(pair * 128, pair * 128 + 128)
            q_pair = qkv_ref[0, :, span]
            k_pair = qkv_ref[0, :, cols + pair * 128 : cols + pair * 128 + 128]
            v_pair = qkv_ref[0, :, 2 * cols + pair * 128 : 2 * cols + pair * 128 + 128]
            outs = []
            for half in range(2):
                h = 2 * pair + half
                raw = dot_nt(q_pair * keep[half], k_pair) + prev_ref[0, h].astype(f32)
                raw_ref[0, h] = raw.astype(bf16)
                masked = jnp.where(same, raw, masked_fill)
                top = jnp.max(masked, axis=-1, keepdims=True)
                grown = jnp.exp(masked - top)
                total = jnp.sum(grown, axis=-1, keepdims=True)
                probs = (grown * (1.0 / total)).astype(bf16)
                outs.append(dot_nn(probs, v_pair))
                lse_tile = jnp.where(lane == h, top + jnp.log(total), lse_tile)
            ctx_all[:, span] = jnp.where(low_half, outs[0], outs[1]).astype(bf16)
        lse_ref[0] = lse_tile
        for k in range(nh):
            ctx_refs[k][0] = ctx_all[pl.ds(pl.multiple_of((mine ^ k) * part, part), part), :]

    def shifted(shape):
        return pl.BlockSpec(shape, lambda r, *_: (first + r,) + (0,) * (len(shape) - 1))

    return pl.pallas_call(
        body,
        grid_spec=pltpu.PrefetchScalarGridSpec(
            num_scalar_prefetch=1,
            grid=(rows,),
            in_specs=[by_step((1,) + p.shape[1:]) for _, _, p in pieces]
            + [
                whole((width, 3 * cols)),
                whole((1, 3 * cols)),
                shifted((1, 1, slots)),
                shifted((1, slots, 1)),
                shifted((1, heads, slots, slots)),
            ]
            + [pl.BlockSpec(memory_space=pl.ANY)] * chained,
            out_specs=[
                by_step((1, slots, 3 * cols)),
                shifted((1, heads, slots, slots)),
                by_step((1, slots, width)),
                by_step((1, slots, 128)),
            ]
            + [by_step((1, part, cols))] * nh,
            scratch_shapes=[pltpu.VMEM((slots, cols), bf16)],
        ),
        out_shape=[
            jax.ShapeDtypeStruct((rows, slots, 3 * cols), bf16),
            jax.ShapeDtypeStruct((total_rows, heads, slots, slots), bf16),
            jax.ShapeDtypeStruct((rows, slots, width), bf16),
            jax.ShapeDtypeStruct((rows, slots, 128), f32),
        ]
        + [jax.ShapeDtypeStruct((rows, part, cols), bf16)] * nh,
        input_output_aliases={np_ + 6: 1} if chained else {},
        compiler_params=params(),
        cost_estimate=cost(
            2 * rows * slots * cols * (3 * width + 2 * slots), 5 * rows * heads * slots * slots, rows * heads * slots * slots
        ),
        name="attend",
    )(me, *[p for _, _, p in pieces], w_flat, bias_row, seg_row, seg_col, prev, *([raw_so_far] if chained else []))


def attend_back(me, first, tok, ctx_grads, qkv, prev, logit_grad, seg_row, seg_col, lse, w_flat, so_far):
    total_rows, heads, slots, _ = prev.shape
    nh = len(ctx_grads)
    rows, _, width = tok.shape
    part = slots // nh
    cols = heads * head_dim
    half_rows = 3 * cols // 2
    scale = head_dim ** (-0.5)
    chained = so_far is not None

    def body(me_ref, *refs):
        grads = refs[:nh]
        tok_ref, qkv_ref, prev_ref, lg_ref, sr_ref, sc_ref, lse_ref, w_ref = refs[nh : nh + 8]
        rest = refs[nh + 8 :]
        if chained:
            gw_before = rest[1]
            rest = rest[2:]
        pg_ref, gw_ref = rest[:2]
        in_refs = rest[2 : 2 + nh]
        go_all, p_all, dt_all, in_all = rest[2 + nh :]
        mine = me_ref[0]
        for k in range(nh):
            go_all[pl.ds(pl.multiple_of((mine ^ k) * part, part), part), :] = grads[k][0]
        low_half = lane_halves()
        keep_q = [jnp.where(low_half, scale, 0.0).astype(bf16), jnp.where(low_half, 0.0, scale).astype(bf16)]
        keep_g = [jnp.where(low_half, 1.0, 0.0).astype(bf16), jnp.where(low_half, 0.0, 1.0).astype(bf16)]

        same = sc_ref[0] == sr_ref[0]
        for pair in range(heads // 2):
            span = slice(pair * 128, pair * 128 + 128)
            q_pair = qkv_ref[0, :, span]
            g_pair = go_all[:, span]
            k_pair = qkv_ref[0, :, cols + pair * 128 : cols + pair * 128 + 128]
            v_pair = qkv_ref[0, :, 2 * cols + pair * 128 : 2 * cols + pair * 128 + 128]
            for half in range(2):
                h = 2 * pair + half
                raw = dot_nt(q_pair * keep_q[half], k_pair) + prev_ref[0, h].astype(f32)
                probs = jnp.exp(jnp.where(same, raw, masked_fill) - lse_ref[0, :, h : h + 1])
                p_all[h] = probs.astype(bf16)
                pulled = probs * dot_nt(g_pair * keep_g[half], v_pair)
                inner = jnp.sum(pulled, axis=-1, keepdims=True)
                pg_ref[0, h] = (pulled - probs * inner + lg_ref[0, h].astype(f32)).astype(bf16)
        q_t = qkv_ref[0, :, :cols].T
        k_t = qkv_ref[0, :, cols : 2 * cols].T
        g_t = go_all[...].T
        for h in range(heads):
            span = slice(h * head_dim, h * head_dim + head_dim)
            grad_raw = pg_ref[0, h]
            dt_all[h * head_dim : (h + 1) * head_dim, :] = (dot_nt(k_t[span], grad_raw) * scale).astype(bf16)
            dt_all[cols + h * head_dim : cols + (h + 1) * head_dim, :] = (dot_nn(q_t[span], grad_raw) * scale).astype(bf16)
            dt_all[2 * cols + h * head_dim : 2 * cols + (h + 1) * head_dim, :] = dot_nn(g_t[span], p_all[h]).astype(bf16)
        grad_qkv = dt_all[...].T
        in_all[...] = dot_nt(grad_qkv, w_ref[...]).astype(bf16)
        for k in range(nh):
            in_refs[k][0] = in_all[pl.ds(pl.multiple_of((mine ^ k) * part, part), part), :]
        starts = pl.program_id(0) == 0

        @pl.when(starts)
        def _():
            gw_ref[...] = gw_before[...] if chained else jnp.zeros_like(gw_ref)

        gb = dot_nn(jnp.ones((bias_rows, slots), bf16), grad_qkv)
        for half in range(2):
            gw_ref[half, : half_rows, :] += dot_nn(dt_all[half * half_rows : (half + 1) * half_rows, :], tok_ref[0])
            gw_ref[half, half_rows:, : 3 * cols] += gb

    def shifted(shape):
        return pl.BlockSpec(shape, lambda r, *_: (first + r,) + (0,) * (len(shape) - 1))

    sums = [whole((2, half_rows + bias_rows, width))]
    return pl.pallas_call(
        body,
        grid_spec=pltpu.PrefetchScalarGridSpec(
            num_scalar_prefetch=1,
            grid=(rows,),
            in_specs=[by_step((1, part, cols))] * nh
            + [
                by_step((1, slots, width)),
                by_step((1, slots, 3 * cols)),
                shifted((1, heads, slots, slots)),
                shifted((1, heads, slots, slots)),
                shifted((1, 1, slots)),
                shifted((1, slots, 1)),
                by_step((1, slots, 128)),
                whole((width, 3 * cols)),
            ]
            + ([pl.BlockSpec(memory_space=pl.ANY)] + sums if chained else []),
            out_specs=[shifted((1, heads, slots, slots))] + sums + [by_step((1, part, width))] * nh,
            scratch_shapes=[
                pltpu.VMEM((slots, cols), bf16),
                pltpu.VMEM((heads, slots, slots), bf16),
                pltpu.VMEM((3 * cols, slots), bf16),
                pltpu.VMEM((slots, width), bf16),
            ],
        ),
        out_shape=[
            jax.ShapeDtypeStruct((total_rows, heads, slots, slots), bf16),
            jax.ShapeDtypeStruct((2, half_rows + bias_rows, width), f32),
        ]
        + [jax.ShapeDtypeStruct((rows, part, width), bf16)] * nh,
        input_output_aliases={nh + 9: 0} if chained else {},
        compiler_params=params(),
        cost_estimate=cost(
            2 * rows * slots * cols * (6 * width + 5 * slots), 7 * rows * heads * slots * slots, rows * heads * slots * slots
        ),
        name="attend_back",
    )(me, *ctx_grads, tok, qkv, prev, logit_grad, seg_row, seg_col, lse, w_flat, *(so_far if chained else []))


def resident(shape):
    return pl.BlockSpec(shape, lambda *_: (0,) * len(shape), pipeline_mode=pl.Buffered(1))


def fold(values):
    return jnp.sum(values.reshape(values.shape[0] // 8, 8, values.shape[1]), axis=0)


def feed(ctx_pieces, w_out, tokens, vectors, bias_blocks, weights, plan, out_grad):
    count, width = tokens.shape
    nh, nc = len(ctx_pieces), len(ctx_pieces[0])
    cols = ctx_pieces[0][0].shape[1]
    sizes = [p.shape[0] for p in ctx_pieces[0]]
    shard = weights[0].shape[1]
    per_block = hidden_block // shard
    blocks = len(plan)
    hidden = blocks * hidden_block
    strip = 128
    nw = len(weights)
    n_in = nh * nc + 5 + nw

    def body(*refs):
        ctx = refs[: nh * nc]
        wo_ref, tok_ref, vec_ref, bias_ref, og_ref = refs[nh * nc : nh * nc + 5]
        w_refs = refs[nh * nc + 5 : n_in]
        res_out, x_out, gf_out, gres_out, low_out, act_ref, gh_ref, gb_ref, sum_ref = refs[n_in : n_in + 9]
        gc_refs = refs[n_in + 9 : n_in + 9 + nh * nc]
        gwo_ref = refs[n_in + 9 + nh * nc]
        w_all, slope, unit, inv, acc, x_low, res, gf, low, w_sem, out_sem = refs[n_in + 10 + nh * nc :]
        t = pl.program_id(0)

        def sends(which):
            pairs = ((x_low, x_out), (res, res_out), (gf, gf_out), (acc, gres_out), (low, low_out))
            return [pltpu.make_async_copy(*pairs[i], out_sem.at[i]) for i in which]

        def strips(step, init):
            def one(i, carry):
                return step(pl.ds(pl.multiple_of(i * strip, strip), strip), carry)

            return lax.fori_loop(0, count // strip, one, init)

        @pl.when(t == 0)
        def _():
            for block, copies in enumerate(plan):
                for array, low_shard, size, side, to in copies:
                    pltpu.make_async_copy(
                        w_refs[array].at[pl.ds(low_shard, size)], w_all.at[block, side, pl.ds(to, size)], w_sem.at[block]
                    ).start()
            start = 0
            for c in range(nc):
                at = slice(start, start + sizes[c])
                start += sizes[c]
                branch = dot_nn(ctx[c][...], wo_ref[0:cols, :])
                for k in range(1, nh):
                    branch = branch + dot_nn(ctx[k * nc + c][...], wo_ref[k * cols : (k + 1) * cols, :])
                acc[at, :] = branch

            def first_norm(at, carry):
                unit_one, inverse = norm_parts(tok_ref[at, :].astype(f32) + (acc[at, :] + vec_ref[0:1, :]))
                unit[at, :] = unit_one
                inv[at, :] = jnp.broadcast_to(inverse, (strip, 128))
                normed = unit_one * vec_ref[1:2, :] + vec_ref[2:3, :]
                x_low[at, :] = normed.astype(bf16)
                acc[at, :] = normed + vec_ref[3:4, :]
                return carry

            strips(first_norm, 0)
            sends((0,))[0].start()

        @pl.when(t < blocks)
        def _():
            pltpu.make_async_copy(w_all.at[t], w_all.at[t], w_sem.at[t]).wait()
            w_in = w_all[t, 0].reshape(hidden_block, width)
            w_down = w_all[t, 1].reshape(hidden_block, width)
            for m in range(tiles):
                at = slice(m * (count // tiles), (m + 1) * (count // tiles))
                pre = dot_nt(x_low[at, :], w_in) + bias_ref[0]
                below = 0.5 * (1.0 + lax.erf(pre * (0.5**0.5)))
                active = (pre * below).astype(bf16)
                act_ref[at, :] = active
                slope[t, at, :] = (below + pre * (jnp.exp(-0.5 * pre * pre) * 0.3989422804014327)).astype(bf16)
                acc[at, :] += dot_nn(active, w_down)

        @pl.when(t == blocks - 1)
        def _():
            def second_norm(at, carry):
                unit_two, inverse = norm_parts(acc[at, :])
                res[at, :] = (unit_two * vec_ref[4:5, :] + vec_ref[5:6, :]).astype(bf16)
                top = og_ref[at, :].astype(f32)
                grad_two = norm_back(top, unit_two, inverse, vec_ref[4:5, :])
                acc[at, :] = grad_two
                grad_low = grad_two.astype(bf16)
                gf[at, :] = grad_low
                values = (top * unit_two, top, grad_low.astype(f32))
                return tuple(c + fold(v) for c, v in zip(carry, values))

            sums = strips(second_norm, (jnp.zeros((8, width), f32),) * 3)
            for i in range(3):
                sum_ref[i : i + 1, :] = jnp.sum(sums[i], axis=0, keepdims=True)
            for copy in sends((1, 2)):
                copy.start()

        @pl.when(t >= blocks)
        def _():
            w_in = w_all[t - blocks, 0].reshape(hidden_block, width)
            w_down = w_all[t - blocks, 1].reshape(hidden_block, width)
            total = jnp.zeros((8, hidden_block), f32)
            for m in range(tiles):
                at = slice(m * (count // tiles), (m + 1) * (count // tiles))
                grad_hidden = (dot_nt(gf[at, :], w_down) * slope[t - blocks, at, :].astype(f32)).astype(bf16)
                gh_ref[at, :] = grad_hidden
                total = total + fold(grad_hidden.astype(f32))
                acc[at, :] += dot_nn(grad_hidden, w_in)
            gb_ref[0] = jnp.sum(total, axis=0, keepdims=True)

        @pl.when(t == 2 * blocks - 1)
        def _():
            def first_back(at, carry):
                grad_one = acc[at, :]
                unit_one = unit[at, :]
                grad_res = norm_back(grad_one, unit_one, inv[at, 0:1], vec_ref[1:2, :])
                acc[at, :] = grad_res
                grad_low = grad_res.astype(bf16)
                low[at, :] = grad_low
                values = (grad_one * unit_one, grad_one, grad_low.astype(f32))
                return tuple(c + fold(v) for c, v in zip(carry, values))

            sums = strips(first_back, (jnp.zeros((8, width), f32),) * 3)
            for i in range(3):
                sum_ref[3 + i : 4 + i, :] = jnp.sum(sums[i], axis=0, keepdims=True)
            sum_ref[6:8, :] = jnp.zeros((2, width), f32)
            for copy in sends((3, 4)):
                copy.start()
            for k in range(nh):
                grad_ctx = dot_nt(low[...], wo_ref[k * cols : (k + 1) * cols, :]).astype(bf16)
                start = 0
                for c in range(nc):
                    gc_refs[k * nc + c][...] = grad_ctx[start : start + sizes[c]]
                    start += sizes[c]
            for k in range(nh):
                value, start = 0.0, 0
                for c in range(nc):
                    value = value + dot_tn(ctx[k * nc + c][...], low[start : start + sizes[c], :])
                    start += sizes[c]
                gwo_ref[k] = value.astype(bf16)
            for copy in sends(range(5)):
                copy.wait()

    tiles = 1
    anywhere = pl.BlockSpec(memory_space=pl.ANY)
    return pl.pallas_call(
        body,
        grid=(2 * blocks,),
        in_specs=[resident(p.shape) for k in ctx_pieces for p in k]
        + [
            resident(w_out.shape),
            resident((count, width)),
            resident((8, width)),
            pl.BlockSpec((1, 1, hidden_block), lambda t: (jnp.minimum(t, blocks - 1), 0, 0)),
            resident((count, width)),
        ]
        + [anywhere] * nw,
        out_specs=[anywhere] * 5
        + [
            pl.BlockSpec((count, hidden_block), lambda t: (0, jnp.minimum(t, blocks - 1))),
            pl.BlockSpec((count, hidden_block), lambda t: (0, jnp.maximum(t - blocks, 0))),
            pl.BlockSpec((1, 1, hidden_block), lambda t: (jnp.maximum(t - blocks, 0), 0, 0)),
            whole((8, width)),
        ]
        + [whole((n, cols)) for _ in range(nh) for n in sizes]
        + [resident((nh, cols, width))],
        out_shape=[
            jax.ShapeDtypeStruct((count, width), bf16),
            jax.ShapeDtypeStruct((count, width), bf16),
            jax.ShapeDtypeStruct((count, width), bf16),
            jax.ShapeDtypeStruct((count, width), f32),
            jax.ShapeDtypeStruct((count, width), bf16),
            jax.ShapeDtypeStruct((count, hidden), bf16),
            jax.ShapeDtypeStruct((count, hidden), bf16),
            jax.ShapeDtypeStruct((blocks, 1, hidden_block), f32),
            jax.ShapeDtypeStruct((8, width), f32),
        ]
        + [jax.ShapeDtypeStruct((n, cols), bf16) for _ in range(nh) for n in sizes]
        + [jax.ShapeDtypeStruct((nh, cols, width), bf16)],
        scratch_shapes=[
            pltpu.VMEM((blocks, 2, per_block, shard, width), bf16),
            pltpu.VMEM((blocks, count, hidden_block), bf16),
            pltpu.VMEM((count, width), f32),
            pltpu.VMEM((count, 128), f32),
            pltpu.VMEM((count, width), f32),
            pltpu.VMEM((count, width), bf16),
            pltpu.VMEM((count, width), bf16),
            pltpu.VMEM((count, width), bf16),
            pltpu.VMEM((count, width), bf16),
            pltpu.SemaphoreType.DMA((blocks,)),
            pltpu.SemaphoreType.DMA((5,)),
        ],
        compiler_params=params(),
        cost_estimate=cost(4 * count * width * (2 * hidden + width), 4 * hidden * (width + count), 2 * count * hidden),
        name="feed",
    )(*[p for k in ctx_pieces for p in k], w_out, tokens, vectors, bias_blocks, out_grad, *weights)


def weight_grad(left, right, blocks, stride, first, shard, by_place, addend):
    count, width = right.shape
    per_block = hidden_block // shard
    adding = addend is not None
    if by_place:
        spec = pl.BlockSpec((per_block, None, shard, width), lambda t: (0, t, 0, 0))
        shape = (per_block, blocks, shard, width)
    else:
        spec = pl.BlockSpec((None, per_block, shard, width), lambda t: (t, 0, 0, 0))
        shape = (blocks, per_block, shard, width)

    def body(left_ref, right_ref, *refs):
        value = dot_tn(left_ref[...], right_ref[...]).reshape(per_block, shard, width)
        if adding:
            value = value + refs[0][...].astype(f32)
        refs[-1][...] = value.astype(bf16)

    return pl.pallas_call(
        body,
        grid=(blocks,),
        in_specs=[pl.BlockSpec((count, hidden_block), lambda t: (0, first + stride * t)), whole((count, width))]
        + [spec] * adding,
        out_specs=spec,
        out_shape=jax.ShapeDtypeStruct(shape, bf16),
        compiler_params=params(),
        cost_estimate=cost(2 * count * width * hidden_block * blocks, 4 * hidden_block * blocks * (width + count)),
        name="weight_grad",
    )(left, right, *([addend] if adding else []))


def add_turned(pieces):
    def body(*refs):
        refs[-1][...] = sum_of([r[...] for r in refs[:-1]]).T

    rows, width = pieces[0].shape
    return pl.pallas_call(
        body,
        out_shape=jax.ShapeDtypeStruct((width, rows), f32),
        compiler_params=pltpu.CompilerParams(vmem_limit_bytes=32 * 1024 * 1024),
        name="add_turned",
    )(*pieces)


def turn_weights(mine, other, core):
    half, width = mine.shape
    half -= bias_rows
    cols = 2 * half // 3

    def body(core_ref, mine_ref, other_ref, out_ref, all_rows):
        @pl.when(core_ref[0] == 0)
        def _():
            all_rows[0:half, :] = mine_ref[0:half, :].astype(f32)
            all_rows[half : 2 * half, :] = other_ref[0:half, :].astype(f32)

        @pl.when(core_ref[0] != 0)
        def _():
            all_rows[0:half, :] = other_ref[0:half, :].astype(f32)
            all_rows[half : 2 * half, :] = mine_ref[0:half, :].astype(f32)

        for c in range(3):
            out_ref[c] = all_rows[c * cols : (c + 1) * cols, :].T

    return pl.pallas_call(
        body,
        grid_spec=pltpu.PrefetchScalarGridSpec(
            num_scalar_prefetch=1,
            grid=(1,),
            in_specs=[whole(mine.shape)] * 2,
            out_specs=whole((3, width, cols)),
            scratch_shapes=[pltpu.VMEM((2 * half, width), f32)],
        ),
        out_shape=jax.ShapeDtypeStruct((3, width, cols), f32),
        compiler_params=params(),
        name="turn_weights",
    )(core, mine, other)


class Links:
    def __init__(self, head_axes, row_axes, nh, nr):
        self.head_axes, self.row_axes, self.nh, self.nr = head_axes, row_axes, nh, nr
        self.axes = head_axes + row_axes
        self.factored = len(row_axes) == 2

    def swap(self, value, head_bits=0, row_bits=0):
        mask = head_bits * self.nr + row_bits
        return lax.ppermute(value, self.axes, [(i, i ^ mask) for i in range(self.nh * self.nr)])

    def sum_rows(self, value):
        bit = 1
        while bit < self.nr:
            value = value + self.swap(value, 0, bit)
            bit *= 2
        return value

    def sum_heads(self, value):
        bit = 1
        while bit < self.nh:
            value = value + self.swap(value, bit, 0)
            bit *= 2
        return value

    def sum_all(self, value):
        return self.sum_heads(self.sum_rows(value))


def after(value, *others):
    return lax.optimization_barrier((value, *others))[0]


def gather_tokens(links, tokens, chunks, small, early):
    own = [tokens[low : low + size] for low, size in chunks]
    if links.nh != 4:
        return [[(0, 0, t)] + [(k, 0, links.swap(t, k)) for k in range(1, links.nh)] for t in own], None
    result, others, gate = [], None, ()
    for mine in own:
        mine = after(mine, *gate)
        half = mine.shape[1] // 2
        beside, across = links.swap(mine, 1), links.swap(mine, 2)
        if others is None:
            others = exchange(links, small)
            beside, across = hold((beside, across), *early)
        else:
            beside, across = hold((beside, across), *far)
        far = links.swap(across[:, :half], 1), links.swap(beside[:, half:], 2)
        gate = (beside, across)
        result.append([(0, 0, mine), (1, 0, beside), (2, 0, across), (3, 0, far[0]), (3, half, far[1])])
    return result, others


def exchange_first(links, mine):
    return mine, links.swap(mine, 1), links.swap(mine, 2)


def exchange_second(links, mine, beside, across):
    half = mine.shape[0] // 2
    return mine, beside, across, links.swap(across[:half], 1), links.swap(beside[half:], 2)


def exchange(links, mine):
    return exchange_second(links, *exchange_first(links, mine))


def hold(values, *others):
    flat, tree = jax.tree.flatten(values)
    return jax.tree.unflatten(tree, lax.optimization_barrier((*flat, *others))[: len(flat)])


def all_weights(links, in_all, column, beside, across, low, high):
    mine = [in_all, column, beside, across, low, high]
    arrays = mine + [links.swap(a, 0, 1) for a in mine]
    plan = []
    for k in range(4):
        for base in (0, 6):
            copies = [(base, z * 4 + k, 1, 0, z) for z in range(4)]
            if k < 3:
                copies.append((base + 1 + k, 0, 4, 1, 0))
            else:
                copies += [(base + 4, 0, 2, 1, 0), (base + 5, 0, 2, 1, 2)]
            plan.append(copies)
    return arrays, plan


def by_core(first, second, core):
    return jnp.where(core == 0, first, second)


def add_low(a, b):
    return (a.astype(f32) + b.astype(f32)).astype(bf16)


def scatter_first(links, own, beside, across, far):
    half = far.shape[0] // 2
    return own, beside, across, links.swap(far[:half], 1), links.swap(far[half:], 2)


def scatter_second(links, own, beside, across, for_across, for_beside):
    half = for_across.shape[0]
    across = jnp.concatenate([add_low(across[:half], for_across), across[half:]])
    beside = jnp.concatenate([beside[:half], add_low(beside[half:], for_beside)])
    return own, links.swap(beside, 1), links.swap(across, 2)


def scatter_sum(own, beside, across):
    return own.astype(f32) + beside.astype(f32) + across.astype(f32)


def scatter_places(links, total):
    here = lax.axis_index("z")
    pieces = [lax.dynamic_index_in_dim(total, here ^ k, keepdims=False) for k in range(4)]
    return [pieces[0]] + [links.swap(pieces[k], 0, 2 * k) for k in range(1, 4)]


def sum_of(pieces):
    total = pieces[0].astype(f32)
    for piece in pieces[1:]:
        total = total + piece.astype(f32)
    return total


def core_half(links, value, axis):
    core = lax.axis_index("core")
    size = value.shape[axis] // 2
    keep = lax.dynamic_slice_in_dim(value, core * size, size, axis)
    give = lax.dynamic_slice_in_dim(value, (1 - core) * size, size, axis)
    return keep.astype(f32) + links.swap(give.astype(bf16), 0, 1).astype(f32)


def per_device(
    links,
    tokens,
    prev_logits,
    segment_ids,
    w_qkv,
    b_qv,
    w_out,
    b_out,
    ln1_gain,
    ln1_shift,
    w_in,
    b_in,
    w_down,
    b_down,
    ln2_gain,
    ln2_shift,
    out_grad,
    logit_grad,
):
    rows, part, width = tokens.shape
    heads = prev_logits.shape[1]
    cols = heads * head_dim
    shard = w_in.shape[1]
    count = rows * part
    nh, nr = links.nh, links.nr
    me = lax.axis_index(links.head_axes).astype(jnp.int32).reshape(1)
    place = lax.axis_index(links.axes)
    chunks = [(0, rows // 2), (rows // 2, rows - rows // 2)]

    bias_qv = b_qv.astype(f32)
    bias_row = jnp.concatenate([bias_qv[0], jnp.zeros_like(bias_qv[0]), bias_qv[1]])[None]
    w_flat = w_qkv.reshape(width, 3 * cols)
    seg_row = segment_ids[:, None, :]
    seg_col = segment_ids[:, :, None]
    shards = nh * nr
    mine = lax.broadcasted_iota(jnp.int32, (shards, 1), 0) == place
    bias_all = links.sum_all(jnp.where(mine, b_in.astype(f32)[None], 0.0))
    core = lax.axis_index("core") if links.factored else 0
    if links.factored:
        here_h = lax.axis_index(links.head_axes)
        order = jnp.stack(
            [(here_h ^ k) * nr + z * 2 + (core ^ c) for k in range(4) for c in range(2) for z in range(4)]
        )
        bias_blocks = bias_all[order].reshape(-1, 1, hidden_block)
        column = lax.all_gather(w_down[None], "z", axis=0, tiled=True)
        out_half = lax.dynamic_slice_in_dim(w_out, core * (cols // 2), cols // 2)
        small = jnp.concatenate([w_in.T, out_half])
    else:
        bias_blocks = bias_all.reshape(-1, 1, hidden_block)
        small = None
    blocks = bias_blocks.shape[0]
    vectors = jnp.stack(
        [
            b_out.astype(f32),
            ln1_gain,
            ln1_shift,
            b_down.astype(f32),
            ln2_gain,
            ln2_shift,
            jnp.zeros_like(ln1_gain),
            jnp.zeros_like(ln1_gain),
        ]
    )

    early = (bias_row, w_flat, seg_row, seg_col, vectors, bias_blocks)
    tok_pieces, others = gather_tokens(links, tokens, chunks, small, early)
    if links.factored:
        rows_in = [others[0][:shard], others[1][:shard], others[2][:shard], others[3]]
        in_all = lax.all_gather(
            after(jnp.stack(rows_in), column, *(p for _, _, p in tok_pieces[0][1:3])), "z", axis=0, tiled=True
        )
        arrived = [p for _, _, p in tok_pieces[1][1:3]]
        tok_pieces[0] = hold(tok_pieces[0], *arrived)
        tok_pieces[0] = [(k, off, p) for (k, off, _), (_, _, p) in zip(tok_pieces[1], tok_pieces[0])]
        weight_pieces = exchange_first(links, after(column, *arrived))

    raw_logits, saved, ctx_pieces = None, [], [[] for _ in range(nh)]
    for c, ((low, size), pieces) in enumerate(zip(chunks, tok_pieces)):
        if c and links.factored:
            weight_pieces = hold(weight_pieces, raw_logits_gate)
            weight_pieces = exchange_second(links, *weight_pieces)
            near = weight_pieces[1:3] + tuple(p[0] for p in ctx_pieces)
            pieces = [(k, off, after(p, *near) if k == 3 else p) for k, off, p in pieces]
        qkv, raw_logits, tok_all, lse, *ctx = attend(
            me, low, pieces, w_flat, bias_row, seg_row, seg_col, prev_logits, raw_logits
        )
        raw_logits_gate = ctx[0]
        saved.append((qkv, tok_all, lse))
        if c and links.factored:
            ctx = hold(ctx, *(p[0] for p in ctx_pieces))
        for k in range(nh):
            piece = links.swap(ctx[k], k) if k else ctx[k]
            ctx_pieces[k].append(piece.reshape(size * part, cols))
    if links.factored:
        weights, plan = all_weights(links, *hold([in_all, *weight_pieces], raw_logits_gate))
        rows_out = jnp.stack([others[0][shard:], others[1][shard:], others[2][shard:], others[4]])
        rows_out = after(rows_out, raw_logits_gate)
        theirs = links.swap(rows_out, 0, 1)
        w_out_all = jnp.stack([by_core(rows_out, theirs, core), by_core(theirs, rows_out, core)], axis=1)
        w_out_all = w_out_all.reshape(nh * cols, width)
    else:
        weights = [lax.all_gather(a[None], links.axes, axis=0, tiled=True) for a in (w_in.T, w_down)]
        per_block = hidden_block // shard
        plan = [[(side, t * per_block, per_block, side, 0) for side in range(2)] for t in range(blocks)]
        w_out_all = jnp.concatenate([w_out] + [links.swap(w_out, k) for k in range(1, nh)])
    layer_out, x_low, grad_ffn, grad_res, grad_low, active, grad_hidden, gb_in, norm_sums, *rest = feed(
        ctx_pieces,
        w_out_all,
        tokens.reshape(count, width),
        vectors,
        bias_blocks,
        weights,
        plan,
        out_grad.reshape(count, width),
    )
    ctx_grad, gwo = rest[:-1], rest[-1]
    nc = len(chunks)

    def send_ctx(c, *others):
        pieces = hold([ctx_grad[k * nc + c] for k in range(nh)], *others)
        return [(links.swap(p, k) if k else p).reshape(chunks[c][1], part, cols) for k, p in enumerate(pieces)]

    gb_in = gb_in.reshape(shards, shard)
    if links.factored:
        seq = jnp.arange(shards)
        gb_in = gb_in[((seq // nr) ^ here_h) * 8 + ((seq % 2) ^ core) * 4 + (seq % nr) // 2]
    sums = jnp.concatenate([norm_sums[:6], gb_in.reshape(-1, width)])
    ctx_grads = [send_ctx(0)]
    if links.factored:

        def core_swap(g):
            return links.swap(g.reshape(-1, shard, width), 0, 1).reshape(g.shape)

        half = (blocks // 2, 2)
        down_theirs = weight_grad(active, grad_ffn, *half, 1, shard, False, None)
        in_theirs = weight_grad(after(grad_hidden, down_theirs), x_low, *half, 1, shard, True, None)
        down_swapped, in_swapped = core_swap(down_theirs), core_swap(in_theirs)
        ctx_grads.append(send_ctx(1, in_theirs, *ctx_grads[0]))
        gwo = core_half(links, after(gwo, down_theirs), 1).astype(bf16)
        down_own = weight_grad(after(active, in_theirs), grad_ffn, *half, 0, shard, False, down_swapped)
        gwo = after(gwo, down_own, *ctx_grads[0])
        gwo_parts = [gwo[0]] + [links.swap(gwo[k], k) for k in range(1, nh)]
        down_state = scatter_first(links, *(down_own[k] for k in range(4)))
        in_own = weight_grad(after(grad_hidden, down_own), x_low, *half, 0, shard, True, in_swapped)
        in_sum = lax.psum_scatter(in_own.reshape(-1, shard, width), "z", scatter_dimension=0, tiled=True)
        ctx_grads[0] = hold(ctx_grads[0], in_own, *down_state[3:], *ctx_grads[1])
        down_state = scatter_second(links, *hold(down_state, in_own))
        sums = links.sum_rows(after(sums, in_theirs))
    else:
        ctx_grads.append(send_ctx(1))
        own = [
            weight_grad(left, right, blocks, 1, 0, shard, False, None)
            for left, right in ((grad_hidden, x_low), (active, grad_ffn))
        ]
        own_in, own_down = (
            lax.psum_scatter(g.reshape(-1, shard, width), links.axes, scatter_dimension=0, tiled=True)[0] for g in own
        )
        own_in = own_in.astype(f32).T
        gwo_parts = [gwo[0]] + [links.swap(gwo[k], k) for k in range(1, nh)]
        sums = links.sum_rows(sums)

    so_far, returned = None, []
    for c, (low, size) in enumerate(chunks):
        qkv, tok_all, lse = saved[c]
        if links.factored and c:
            down_state, gwo_parts, sums = hold((down_state, gwo_parts, sums), gw)
            down_parts = scatter_places(links, scatter_sum(*down_state).astype(bf16))
            sums = links.sum_heads(sums)
            gwo_total = sum_of(gwo_parts)
            ctx_grads[c] = hold(ctx_grads[c], gwo_total)
        prev_grad, gw, *input_part = attend_back(
            me, low, tok_all, ctx_grads[c], qkv, prev_logits, logit_grad, seg_row, seg_col, lse, w_flat, so_far
        )
        so_far = (prev_grad, gw)
        if links.factored and c:
            gw = core_half(links, after(gw, in_sum), 0)[0].astype(bf16)
            input_part = hold(input_part, gw, *returned[-1])
        returned.append([input_part[0]] + [links.swap(input_part[k], k) for k in range(1, nh)])
    if links.factored:
        in_sum = after(in_sum, gw)
        in_state = scatter_first(links, *(in_sum[k] for k in range(4)))
        own_in = add_turned(scatter_second(links, *in_state))
        own_down = sum_of(down_parts)
        gwo_total, gw = lax.psum((gwo_total.astype(bf16), gw), "z")
        gwo_other, gw_other = links.swap(gwo_total, 0, 1), links.swap(gw, 0, 1)
        grad_w_out = jnp.concatenate([by_core(gwo_total, gwo_other, core), by_core(gwo_other, gwo_total, core)])
        grad_w_qkv = turn_weights(gw, gw_other, core.astype(jnp.int32).reshape(1)).transpose(1, 0, 2)
        gb = gw[-1].astype(f32)
    else:
        sums = links.sum_heads(sums)
        grad_w_out, gw = lax.psum((sum_of(gwo_parts).astype(bf16), gw.astype(bf16)), links.row_axes)
        grad_w_qkv = gw[:, :-bias_rows].astype(f32).reshape(3 * cols, width).T.reshape(width, 3, cols)
        gb = gw[0, -1].astype(f32)
    parts = []
    for (low, size), pieces in zip(chunks, returned):
        total = grad_res.reshape(rows, part, width)[low : low + size]
        for piece in pieces:
            total = total + piece.astype(f32)
        parts.append(total)
    tokens_grad = jnp.concatenate(parts)
    grad_b_qv = jnp.stack([gb[:cols], gb[2 * cols : 3 * cols]])
    totals = sums
    grad_b_in = lax.dynamic_slice_in_dim(totals[6:].reshape(-1), place * shard, shard)
    return (
        layer_out.reshape(rows, part, width),
        raw_logits,
        tokens_grad,
        prev_grad,
        grad_w_qkv,
        grad_b_qv,
        grad_w_out.astype(f32),
        totals[5],
        totals[3],
        totals[4],
        own_in,
        grad_b_in,
        own_down.astype(f32),
        totals[2],
        totals[0],
        totals[1],
    )


def solution(mesh):
    nh, nr = mesh.shape["head"], mesh.shape["row"]
    if (nh, nr) == (4, 8):
        head, row = ("y", "x"), ("z", "core")
        mesh = Mesh(mesh.devices.reshape(2, 2, 4, 2), head + row)
    else:
        head, row = ("head",), ("row",)
    every = head + row
    placed = (
        P(row, head, None),
        P(row, head, None, None),
        P(row, None),
        P(None, None, head),
        P(None, head),
        P(head, None),
        P(),
        P(),
        P(),
        P(None, every),
        P(every),
        P(every, None),
        P(),
        P(),
        P(),
        P(row, head, None),
        P(row, head, None, None),
    )
    return jax.shard_map(
        functools.partial(per_device, Links(head, row, nh, nr)),
        mesh=mesh,
        in_specs=placed,
        out_specs=(
            P(row, head, None),
            P(row, head, None, None),
            P(row, head, None),
            P(row, head, None, None),
            P(None, None, head),
            P(None, head),
            P(head, None),
            P(),
            P(),
            P(),
            P(None, every),
            P(every),
            P(every, None),
            P(),
            P(),
            P(),
        ),
        check_vma=False,
    )
```

```python
import functools

import jax
import jax.numpy as jnp
from jax import lax
from jax.experimental import pallas as pl
from jax.experimental.pallas import tpu as pltpu
from jax.sharding import Mesh
from jax.sharding import PartitionSpec as P

norm_eps = 1e-12
masked_fill = -1000000000.0
head_dim = 64
hidden_block = 512
bias_rows = 16
bf16 = jnp.bfloat16
f32 = jnp.float32


def dot_nn(a, b):
    return lax.dot_general(a, b, (((1,), (0,)), ((), ())), preferred_element_type=f32)


def dot_nt(a, b):
    return lax.dot_general(a, b, (((1,), (1,)), ((), ())), preferred_element_type=f32)


def dot_tn(a, b):
    return lax.dot_general(a, b, (((0,), (0,)), ((), ())), preferred_element_type=f32)


def params(limit_mib=60):
    return pltpu.CompilerParams(
        dimension_semantics=("arbitrary",), vmem_limit_bytes=limit_mib * 1024 * 1024
    )


def cost(flops, nbytes, exps=0):
    return pl.CostEstimate(flops=int(flops), bytes_accessed=int(nbytes), transcendentals=int(exps))


def whole(shape):
    return pl.BlockSpec(shape, lambda *_: (0,) * len(shape))


def by_step(shape, axis=0):
    return pl.BlockSpec(shape, lambda t, *_: tuple(t if d == axis else 0 for d in range(len(shape))))


def norm_parts(values):
    center = jnp.mean(values, axis=-1, keepdims=True)
    offset = values - center
    inverse = lax.rsqrt(jnp.mean(offset * offset, axis=-1, keepdims=True) + norm_eps)
    return offset * inverse, inverse


def norm_back(grad_in, unit_vals, inverse, gain_vec):
    scaled = grad_in * gain_vec
    return inverse * (
        scaled
        - jnp.mean(scaled, axis=-1, keepdims=True)
        - unit_vals * jnp.mean(scaled * unit_vals, axis=-1, keepdims=True)
    )


def lane_halves():
    lane = lax.broadcasted_iota(jnp.int32, (1, 2 * head_dim), 1)
    return lane < head_dim


def attend(me, first, pieces, w_flat, bias_row, seg_row, seg_col, prev, raw_so_far):
    total_rows, heads, slots, _ = prev.shape
    rows, _, width = pieces[0][2].shape
    cols = heads * head_dim
    nh = len({k for k, _, _ in pieces})
    part = slots // nh
    scale = head_dim ** (-0.5)
    np_ = len(pieces)
    places = [(k, off, p.shape[1]) for k, off, p in pieces]
    chained = raw_so_far is not None

    def body(me_ref, *refs):
        toks = refs[:np_]
        w_ref, b_ref, sr_ref, sc_ref, prev_ref = refs[np_ : np_ + 5]
        outs = refs[np_ + 5 + chained :]
        qkv_ref, raw_ref, tok_all, lse_ref = outs[:4]
        ctx_refs = outs[4 : 4 + nh]
        ctx_all = outs[4 + nh]
        mine = me_ref[0]
        for ref, (k, off, size) in zip(toks, places):
            tok_all[0, pl.ds(pl.multiple_of((mine ^ k) * part + off, size), size), :] = ref[0]
        qkv_ref[0] = (dot_nn(tok_all[0], w_ref[...]) + b_ref[...]).astype(bf16)
        low_half = lane_halves()
        keep = [jnp.where(low_half, scale, 0.0).astype(bf16), jnp.where(low_half, 0.0, scale).astype(bf16)]
        lane = lax.broadcasted_iota(jnp.int32, (1, 128), 1)
        same = sc_ref[0] == sr_ref[0]
        lse_tile = jnp.zeros((slots, 128), f32)
        for pair in range(heads // 2):
            span = slice(pair * 128, pair * 128 + 128)
            q_pair = qkv_ref[0, :, span]
            k_pair = qkv_ref[0, :, cols + pair * 128 : cols + pair * 128 + 128]
            v_pair = qkv_ref[0, :, 2 * cols + pair * 128 : 2 * cols + pair * 128 + 128]
            outs = []
            for half in range(2):
                h = 2 * pair + half
                raw = dot_nt(q_pair * keep[half], k_pair) + prev_ref[0, h].astype(f32)
                raw_ref[0, h] = raw.astype(bf16)
                masked = jnp.where(same, raw, masked_fill)
                top = jnp.max(masked, axis=-1, keepdims=True)
                grown = jnp.exp(masked - top)
                total = jnp.sum(grown, axis=-1, keepdims=True)
                probs = (grown * (1.0 / total)).astype(bf16)
                outs.append(dot_nn(probs, v_pair))
                lse_tile = jnp.where(lane == h, top + jnp.log(total), lse_tile)
            ctx_all[:, span] = jnp.where(low_half, outs[0], outs[1]).astype(bf16)
        lse_ref[0] = lse_tile
        for k in range(nh):
            ctx_refs[k][0] = ctx_all[pl.ds(pl.multiple_of((mine ^ k) * part, part), part), :]

    def shifted(shape):
        return pl.BlockSpec(shape, lambda r, *_: (first + r,) + (0,) * (len(shape) - 1))

    return pl.pallas_call(
        body,
        grid_spec=pltpu.PrefetchScalarGridSpec(
            num_scalar_prefetch=1,
            grid=(rows,),
            in_specs=[by_step((1,) + p.shape[1:]) for _, _, p in pieces]
            + [
                whole((width, 3 * cols)),
                whole((1, 3 * cols)),
                shifted((1, 1, slots)),
                shifted((1, slots, 1)),
                shifted((1, heads, slots, slots)),
            ]
            + [pl.BlockSpec(memory_space=pl.ANY)] * chained,
            out_specs=[
                by_step((1, slots, 3 * cols)),
                shifted((1, heads, slots, slots)),
                by_step((1, slots, width)),
                by_step((1, slots, 128)),
            ]
            + [by_step((1, part, cols))] * nh,
            scratch_shapes=[pltpu.VMEM((slots, cols), bf16)],
        ),
        out_shape=[
            jax.ShapeDtypeStruct((rows, slots, 3 * cols), bf16),
            jax.ShapeDtypeStruct((total_rows, heads, slots, slots), bf16),
            jax.ShapeDtypeStruct((rows, slots, width), bf16),
            jax.ShapeDtypeStruct((rows, slots, 128), f32),
        ]
        + [jax.ShapeDtypeStruct((rows, part, cols), bf16)] * nh,
        input_output_aliases={np_ + 6: 1} if chained else {},
        compiler_params=params(),
        cost_estimate=cost(
            2 * rows * slots * cols * (3 * width + 2 * slots), 5 * rows * heads * slots * slots, rows * heads * slots * slots
        ),
        name="attend",
    )(me, *[p for _, _, p in pieces], w_flat, bias_row, seg_row, seg_col, prev, *([raw_so_far] if chained else []))


def attend_back(me, first, tok, ctx_grads, qkv, prev, logit_grad, seg_row, seg_col, lse, w_flat, start_sums, so_far):
    total_rows, heads, slots, _ = prev.shape
    nh = len(ctx_grads)
    rows, _, width = tok.shape
    part = slots // nh
    cols = heads * head_dim
    half_rows = 3 * cols // 2
    scale = head_dim ** (-0.5)
    chained = so_far is not None

    def body(me_ref, *refs):
        grads = refs[:nh]
        tok_ref, qkv_ref, prev_ref, lg_ref, sr_ref, sc_ref, lse_ref, w_ref, sums_ref = refs[nh : nh + 9]
        rest = refs[nh + 9 :]
        if chained:
            gw_before = rest[1]
            rest = rest[2:]
        pg_ref, gw_ref = rest[:2]
        in_refs = rest[2 : 2 + nh]
        go_all, p_all, dt_all, in_all = rest[2 + nh :]
        mine = me_ref[0]
        for k in range(nh):
            go_all[pl.ds(pl.multiple_of((mine ^ k) * part, part), part), :] = grads[k][0]
        low_half = lane_halves()
        keep_q = [jnp.where(low_half, scale, 0.0).astype(bf16), jnp.where(low_half, 0.0, scale).astype(bf16)]
        keep_g = [jnp.where(low_half, 1.0, 0.0).astype(bf16), jnp.where(low_half, 0.0, 1.0).astype(bf16)]

        same = sc_ref[0] == sr_ref[0]
        for pair in range(heads // 2):
            span = slice(pair * 128, pair * 128 + 128)
            q_pair = qkv_ref[0, :, span]
            g_pair = go_all[:, span]
            k_pair = qkv_ref[0, :, cols + pair * 128 : cols + pair * 128 + 128]
            v_pair = qkv_ref[0, :, 2 * cols + pair * 128 : 2 * cols + pair * 128 + 128]
            for half in range(2):
                h = 2 * pair + half
                raw = dot_nt(q_pair * keep_q[half], k_pair) + prev_ref[0, h].astype(f32)
                probs = jnp.exp(jnp.where(same, raw, masked_fill) - lse_ref[0, :, h : h + 1])
                p_all[h] = probs.astype(bf16)
                pulled = probs * dot_nt(g_pair * keep_g[half], v_pair)
                inner = jnp.sum(pulled, axis=-1, keepdims=True)
                pg_ref[0, h] = (pulled - probs * inner + lg_ref[0, h].astype(f32)).astype(bf16)
        q_t = qkv_ref[0, :, :cols].T
        k_t = qkv_ref[0, :, cols : 2 * cols].T
        g_t = go_all[...].T
        for h in range(heads):
            span = slice(h * head_dim, h * head_dim + head_dim)
            grad_raw = pg_ref[0, h]
            dt_all[h * head_dim : (h + 1) * head_dim, :] = (dot_nt(k_t[span], grad_raw) * scale).astype(bf16)
            dt_all[cols + h * head_dim : cols + (h + 1) * head_dim, :] = (dot_nn(q_t[span], grad_raw) * scale).astype(bf16)
            dt_all[2 * cols + h * head_dim : 2 * cols + (h + 1) * head_dim, :] = dot_nn(g_t[span], p_all[h]).astype(bf16)
        grad_qkv = dt_all[...].T
        in_all[...] = dot_nt(grad_qkv, w_ref[...]).astype(bf16)
        for k in range(nh):
            in_refs[k][0] = in_all[pl.ds(pl.multiple_of((mine ^ k) * part, part), part), :]
        starts = pl.program_id(0) == 0

        @pl.when(starts)
        def _():
            if chained:
                gw_ref[...] = gw_before[...]
                for half in range(2):
                    gw_ref[half, half_rows:, :] += sums_ref[...]
            else:
                gw_ref[...] = jnp.zeros_like(gw_ref)

        first_row = lax.broadcasted_iota(jnp.int32, (bias_rows, 1), 0) == 0
        gb = jnp.where(first_row, dot_nn(jnp.ones((bias_rows, slots), bf16), grad_qkv), 0.0)
        for half in range(2):
            gw_ref[half, : half_rows, :] += dot_nn(dt_all[half * half_rows : (half + 1) * half_rows, :], tok_ref[0])
            gw_ref[half, half_rows:, : 3 * cols] += gb

    def shifted(shape):
        return pl.BlockSpec(shape, lambda r, *_: (first + r,) + (0,) * (len(shape) - 1))

    sums = [whole((2, half_rows + bias_rows, width))]
    return pl.pallas_call(
        body,
        grid_spec=pltpu.PrefetchScalarGridSpec(
            num_scalar_prefetch=1,
            grid=(rows,),
            in_specs=[by_step((1, part, cols))] * nh
            + [
                by_step((1, slots, width)),
                by_step((1, slots, 3 * cols)),
                shifted((1, heads, slots, slots)),
                shifted((1, heads, slots, slots)),
                shifted((1, 1, slots)),
                shifted((1, slots, 1)),
                by_step((1, slots, 128)),
                whole((width, 3 * cols)),
                whole((bias_rows, width)),
            ]
            + ([pl.BlockSpec(memory_space=pl.ANY)] + sums if chained else []),
            out_specs=[shifted((1, heads, slots, slots))] + sums + [by_step((1, part, width))] * nh,
            scratch_shapes=[
                pltpu.VMEM((slots, cols), bf16),
                pltpu.VMEM((heads, slots, slots), bf16),
                pltpu.VMEM((3 * cols, slots), bf16),
                pltpu.VMEM((slots, width), bf16),
            ],
        ),
        out_shape=[
            jax.ShapeDtypeStruct((total_rows, heads, slots, slots), bf16),
            jax.ShapeDtypeStruct((2, half_rows + bias_rows, width), f32),
        ]
        + [jax.ShapeDtypeStruct((rows, part, width), bf16)] * nh,
        input_output_aliases={nh + 10: 0} if chained else {},
        compiler_params=params(),
        cost_estimate=cost(
            2 * rows * slots * cols * (6 * width + 5 * slots), 7 * rows * heads * slots * slots, rows * heads * slots * slots
        ),
        name="attend_back",
    )(me, *ctx_grads, tok, qkv, prev, logit_grad, seg_row, seg_col, lse, w_flat, start_sums, *(so_far if chained else []))


def resident(shape):
    return pl.BlockSpec(shape, lambda *_: (0,) * len(shape), pipeline_mode=pl.Buffered(1))


def fold(values):
    return jnp.sum(values.reshape(values.shape[0] // 8, 8, values.shape[1]), axis=0)


def feed(ctx_pieces, w_out, tokens, vectors, bias_blocks, weights, plan, out_grad):
    count, width = tokens.shape
    nh, nc = len(ctx_pieces), len(ctx_pieces[0])
    cols = ctx_pieces[0][0].shape[1]
    sizes = [p.shape[0] for p in ctx_pieces[0]]
    blocks = len(plan)
    per_block = sum(size for _, _, size, side, _ in plan[0] if side == 0)
    shard = hidden_block // per_block
    hidden = blocks * hidden_block
    strip = 128
    nw = len(weights)
    riding = bias_blocks is None
    n_in = nh * nc + 5 - riding + nw

    def body(*refs):
        ctx = refs[: nh * nc]
        wo_ref, tok_ref, vec_ref, og_ref = refs[nh * nc : nh * nc + 4]
        bias_ref = None if riding else refs[nh * nc + 4]
        w_refs = refs[n_in - nw : n_in]
        res_out, x_out, gf_out, gres_out, low_out, act_ref, gh_ref, gb_ref, sum_ref = refs[n_in : n_in + 9]
        gc_refs = refs[n_in + 9 : n_in + 9 + nh * nc]
        gwo_ref = refs[n_in + 9 + nh * nc]
        w_all, b_all, slope, unit, inv, acc, x_low, res, gf, low, w_sem, b_sem, out_sem = refs[n_in + 10 + nh * nc :]
        t = pl.program_id(0)

        def sends(which):
            pairs = ((x_low, x_out), (res, res_out), (gf, gf_out), (acc, gres_out), (low, low_out))
            return [pltpu.make_async_copy(*pairs[i], out_sem.at[i]) for i in which]

        def strips(step, init):
            def one(i, carry):
                return step(pl.ds(pl.multiple_of(i * strip, strip), strip), carry)

            return lax.fori_loop(0, count // strip, one, init)

        @pl.when(t == 0)
        def _():
            for block, copies in enumerate(plan):
                for array, low_shard, size, side, to in copies:
                    source = w_refs[array].at[pl.ds(low_shard, size)]
                    pltpu.make_async_copy(
                        source.at[:, pl.ds(0, shard)], w_all.at[block, side, pl.ds(to, size)], w_sem.at[block]
                    ).start()
                    if riding and side:
                        pltpu.make_async_copy(
                            source.at[:, pl.ds(shard, bias_rows), pl.ds(0, shard)],
                            b_all.at[block, pl.ds(to, size)],
                            b_sem.at[block],
                        ).start()
            start = 0
            for c in range(nc):
                at = slice(start, start + sizes[c])
                start += sizes[c]
                branch = dot_nn(ctx[c][...], wo_ref[0:cols, :])
                for k in range(1, nh):
                    branch = branch + dot_nn(ctx[k * nc + c][...], wo_ref[k * cols : (k + 1) * cols, :])
                acc[at, :] = branch

            def first_norm(at, carry):
                unit_one, inverse = norm_parts(tok_ref[at, :].astype(f32) + (acc[at, :] + vec_ref[0:1, :]))
                unit[at, :] = unit_one
                inv[at, :] = jnp.broadcast_to(inverse, (strip, 128))
                normed = unit_one * vec_ref[1:2, :] + vec_ref[2:3, :]
                x_low[at, :] = normed.astype(bf16)
                acc[at, :] = normed + vec_ref[3:4, :]
                return carry

            strips(first_norm, 0)
            sends((0,))[0].start()

        @pl.when(t < blocks)
        def _():
            pltpu.make_async_copy(w_all.at[t], w_all.at[t], w_sem.at[t]).wait()
            if riding:
                pltpu.make_async_copy(b_all.at[t], b_all.at[t], b_sem.at[t]).wait()
                bias = jnp.concatenate([b_all[t, j, 0:1, :].astype(f32) for j in range(per_block)], axis=1)
            else:
                bias = bias_ref[0]
            w_in = w_all[t, 0].reshape(hidden_block, width)
            w_down = w_all[t, 1].reshape(hidden_block, width)
            for m in range(tiles):
                at = slice(m * (count // tiles), (m + 1) * (count // tiles))
                pre = dot_nt(x_low[at, :], w_in) + bias
                below = 0.5 * (1.0 + lax.erf(pre * (0.5**0.5)))
                active = (pre * below).astype(bf16)
                act_ref[at, :] = active
                slope[t, at, :] = (below + pre * (jnp.exp(-0.5 * pre * pre) * 0.3989422804014327)).astype(bf16)
                acc[at, :] += dot_nn(active, w_down)

        @pl.when(t == blocks - 1)
        def _():
            def second_norm(at, carry):
                unit_two, inverse = norm_parts(acc[at, :])
                res[at, :] = (unit_two * vec_ref[4:5, :] + vec_ref[5:6, :]).astype(bf16)
                top = og_ref[at, :].astype(f32)
                grad_two = norm_back(top, unit_two, inverse, vec_ref[4:5, :])
                acc[at, :] = grad_two
                grad_low = grad_two.astype(bf16)
                gf[at, :] = grad_low
                values = (top * unit_two, top, grad_low.astype(f32))
                return tuple(c + fold(v) for c, v in zip(carry, values))

            sums = strips(second_norm, (jnp.zeros((8, width), f32),) * 3)
            for i in range(3):
                sum_ref[i : i + 1, :] = jnp.sum(sums[i], axis=0, keepdims=True)
            for copy in sends((1, 2)):
                copy.start()

        @pl.when(t >= blocks)
        def _():
            w_in = w_all[t - blocks, 0].reshape(hidden_block, width)
            w_down = w_all[t - blocks, 1].reshape(hidden_block, width)
            total = jnp.zeros((8, hidden_block), f32)
            for m in range(tiles):
                at = slice(m * (count // tiles), (m + 1) * (count // tiles))
                grad_hidden = (dot_nt(gf[at, :], w_down) * slope[t - blocks, at, :].astype(f32)).astype(bf16)
                gh_ref[at, :] = grad_hidden
                total = total + fold(grad_hidden.astype(f32))
                acc[at, :] += dot_nn(grad_hidden, w_in)
            gb_ref[0] = jnp.sum(total, axis=0, keepdims=True)

        @pl.when(t == 2 * blocks - 1)
        def _():
            def first_back(at, carry):
                grad_one = acc[at, :]
                unit_one = unit[at, :]
                grad_res = norm_back(grad_one, unit_one, inv[at, 0:1], vec_ref[1:2, :])
                acc[at, :] = grad_res
                grad_low = grad_res.astype(bf16)
                low[at, :] = grad_low
                values = (grad_one * unit_one, grad_one, grad_low.astype(f32))
                return tuple(c + fold(v) for c, v in zip(carry, values))

            sums = strips(first_back, (jnp.zeros((8, width), f32),) * 3)
            for i in range(3):
                sum_ref[3 + i : 4 + i, :] = jnp.sum(sums[i], axis=0, keepdims=True)
            sum_ref[6:8, :] = jnp.zeros((2, width), f32)
            for copy in sends((3, 4)):
                copy.start()
            for k in range(nh):
                grad_ctx = dot_nt(low[...], wo_ref[k * cols : (k + 1) * cols, :]).astype(bf16)
                start = 0
                for c in range(nc):
                    gc_refs[k * nc + c][...] = grad_ctx[start : start + sizes[c]]
                    start += sizes[c]
            for k in range(nh):
                value, start = 0.0, 0
                for c in range(nc):
                    value = value + dot_tn(ctx[k * nc + c][...], low[start : start + sizes[c], :])
                    start += sizes[c]
                gwo_ref[k] = value.astype(bf16)
            for copy in sends(range(5)):
                copy.wait()

    tiles = 1
    anywhere = pl.BlockSpec(memory_space=pl.ANY)
    return pl.pallas_call(
        body,
        grid=(2 * blocks,),
        in_specs=[resident(p.shape) for k in ctx_pieces for p in k]
        + [
            resident(w_out.shape),
            resident((count, width)),
            resident((8, width)),
            resident((count, width)),
        ]
        + [pl.BlockSpec((1, 1, hidden_block), lambda t: (jnp.minimum(t, blocks - 1), 0, 0))] * (not riding)
        + [anywhere] * nw,
        out_specs=[anywhere] * 5
        + [
            pl.BlockSpec((count, hidden_block), lambda t: (0, jnp.minimum(t, blocks - 1))),
            pl.BlockSpec((count, hidden_block), lambda t: (0, jnp.maximum(t - blocks, 0))),
            pl.BlockSpec((1, 1, hidden_block), lambda t: (jnp.maximum(t - blocks, 0), 0, 0)),
            whole((8, width)),
        ]
        + [whole((n, cols)) for _ in range(nh) for n in sizes]
        + [resident((nh, cols, width))],
        out_shape=[
            jax.ShapeDtypeStruct((count, width), bf16),
            jax.ShapeDtypeStruct((count, width), bf16),
            jax.ShapeDtypeStruct((count, width), bf16),
            jax.ShapeDtypeStruct((count, width), f32),
            jax.ShapeDtypeStruct((count, width), bf16),
            jax.ShapeDtypeStruct((count, hidden), bf16),
            jax.ShapeDtypeStruct((count, hidden), bf16),
            jax.ShapeDtypeStruct((blocks, 1, hidden_block), f32),
            jax.ShapeDtypeStruct((8, width), f32),
        ]
        + [jax.ShapeDtypeStruct((n, cols), bf16) for _ in range(nh) for n in sizes]
        + [jax.ShapeDtypeStruct((nh, cols, width), bf16)],
        scratch_shapes=[
            pltpu.VMEM((blocks, 2, per_block, shard, width), bf16),
            pltpu.VMEM((blocks, per_block, bias_rows, shard), bf16),
            pltpu.VMEM((blocks, count, hidden_block), bf16),
            pltpu.VMEM((count, width), f32),
            pltpu.VMEM((count, 128), f32),
            pltpu.VMEM((count, width), f32),
            pltpu.VMEM((count, width), bf16),
            pltpu.VMEM((count, width), bf16),
            pltpu.VMEM((count, width), bf16),
            pltpu.VMEM((count, width), bf16),
            pltpu.SemaphoreType.DMA((blocks,)),
            pltpu.SemaphoreType.DMA((blocks,)),
            pltpu.SemaphoreType.DMA((5,)),
        ],
        compiler_params=params(),
        cost_estimate=cost(4 * count * width * (2 * hidden + width), 4 * hidden * (width + count), 2 * count * hidden),
        name="feed",
    )(*[p for k in ctx_pieces for p in k], w_out, tokens, vectors, out_grad, *([] if riding else [bias_blocks]), *weights)


def weight_grad(left, right, blocks, stride, first, shard, by_place, addend):
    count, width = right.shape
    per_block = hidden_block // shard
    adding = addend is not None
    if by_place:
        spec = pl.BlockSpec((per_block, None, shard, width), lambda t: (0, t, 0, 0))
        shape = (per_block, blocks, shard, width)
    else:
        spec = pl.BlockSpec((None, per_block, shard, width), lambda t: (t, 0, 0, 0))
        shape = (blocks, per_block, shard, width)

    def body(left_ref, right_ref, *refs):
        value = dot_tn(left_ref[...], right_ref[...]).reshape(per_block, shard, width)
        if adding:
            value = value + refs[0][...].astype(f32)
        refs[-1][...] = value.astype(bf16)

    return pl.pallas_call(
        body,
        grid=(blocks,),
        in_specs=[pl.BlockSpec((count, hidden_block), lambda t: (0, first + stride * t)), whole((count, width))]
        + [spec] * adding,
        out_specs=spec,
        out_shape=jax.ShapeDtypeStruct(shape, bf16),
        input_output_aliases={2: 0} if adding else {},
        compiler_params=params(),
        cost_estimate=cost(2 * count * width * hidden_block * blocks, 4 * hidden_block * blocks * (width + count)),
        name="weight_grad",
    )(left, right, *([addend] if adding else []))


def add_turned(pieces):
    def body(*refs):
        refs[-1][...] = sum_of([r[...] for r in refs[:-1]]).T

    rows, width = pieces[0].shape
    return pl.pallas_call(
        body,
        out_shape=jax.ShapeDtypeStruct((width, rows), f32),
        compiler_params=pltpu.CompilerParams(vmem_limit_bytes=32 * 1024 * 1024),
        name="add_turned",
    )(*pieces)


def turn_weights(mine, other, core):
    half, width = mine.shape
    half -= bias_rows
    cols = 2 * half // 3

    def body(core_ref, mine_ref, other_ref, out_ref, all_rows):
        @pl.when(core_ref[0] == 0)
        def _():
            all_rows[0:half, :] = mine_ref[0:half, :].astype(f32)
            all_rows[half : 2 * half, :] = other_ref[0:half, :].astype(f32)

        @pl.when(core_ref[0] != 0)
        def _():
            all_rows[0:half, :] = other_ref[0:half, :].astype(f32)
            all_rows[half : 2 * half, :] = mine_ref[0:half, :].astype(f32)

        for c in range(3):
            out_ref[c] = all_rows[c * cols : (c + 1) * cols, :].T

    return pl.pallas_call(
        body,
        grid_spec=pltpu.PrefetchScalarGridSpec(
            num_scalar_prefetch=1,
            grid=(1,),
            in_specs=[whole(mine.shape)] * 2,
            out_specs=whole((3, width, cols)),
            scratch_shapes=[pltpu.VMEM((2 * half, width), f32)],
        ),
        out_shape=jax.ShapeDtypeStruct((3, width, cols), f32),
        compiler_params=params(),
        name="turn_weights",
    )(core, mine, other)


class Links:
    def __init__(self, head_axes, row_axes, nh, nr):
        self.head_axes, self.row_axes, self.nh, self.nr = head_axes, row_axes, nh, nr
        self.axes = head_axes + row_axes
        self.factored = len(row_axes) == 2

    def swap(self, value, head_bits=0, row_bits=0):
        mask = head_bits * self.nr + row_bits
        return lax.ppermute(value, self.axes, [(i, i ^ mask) for i in range(self.nh * self.nr)])

    def sum_rows(self, value):
        bit = 1
        while bit < self.nr:
            value = value + self.swap(value, 0, bit)
            bit *= 2
        return value

    def sum_heads(self, value):
        bit = 1
        while bit < self.nh:
            value = value + self.swap(value, bit, 0)
            bit *= 2
        return value

    def sum_all(self, value):
        return self.sum_heads(self.sum_rows(value))


def after(value, *others):
    return lax.optimization_barrier((value, *others))[0]


def gather_tokens(links, tokens, chunks, small, early):
    own = [tokens[low : low + size] for low, size in chunks]
    if links.nh != 4:
        return [[(0, 0, t)] + [(k, 0, links.swap(t, k)) for k in range(1, links.nh)] for t in own], None
    result, others, gate = [], None, ()
    for mine in own:
        mine = after(mine, *gate)
        half = mine.shape[1] // 2
        beside, across = links.swap(mine, 1), links.swap(mine, 2)
        if others is None:
            others = exchange(links, small)
            beside, across = hold((beside, across), *early)
        else:
            beside, across = hold((beside, across), *far)
        far = links.swap(across[:, :half], 1), links.swap(beside[:, half:], 2)
        gate = (beside, across)
        result.append([(0, 0, mine), (1, 0, beside), (2, 0, across), (3, 0, far[0]), (3, half, far[1])])
    return result, others


def exchange_first(links, mine):
    return mine, links.swap(mine, 1), links.swap(mine, 2)


def exchange_second(links, mine, beside, across):
    half = mine.shape[0] // 2
    return mine, beside, across, links.swap(across[:half], 1), links.swap(beside[half:], 2)


def exchange(links, mine):
    return exchange_second(links, *exchange_first(links, mine))


def hold(values, *others):
    flat, tree = jax.tree.flatten(values)
    return jax.tree.unflatten(tree, lax.optimization_barrier((*flat, *others))[: len(flat)])


def all_weights(links, in_all, column, beside, across, low, high):
    mine = [in_all, column, beside, across, low, high]
    arrays = mine + [links.swap(a, 0, 1) for a in mine]
    plan = []
    for k in range(4):
        for base in (0, 6):
            copies = [(base, z * 4 + k, 1, 0, z) for z in range(4)]
            if k < 3:
                copies.append((base + 1 + k, 0, 4, 1, 0))
            else:
                copies += [(base + 4, 0, 2, 1, 0), (base + 5, 0, 2, 1, 2)]
            plan.append(copies)
    return arrays, plan


def by_core(first, second, core):
    return jnp.where(core == 0, first, second)


def add_low(a, b):
    return (a.astype(f32) + b.astype(f32)).astype(bf16)


def scatter_first(links, own, beside, across, far):
    half = far.shape[0] // 2
    return own, beside, across, links.swap(far[:half], 1), links.swap(far[half:], 2)


def scatter_second(links, own, beside, across, for_across, for_beside):
    half = for_across.shape[0]
    across = jnp.concatenate([add_low(across[:half], for_across), across[half:]])
    beside = jnp.concatenate([beside[:half], add_low(beside[half:], for_beside)])
    return own, links.swap(beside, 1), links.swap(across, 2)


def scatter_sum(own, beside, across):
    return own.astype(f32) + beside.astype(f32) + across.astype(f32)


def scatter_places(links, total):
    here = lax.axis_index("z")
    pieces = [lax.dynamic_index_in_dim(total, here ^ k, keepdims=False) for k in range(4)]
    return [pieces[0]] + [links.swap(pieces[k], 0, 2 * k) for k in range(1, 4)]


def sum_of(pieces):
    total = pieces[0].astype(f32)
    for piece in pieces[1:]:
        total = total + piece.astype(f32)
    return total


def core_half(links, value, axis):
    core = lax.axis_index("core")
    size = value.shape[axis] // 2
    keep = lax.dynamic_slice_in_dim(value, core * size, size, axis)
    give = lax.dynamic_slice_in_dim(value, (1 - core) * size, size, axis)
    return keep.astype(f32) + links.swap(give.astype(bf16), 0, 1).astype(f32)


def per_device(
    links,
    tokens,
    prev_logits,
    segment_ids,
    w_qkv,
    b_qv,
    w_out,
    b_out,
    ln1_gain,
    ln1_shift,
    w_in,
    b_in,
    w_down,
    b_down,
    ln2_gain,
    ln2_shift,
    out_grad,
    logit_grad,
):
    rows, part, width = tokens.shape
    heads = prev_logits.shape[1]
    cols = heads * head_dim
    shard = w_in.shape[1]
    count = rows * part
    nh, nr = links.nh, links.nr
    me = lax.axis_index(links.head_axes).astype(jnp.int32).reshape(1)
    place = lax.axis_index(links.axes)
    chunks = [(0, rows // 2), (rows // 2, rows - rows // 2)]

    bias_qv = b_qv.astype(f32)
    bias_row = jnp.concatenate([bias_qv[0], jnp.zeros_like(bias_qv[0]), bias_qv[1]])[None]
    w_flat = w_qkv.reshape(width, 3 * cols)
    seg_row = segment_ids[:, None, :]
    seg_col = segment_ids[:, :, None]
    shards = nh * nr
    blocks = shards * shard // hidden_block
    core = lax.axis_index("core") if links.factored else 0
    if links.factored:
        here_h = lax.axis_index(links.head_axes)
        bias_blocks = None
        bias_row_in = jnp.pad(b_in[None], ((0, bias_rows - 1), (0, width - shard)))
        column = lax.all_gather(jnp.concatenate([w_down, bias_row_in])[None], "z", axis=0, tiled=True)
        out_half = lax.dynamic_slice_in_dim(w_out, core * (cols // 2), cols // 2)
        small = jnp.concatenate([w_in.T, out_half])
    else:
        mine = lax.broadcasted_iota(jnp.int32, (shards, 1), 0) == place
        bias_all = links.sum_all(jnp.where(mine, b_in.astype(f32)[None], 0.0))
        bias_blocks = bias_all.reshape(-1, 1, hidden_block)
        small = None
    vectors = jnp.stack(
        [
            b_out.astype(f32),
            ln1_gain,
            ln1_shift,
            b_down.astype(f32),
            ln2_gain,
            ln2_shift,
            jnp.zeros_like(ln1_gain),
            jnp.zeros_like(ln1_gain),
        ]
    )

    early = (bias_row, w_flat, seg_row, seg_col, vectors)
    tok_pieces, others = gather_tokens(links, tokens, chunks, small, early)
    if links.factored:
        rows_in = [others[0][:shard], others[1][:shard], others[2][:shard], others[3]]
        in_all = lax.all_gather(
            after(jnp.stack(rows_in), column, *(p for _, _, p in tok_pieces[0][1:3])), "z", axis=0, tiled=True
        )
        arrived = [p for _, _, p in tok_pieces[1][1:3]]
        tok_pieces[0] = hold(tok_pieces[0], *arrived)
        tok_pieces[0] = [(k, off, p) for (k, off, _), (_, _, p) in zip(tok_pieces[1], tok_pieces[0])]
        tok_pieces[1] = [(k, off, after(p, others[4]) if k in (1, 2) else p) for k, off, p in tok_pieces[1]]
        weight_pieces = exchange_first(links, after(column, *arrived, others[4]))

    raw_logits, saved, ctx_pieces = None, [], [[] for _ in range(nh)]
    for c, ((low, size), pieces) in enumerate(zip(chunks, tok_pieces)):
        if c and links.factored:
            weight_pieces = hold(weight_pieces, raw_logits_gate)
            weight_pieces = exchange_second(links, *weight_pieces)
            near = weight_pieces[1:3]
            pieces = [(k, off, after(p, *near) if k == 3 else p) for k, off, p in pieces]
        qkv, raw_logits, tok_all, lse, *ctx = attend(
            me, low, pieces, w_flat, bias_row, seg_row, seg_col, prev_logits, raw_logits
        )
        raw_logits_gate = ctx[0]
        saved.append((qkv, tok_all, lse))
        if c and links.factored:
            ctx = hold(ctx, *(p[0] for p in ctx_pieces), *weight_pieces[3:])
        for k in range(nh):
            piece = links.swap(ctx[k], k) if k else ctx[k]
            ctx_pieces[k].append(piece.reshape(size * part, cols))
    if links.factored:
        weights, plan = all_weights(links, *hold([in_all, *weight_pieces], raw_logits_gate, *(p[0] for p in ctx_pieces)))
        rows_out = jnp.stack([others[0][shard:], others[1][shard:], others[2][shard:], others[4]])
        rows_out = after(rows_out, raw_logits_gate, *(p[0] for p in ctx_pieces))
        theirs = links.swap(rows_out, 0, 1)
        w_out_all = jnp.stack([by_core(rows_out, theirs, core), by_core(theirs, rows_out, core)], axis=1)
        w_out_all = w_out_all.reshape(nh * cols, width)
    else:
        weights = [lax.all_gather(a[None], links.axes, axis=0, tiled=True) for a in (w_in.T, w_down)]
        per_block = hidden_block // shard
        plan = [[(side, t * per_block, per_block, side, 0) for side in range(2)] for t in range(blocks)]
        w_out_all = jnp.concatenate([w_out] + [links.swap(w_out, k) for k in range(1, nh)])
    layer_out, x_low, grad_ffn, grad_res, grad_low, active, grad_hidden, gb_in, norm_sums, *rest = feed(
        ctx_pieces,
        w_out_all,
        tokens.reshape(count, width),
        vectors,
        bias_blocks,
        weights,
        plan,
        out_grad.reshape(count, width),
    )
    ctx_grad, gwo = rest[:-1], rest[-1]
    nc = len(chunks)

    def send_ctx(c, *others):
        pieces = hold([ctx_grad[k * nc + c] for k in range(nh)], *others)
        return [(links.swap(p, k) if k else p).reshape(chunks[c][1], part, cols) for k, p in enumerate(pieces)]

    gb_in = gb_in.reshape(shards, shard)
    if links.factored:
        seq = jnp.arange(shards)
        gb_in = gb_in[((seq // nr) ^ here_h) * 8 + ((seq % 2) ^ core) * 4 + (seq % nr) // 2]
    sums = jnp.concatenate([norm_sums[:6], gb_in.reshape(-1, width)])
    ctx_grads = [send_ctx(0)]
    sums = jnp.pad(sums, ((1, bias_rows - 1 - sums.shape[0]), (0, 0)))
    if links.factored:

        def core_swap(g):
            return links.swap(g.reshape(-1, shard, width), 0, 1).reshape(g.shape)

        half = (blocks // 2, 2)
        down_theirs = weight_grad(active, grad_ffn, *half, 1, shard, False, None)
        sums = sums + links.swap(sums, 1)
        down_swapped = core_swap(after(down_theirs, sums, *ctx_grads[0]))
        ctx_grads.append(send_ctx(1, *ctx_grads[0]))
        in_theirs = weight_grad(after(grad_hidden, down_theirs, sums, *ctx_grads[0]), x_low, *half, 1, shard, True, None)
        gwo = core_half(links, after(gwo, down_theirs), 1).astype(bf16)
        in_swapped = core_swap(after(in_theirs, gwo, *ctx_grads[1]))
        sums = after(sums, down_theirs)
        sums = sums + links.swap(sums, 2)
        gwo_parts = [gwo[0]] + [links.swap(gwo[k], k) for k in range(1, nh)]
        down_own = weight_grad(after(active, in_theirs, sums), grad_ffn, *half, 0, shard, False, down_swapped)
        down_state = scatter_first(links, *(down_own[k] for k in range(4)))
        in_own = weight_grad(after(grad_hidden, down_own, *gwo_parts), x_low, *half, 0, shard, True, in_swapped)
        in_own = after(in_own, *down_state[3:])
        in_sum = lax.psum_scatter(in_own.reshape(-1, shard, width), "z", scatter_dimension=0, tiled=True)
        ctx_grads[0] = hold(ctx_grads[0], in_own)
        down_state = scatter_second(links, *hold(down_state, in_own))
    else:
        ctx_grads.append(send_ctx(1))
        own = [
            weight_grad(left, right, blocks, 1, 0, shard, False, None)
            for left, right in ((grad_hidden, x_low), (active, grad_ffn))
        ]
        own_in, own_down = (
            lax.psum_scatter(g.reshape(-1, shard, width), links.axes, scatter_dimension=0, tiled=True)[0] for g in own
        )
        own_in = own_in.astype(f32).T
        gwo_parts = [gwo[0]] + [links.swap(gwo[k], k) for k in range(1, nh)]
        sums = links.sum_heads(sums)

    so_far, returned = None, []
    for c, (low, size) in enumerate(chunks):
        qkv, tok_all, lse = saved[c]
        if links.factored and c:
            gwo_total = sum_of(hold(gwo_parts, gw)).astype(bf16)
            ctx_grads[c] = hold(ctx_grads[c], gwo_total, sums)
        prev_grad, gw, *input_part = attend_back(
            me, low, tok_all, ctx_grads[c], qkv, prev_logits, logit_grad, seg_row, seg_col, lse, w_flat, sums, so_far
        )
        so_far = (prev_grad, gw)
        if links.factored:
            if c:
                gw = core_half(links, after(gw, *returned[0]), 0)[0].astype(bf16)
                gw, in_sum = hold((gw, in_sum))
                input_part = hold(input_part, gw)
            else:
                input_part = hold(input_part, *down_state[1:])
        returned.append([input_part[0]] + [links.swap(input_part[k], k) for k in range(1, nh)])
    if links.factored:
        down_state = hold(down_state, *returned[1][1:3])
        in_sum = after(in_sum, *returned[1])
        down_parts = scatter_places(links, scatter_sum(*down_state).astype(bf16))
        in_state = scatter_first(links, *(in_sum[k] for k in range(4)))
        own_in = add_turned(scatter_second(links, *in_state))
        own_down = sum_of(down_parts)
        gwo_total, gw = lax.psum((gwo_total, gw), "z")
        gwo_other, gw_other = links.swap(gwo_total, 0, 1), links.swap(gw, 0, 1)
        grad_w_out = jnp.concatenate([by_core(gwo_total, gwo_other, core), by_core(gwo_other, gwo_total, core)])
        grad_w_qkv = turn_weights(gw, gw_other, core.astype(jnp.int32).reshape(1)).transpose(1, 0, 2)
        low_rows = gw[-bias_rows:].astype(f32)
        returned[0] = hold(returned[0], *returned[1])
    else:
        grad_w_out, gw = lax.psum((sum_of(gwo_parts).astype(bf16), gw.astype(bf16)), links.row_axes)
        grad_w_qkv = gw[:, :-bias_rows].astype(f32).reshape(3 * cols, width).T.reshape(width, 3, cols)
        low_rows = gw[0, -bias_rows:].astype(f32)
    parts = []
    for (low, size), pieces in zip(chunks, returned):
        total = grad_res.reshape(rows, part, width)[low : low + size]
        for piece in pieces:
            total = total + piece.astype(f32)
        parts.append(total)
    tokens_grad = jnp.concatenate(parts)
    grad_b_qv = jnp.stack([low_rows[0, :cols], low_rows[0, 2 * cols : 3 * cols]])
    totals = low_rows[1:]
    grad_b_in = lax.dynamic_slice_in_dim(totals[6 : 6 + shards * shard // width].reshape(-1), place * shard, shard)
    return (
        layer_out.reshape(rows, part, width),
        raw_logits,
        tokens_grad,
        prev_grad,
        grad_w_qkv,
        grad_b_qv,
        grad_w_out.astype(f32),
        totals[5],
        totals[3],
        totals[4],
        own_in,
        grad_b_in,
        own_down.astype(f32),
        totals[2],
        totals[0],
        totals[1],
    )


def solution(mesh):
    nh, nr = mesh.shape["head"], mesh.shape["row"]
    if (nh, nr) == (4, 8):
        head, row = ("y", "x"), ("z", "core")
        mesh = Mesh(mesh.devices.reshape(2, 2, 4, 2), head + row)
    else:
        head, row = ("head",), ("row",)
    every = head + row
    placed = (
        P(row, head, None),
        P(row, head, None, None),
        P(row, None),
        P(None, None, head),
        P(None, head),
        P(head, None),
        P(),
        P(),
        P(),
        P(None, every),
        P(every),
        P(every, None),
        P(),
        P(),
        P(),
        P(row, head, None),
        P(row, head, None, None),
    )
    return jax.shard_map(
        functools.partial(per_device, Links(head, row, nh, nr)),
        mesh=mesh,
        in_specs=placed,
        out_specs=(
            P(row, head, None),
            P(row, head, None, None),
            P(row, head, None),
            P(row, head, None, None),
            P(None, None, head),
            P(None, head),
            P(head, None),
            P(),
            P(),
            P(),
            P(None, every),
            P(every),
            P(every, None),
            P(),
            P(),
            P(),
        ),
        check_vma=False,
    )
```

```python
import functools

import jax
import jax.numpy as jnp
from jax import lax
from jax.experimental import pallas as pl
from jax.experimental.pallas import tpu as pltpu
from jax.sharding import Mesh
from jax.sharding import PartitionSpec as P

norm_eps = 1e-12
masked_fill = -1000000000.0
head_dim = 64
hidden_block = 512
bias_rows = 16
bf16 = jnp.bfloat16
f32 = jnp.float32


def dot_nn(a, b):
    return lax.dot_general(a, b, (((1,), (0,)), ((), ())), preferred_element_type=f32)


def dot_nt(a, b):
    return lax.dot_general(a, b, (((1,), (1,)), ((), ())), preferred_element_type=f32)


def dot_tn(a, b):
    return lax.dot_general(a, b, (((0,), (0,)), ((), ())), preferred_element_type=f32)


def params(limit_mib=60):
    return pltpu.CompilerParams(
        dimension_semantics=("arbitrary",), vmem_limit_bytes=limit_mib * 1024 * 1024
    )


def cost(flops, nbytes, exps=0):
    return pl.CostEstimate(flops=int(flops), bytes_accessed=int(nbytes), transcendentals=int(exps))


def whole(shape):
    return pl.BlockSpec(shape, lambda *_: (0,) * len(shape))


def by_step(shape, axis=0):
    return pl.BlockSpec(shape, lambda t, *_: tuple(t if d == axis else 0 for d in range(len(shape))))


def norm_parts(values):
    center = jnp.mean(values, axis=-1, keepdims=True)
    offset = values - center
    inverse = lax.rsqrt(jnp.mean(offset * offset, axis=-1, keepdims=True) + norm_eps)
    return offset * inverse, inverse


def norm_back(grad_in, unit_vals, inverse, gain_vec):
    scaled = grad_in * gain_vec
    return inverse * (
        scaled
        - jnp.mean(scaled, axis=-1, keepdims=True)
        - unit_vals * jnp.mean(scaled * unit_vals, axis=-1, keepdims=True)
    )


def lane_halves():
    lane = lax.broadcasted_iota(jnp.int32, (1, 2 * head_dim), 1)
    return lane < head_dim


def attend(me, first, pieces, w_flat, bias_row, seg_row, prev, raw_so_far):
    total_rows, heads, slots, _ = prev.shape
    rows, _, width = pieces[0][2].shape
    cols = heads * head_dim
    nh = len({k for k, _, _ in pieces})
    part = slots // nh
    scale = head_dim ** (-0.5)
    np_ = len(pieces)
    places = [(k, off, p.shape[1]) for k, off, p in pieces]
    chained = raw_so_far is not None

    def body(me_ref, *refs):
        toks = refs[:np_]
        w_ref, b_ref, sr_ref, prev_ref = refs[np_ : np_ + 4]
        outs = refs[np_ + 4 + chained :]
        qkv_ref, raw_ref, tok_all, lse_ref = outs[:4]
        ctx_refs = outs[4 : 4 + nh]
        ctx_all = outs[4 + nh]
        mine = me_ref[0]
        for ref, (k, off, size) in zip(toks, places):
            tok_all[0, pl.ds(pl.multiple_of((mine ^ k) * part + off, size), size), :] = ref[0]
        for c in range(3):
            at = slice(c * cols, (c + 1) * cols)
            qkv_ref[0, :, at] = (dot_nn(tok_all[0], w_ref[c]) + b_ref[:, at]).astype(bf16)
        low_half = lane_halves()
        keep = [jnp.where(low_half, scale, 0.0).astype(bf16), jnp.where(low_half, 0.0, scale).astype(bf16)]
        lane = lax.broadcasted_iota(jnp.int32, (1, 128), 1)
        same = jnp.broadcast_to(sr_ref[0], (8, slots)).T[:, 0:1] == sr_ref[0]
        lse_tile = jnp.zeros((slots, 128), f32)
        for pair in range(heads // 2):
            span = slice(pair * 128, pair * 128 + 128)
            q_pair = qkv_ref[0, :, span]
            k_pair = qkv_ref[0, :, cols + pair * 128 : cols + pair * 128 + 128]
            v_pair = qkv_ref[0, :, 2 * cols + pair * 128 : 2 * cols + pair * 128 + 128]
            outs = []
            for half in range(2):
                h = 2 * pair + half
                raw = dot_nt(q_pair * keep[half], k_pair) + prev_ref[0, h].astype(f32)
                raw_ref[0, h] = raw.astype(bf16)
                masked = jnp.where(same, raw, masked_fill)
                top = jnp.max(masked, axis=-1, keepdims=True)
                grown = jnp.exp(masked - top)
                total = jnp.sum(grown, axis=-1, keepdims=True)
                probs = (grown * (1.0 / total)).astype(bf16)
                outs.append(dot_nn(probs, v_pair))
                lse_tile = jnp.where(lane == h, top + jnp.log(total), lse_tile)
            ctx_all[:, span] = jnp.where(low_half, outs[0], outs[1]).astype(bf16)
        lse_ref[0] = lse_tile
        for k in range(nh):
            ctx_refs[k][0] = ctx_all[pl.ds(pl.multiple_of((mine ^ k) * part, part), part), :]

    def shifted(shape):
        return pl.BlockSpec(shape, lambda r, *_: (first + r,) + (0,) * (len(shape) - 1))

    return pl.pallas_call(
        body,
        grid_spec=pltpu.PrefetchScalarGridSpec(
            num_scalar_prefetch=1,
            grid=(rows,),
            in_specs=[by_step((1,) + p.shape[1:]) for _, _, p in pieces]
            + [
                whole((3, width, cols)),
                whole((1, 3 * cols)),
                shifted((1, 1, slots)),
                shifted((1, heads, slots, slots)),
            ]
            + [pl.BlockSpec(memory_space=pl.ANY)] * chained,
            out_specs=[
                by_step((1, slots, 3 * cols)),
                shifted((1, heads, slots, slots)),
                by_step((1, slots, width)),
                by_step((1, slots, 128)),
            ]
            + [by_step((1, part, cols))] * nh,
            scratch_shapes=[pltpu.VMEM((slots, cols), bf16)],
        ),
        out_shape=[
            jax.ShapeDtypeStruct((rows, slots, 3 * cols), bf16),
            jax.ShapeDtypeStruct((total_rows, heads, slots, slots), bf16),
            jax.ShapeDtypeStruct((rows, slots, width), bf16),
            jax.ShapeDtypeStruct((rows, slots, 128), f32),
        ]
        + [jax.ShapeDtypeStruct((rows, part, cols), bf16)] * nh,
        input_output_aliases={np_ + 5: 1} if chained else {},
        compiler_params=params(),
        cost_estimate=cost(
            2 * rows * slots * cols * (3 * width + 2 * slots), 5 * rows * heads * slots * slots, rows * heads * slots * slots
        ),
        name="attend",
    )(me, *[p for _, _, p in pieces], w_flat, bias_row, seg_row, prev, *([raw_so_far] if chained else []))


def attend_back(me, first, tok, ctx_grads, qkv, prev, logit_grad, seg_row, lse, w_flat, start_sums, so_far):
    total_rows, heads, slots, _ = prev.shape
    nh = len(ctx_grads)
    rows, _, width = tok.shape
    part = slots // nh
    cols = heads * head_dim
    half_rows = 3 * cols // 2
    scale = head_dim ** (-0.5)
    chained = so_far is not None

    def body(me_ref, *refs):
        grads = refs[:nh]
        tok_ref, qkv_ref, prev_ref, lg_ref, sr_ref, lse_ref, w_ref, sums_ref = refs[nh : nh + 8]
        rest = refs[nh + 8 :]
        if chained:
            gw_before = rest[1]
            rest = rest[2:]
        pg_ref, gw_ref = rest[:2]
        in_refs = rest[2 : 2 + nh]
        go_all, p_all, dt_all, in_all = rest[2 + nh :]
        mine = me_ref[0]
        for k in range(nh):
            go_all[pl.ds(pl.multiple_of((mine ^ k) * part, part), part), :] = grads[k][0]
        low_half = lane_halves()
        keep_q = [jnp.where(low_half, scale, 0.0).astype(bf16), jnp.where(low_half, 0.0, scale).astype(bf16)]
        keep_g = [jnp.where(low_half, 1.0, 0.0).astype(bf16), jnp.where(low_half, 0.0, 1.0).astype(bf16)]

        same = jnp.broadcast_to(sr_ref[0], (8, slots)).T[:, 0:1] == sr_ref[0]
        for pair in range(heads // 2):
            span = slice(pair * 128, pair * 128 + 128)
            q_pair = qkv_ref[0, :, span]
            g_pair = go_all[:, span]
            k_pair = qkv_ref[0, :, cols + pair * 128 : cols + pair * 128 + 128]
            v_pair = qkv_ref[0, :, 2 * cols + pair * 128 : 2 * cols + pair * 128 + 128]
            for half in range(2):
                h = 2 * pair + half
                raw = dot_nt(q_pair * keep_q[half], k_pair) + prev_ref[0, h].astype(f32)
                probs = jnp.exp(jnp.where(same, raw, masked_fill) - lse_ref[0, :, h : h + 1])
                p_all[h] = probs.astype(bf16)
                pulled = probs * dot_nt(g_pair * keep_g[half], v_pair)
                inner = jnp.sum(pulled, axis=-1, keepdims=True)
                pg_ref[0, h] = (pulled - probs * inner + lg_ref[0, h].astype(f32)).astype(bf16)
        q_t = qkv_ref[0, :, :cols].T
        k_t = qkv_ref[0, :, cols : 2 * cols].T
        g_t = go_all[...].T
        for h in range(heads):
            span = slice(h * head_dim, h * head_dim + head_dim)
            grad_raw = pg_ref[0, h]
            dt_all[h * head_dim : (h + 1) * head_dim, :] = (dot_nt(k_t[span], grad_raw) * scale).astype(bf16)
            dt_all[cols + h * head_dim : cols + (h + 1) * head_dim, :] = (dot_nn(q_t[span], grad_raw) * scale).astype(bf16)
            dt_all[2 * cols + h * head_dim : 2 * cols + (h + 1) * head_dim, :] = dot_nn(g_t[span], p_all[h]).astype(bf16)
        grad_qkv = dt_all[...].T
        in_part = dot_nt(grad_qkv[:, :cols], w_ref[0])
        for c in range(1, 3):
            in_part = in_part + dot_nt(grad_qkv[:, c * cols : (c + 1) * cols], w_ref[c])
        in_all[...] = in_part.astype(bf16)
        for k in range(nh):
            in_refs[k][0] = in_all[pl.ds(pl.multiple_of((mine ^ k) * part, part), part), :]
        starts = pl.program_id(0) == 0

        @pl.when(starts)
        def _():
            if chained:
                gw_ref[...] = gw_before[...]
                for half in range(2):
                    gw_ref[half, half_rows:, :] += sums_ref[...]
            else:
                gw_ref[...] = jnp.zeros_like(gw_ref)

        first_row = lax.broadcasted_iota(jnp.int32, (bias_rows, 1), 0) == 0
        gb = jnp.where(first_row, dot_nn(jnp.ones((bias_rows, slots), bf16), grad_qkv), 0.0)
        for half in range(2):
            gw_ref[half, : half_rows, :] += dot_nn(dt_all[half * half_rows : (half + 1) * half_rows, :], tok_ref[0])
            gw_ref[half, half_rows:, : 3 * cols] += gb

    def shifted(shape):
        return pl.BlockSpec(shape, lambda r, *_: (first + r,) + (0,) * (len(shape) - 1))

    sums = [whole((2, half_rows + bias_rows, width))]
    return pl.pallas_call(
        body,
        grid_spec=pltpu.PrefetchScalarGridSpec(
            num_scalar_prefetch=1,
            grid=(rows,),
            in_specs=[by_step((1, part, cols))] * nh
            + [
                by_step((1, slots, width)),
                by_step((1, slots, 3 * cols)),
                shifted((1, heads, slots, slots)),
                shifted((1, heads, slots, slots)),
                shifted((1, 1, slots)),
                by_step((1, slots, 128)),
                whole((3, width, cols)),
                whole((bias_rows, width)),
            ]
            + ([pl.BlockSpec(memory_space=pl.ANY)] + sums if chained else []),
            out_specs=[shifted((1, heads, slots, slots))] + sums + [by_step((1, part, width))] * nh,
            scratch_shapes=[
                pltpu.VMEM((slots, cols), bf16),
                pltpu.VMEM((heads, slots, slots), bf16),
                pltpu.VMEM((3 * cols, slots), bf16),
                pltpu.VMEM((slots, width), bf16),
            ],
        ),
        out_shape=[
            jax.ShapeDtypeStruct((total_rows, heads, slots, slots), bf16),
            jax.ShapeDtypeStruct((2, half_rows + bias_rows, width), f32),
        ]
        + [jax.ShapeDtypeStruct((rows, part, width), bf16)] * nh,
        input_output_aliases={nh + 9: 0} if chained else {},
        compiler_params=params(),
        cost_estimate=cost(
            2 * rows * slots * cols * (6 * width + 5 * slots), 7 * rows * heads * slots * slots, rows * heads * slots * slots
        ),
        name="attend_back",
    )(me, *ctx_grads, tok, qkv, prev, logit_grad, seg_row, lse, w_flat, start_sums, *(so_far if chained else []))


def resident(shape):
    return pl.BlockSpec(shape, lambda *_: (0,) * len(shape), pipeline_mode=pl.Buffered(1))


def fold(values):
    return jnp.sum(values.reshape(values.shape[0] // 8, 8, values.shape[1]), axis=0)


def feed(ctx_pieces, w_out, tokens, vectors, bias_blocks, weights, plan, out_grad):
    count, width = tokens.shape
    nh, nc = len(ctx_pieces), len(ctx_pieces[0])
    cols = ctx_pieces[0][0].shape[1]
    sizes = [p.shape[0] for p in ctx_pieces[0]]
    blocks = len(plan)
    per_block = sum(size for _, _, size, side, _ in plan[0] if side == 0)
    shard = hidden_block // per_block
    hidden = blocks * hidden_block
    strip = 128
    nw = len(weights)
    riding = bias_blocks is None
    n_in = nh * nc + 5 - riding + nw

    def body(*refs):
        ctx = refs[: nh * nc]
        wo_ref, tok_ref, vec_ref, og_ref = refs[nh * nc : nh * nc + 4]
        bias_ref = None if riding else refs[nh * nc + 4]
        w_refs = refs[n_in - nw : n_in]
        res_out, x_out, gf_out, gres_out, low_out, act_ref, gh_ref, gb_ref, sum_ref = refs[n_in : n_in + 9]
        gc_refs = refs[n_in + 9 : n_in + 9 + nh * nc]
        gwo_ref = refs[n_in + 9 + nh * nc]
        w_all, b_all, slope, unit, inv, acc, x_low, res, gf, low, w_sem, b_sem, out_sem = refs[n_in + 10 + nh * nc :]
        t = pl.program_id(0)

        def sends(which):
            pairs = ((x_low, x_out), (res, res_out), (gf, gf_out), (acc, gres_out), (low, low_out))
            return [pltpu.make_async_copy(*pairs[i], out_sem.at[i]) for i in which]

        def strips(step, init):
            def one(i, carry):
                return step(pl.ds(pl.multiple_of(i * strip, strip), strip), carry)

            return lax.fori_loop(0, count // strip, one, init)

        @pl.when(t == 0)
        def _():
            for block, copies in enumerate(plan):
                for array, low_shard, size, side, to in copies:
                    source = w_refs[array].at[pl.ds(low_shard, size)]
                    pltpu.make_async_copy(
                        source.at[:, pl.ds(0, shard)], w_all.at[block, side, pl.ds(to, size)], w_sem.at[block]
                    ).start()
                    if riding and side:
                        pltpu.make_async_copy(
                            source.at[:, pl.ds(shard, bias_rows), pl.ds(0, shard)],
                            b_all.at[block, pl.ds(to, size)],
                            b_sem.at[block],
                        ).start()
            start = 0
            for c in range(nc):
                at = slice(start, start + sizes[c])
                start += sizes[c]
                branch = dot_nn(ctx[c][...], wo_ref[0:cols, :])
                for k in range(1, nh):
                    branch = branch + dot_nn(ctx[k * nc + c][...], wo_ref[k * cols : (k + 1) * cols, :])
                acc[at, :] = branch

            def first_norm(at, carry):
                unit_one, inverse = norm_parts(tok_ref[at, :].astype(f32) + (acc[at, :] + vec_ref[0:1, :]))
                unit[at, :] = unit_one
                inv[at, :] = jnp.broadcast_to(inverse, (strip, 128))
                normed = unit_one * vec_ref[1:2, :] + vec_ref[2:3, :]
                x_low[at, :] = normed.astype(bf16)
                acc[at, :] = normed + vec_ref[3:4, :]
                return carry

            strips(first_norm, 0)
            sends((0,))[0].start()

        @pl.when(t < blocks)
        def _():
            pltpu.make_async_copy(w_all.at[t], w_all.at[t], w_sem.at[t]).wait()
            if riding:
                pltpu.make_async_copy(b_all.at[t], b_all.at[t], b_sem.at[t]).wait()
                bias = jnp.concatenate([b_all[t, j, 0:1, :].astype(f32) for j in range(per_block)], axis=1)
            else:
                bias = bias_ref[0]
            w_in = w_all[t, 0].reshape(hidden_block, width)
            w_down = w_all[t, 1].reshape(hidden_block, width)
            for m in range(tiles):
                at = slice(m * (count // tiles), (m + 1) * (count // tiles))
                pre = dot_nt(x_low[at, :], w_in) + bias
                below = 0.5 * (1.0 + lax.erf(pre * (0.5**0.5)))
                active = (pre * below).astype(bf16)
                act_ref[at, :] = active
                slope[t, at, :] = (below + pre * (jnp.exp(-0.5 * pre * pre) * 0.3989422804014327)).astype(bf16)
                acc[at, :] += dot_nn(active, w_down)

        @pl.when(t == blocks - 1)
        def _():
            def second_norm(at, carry):
                unit_two, inverse = norm_parts(acc[at, :])
                res[at, :] = (unit_two * vec_ref[4:5, :] + vec_ref[5:6, :]).astype(bf16)
                top = og_ref[at, :].astype(f32)
                grad_two = norm_back(top, unit_two, inverse, vec_ref[4:5, :])
                acc[at, :] = grad_two
                grad_low = grad_two.astype(bf16)
                gf[at, :] = grad_low
                values = (top * unit_two, top, grad_low.astype(f32))
                return tuple(c + fold(v) for c, v in zip(carry, values))

            sums = strips(second_norm, (jnp.zeros((8, width), f32),) * 3)
            for i in range(3):
                sum_ref[i : i + 1, :] = jnp.sum(sums[i], axis=0, keepdims=True)
            for copy in sends((1, 2)):
                copy.start()

        @pl.when(t >= blocks)
        def _():
            w_in = w_all[t - blocks, 0].reshape(hidden_block, width)
            w_down = w_all[t - blocks, 1].reshape(hidden_block, width)
            total = jnp.zeros((8, hidden_block), f32)
            for m in range(tiles):
                at = slice(m * (count // tiles), (m + 1) * (count // tiles))
                grad_hidden = (dot_nt(gf[at, :], w_down) * slope[t - blocks, at, :].astype(f32)).astype(bf16)
                gh_ref[at, :] = grad_hidden
                total = total + fold(grad_hidden.astype(f32))
                acc[at, :] += dot_nn(grad_hidden, w_in)
            gb_ref[0] = jnp.sum(total, axis=0, keepdims=True)

        @pl.when(t == 2 * blocks - 1)
        def _():
            def first_back(at, carry):
                grad_one = acc[at, :]
                unit_one = unit[at, :]
                grad_res = norm_back(grad_one, unit_one, inv[at, 0:1], vec_ref[1:2, :])
                acc[at, :] = grad_res
                grad_low = grad_res.astype(bf16)
                low[at, :] = grad_low
                values = (grad_one * unit_one, grad_one, grad_low.astype(f32))
                return tuple(c + fold(v) for c, v in zip(carry, values))

            sums = strips(first_back, (jnp.zeros((8, width), f32),) * 3)
            for i in range(3):
                sum_ref[3 + i : 4 + i, :] = jnp.sum(sums[i], axis=0, keepdims=True)
            sum_ref[6:8, :] = jnp.zeros((2, width), f32)
            for copy in sends((3, 4)):
                copy.start()
            for k in range(nh):
                grad_ctx = dot_nt(low[...], wo_ref[k * cols : (k + 1) * cols, :]).astype(bf16)
                start = 0
                for c in range(nc):
                    gc_refs[k * nc + c][...] = grad_ctx[start : start + sizes[c]]
                    start += sizes[c]
            for k in range(nh):
                value, start = 0.0, 0
                for c in range(nc):
                    value = value + dot_tn(ctx[k * nc + c][...], low[start : start + sizes[c], :])
                    start += sizes[c]
                gwo_ref[k] = value.astype(bf16)
            for copy in sends(range(5)):
                copy.wait()

    tiles = 1
    anywhere = pl.BlockSpec(memory_space=pl.ANY)
    return pl.pallas_call(
        body,
        grid=(2 * blocks,),
        in_specs=[resident(p.shape) for k in ctx_pieces for p in k]
        + [
            resident(w_out.shape),
            resident((count, width)),
            resident((8, width)),
            resident((count, width)),
        ]
        + [pl.BlockSpec((1, 1, hidden_block), lambda t: (jnp.minimum(t, blocks - 1), 0, 0))] * (not riding)
        + [anywhere] * nw,
        out_specs=[anywhere] * 5
        + [
            pl.BlockSpec((count, hidden_block), lambda t: (0, jnp.minimum(t, blocks - 1))),
            pl.BlockSpec((count, hidden_block), lambda t: (0, jnp.maximum(t - blocks, 0))),
            pl.BlockSpec((1, 1, hidden_block), lambda t: (jnp.maximum(t - blocks, 0), 0, 0)),
            whole((8, width)),
        ]
        + [whole((n, cols)) for _ in range(nh) for n in sizes]
        + [resident((nh, cols, width))],
        out_shape=[
            jax.ShapeDtypeStruct((count, width), bf16),
            jax.ShapeDtypeStruct((count, width), bf16),
            jax.ShapeDtypeStruct((count, width), bf16),
            jax.ShapeDtypeStruct((count, width), f32),
            jax.ShapeDtypeStruct((count, width), bf16),
            jax.ShapeDtypeStruct((count, hidden), bf16),
            jax.ShapeDtypeStruct((count, hidden), bf16),
            jax.ShapeDtypeStruct((blocks, 1, hidden_block), f32),
            jax.ShapeDtypeStruct((8, width), f32),
        ]
        + [jax.ShapeDtypeStruct((n, cols), bf16) for _ in range(nh) for n in sizes]
        + [jax.ShapeDtypeStruct((nh, cols, width), bf16)],
        scratch_shapes=[
            pltpu.VMEM((blocks, 2, per_block, shard, width), bf16),
            pltpu.VMEM((blocks, per_block, bias_rows, shard), bf16),
            pltpu.VMEM((blocks, count, hidden_block), bf16),
            pltpu.VMEM((count, width), f32),
            pltpu.VMEM((count, 128), f32),
            pltpu.VMEM((count, width), f32),
            pltpu.VMEM((count, width), bf16),
            pltpu.VMEM((count, width), bf16),
            pltpu.VMEM((count, width), bf16),
            pltpu.VMEM((count, width), bf16),
            pltpu.SemaphoreType.DMA((blocks,)),
            pltpu.SemaphoreType.DMA((blocks,)),
            pltpu.SemaphoreType.DMA((5,)),
        ],
        compiler_params=params(),
        cost_estimate=cost(4 * count * width * (2 * hidden + width), 4 * hidden * (width + count), 2 * count * hidden),
        name="feed",
    )(*[p for k in ctx_pieces for p in k], w_out, tokens, vectors, out_grad, *([] if riding else [bias_blocks]), *weights)


def weight_grad(left, right, blocks, stride, first, shard, by_place, addend):
    count, width = right.shape
    per_block = hidden_block // shard
    adding = addend is not None
    if by_place:
        spec = pl.BlockSpec((per_block, None, shard, width), lambda t: (0, t, 0, 0))
        shape = (per_block, blocks, shard, width)
    else:
        spec = pl.BlockSpec((None, per_block, shard, width), lambda t: (t, 0, 0, 0))
        shape = (blocks, per_block, shard, width)

    def body(left_ref, right_ref, *refs):
        value = dot_tn(left_ref[...], right_ref[...]).reshape(per_block, shard, width)
        if adding:
            value = value + refs[0][...].astype(f32)
        refs[-1][...] = value.astype(bf16)

    return pl.pallas_call(
        body,
        grid=(blocks,),
        in_specs=[pl.BlockSpec((count, hidden_block), lambda t: (0, first + stride * t)), whole((count, width))]
        + [spec] * adding,
        out_specs=spec,
        out_shape=jax.ShapeDtypeStruct(shape, bf16),
        input_output_aliases={2: 0} if adding else {},
        compiler_params=params(),
        cost_estimate=cost(2 * count * width * hidden_block * blocks, 4 * hidden_block * blocks * (width + count)),
        name="weight_grad",
    )(left, right, *([addend] if adding else []))


def add_turned(pieces):
    def body(*refs):
        refs[-1][...] = sum_of([r[...] for r in refs[:-1]]).T

    rows, width = pieces[0].shape
    return pl.pallas_call(
        body,
        out_shape=jax.ShapeDtypeStruct((width, rows), f32),
        compiler_params=pltpu.CompilerParams(vmem_limit_bytes=32 * 1024 * 1024),
        name="add_turned",
    )(*pieces)


def turn_weights(mine, other, core):
    half, width = mine.shape
    half -= bias_rows
    cols = 2 * half // 3

    def body(core_ref, mine_ref, other_ref, out_ref, all_rows):
        @pl.when(core_ref[0] == 0)
        def _():
            all_rows[0:half, :] = mine_ref[0:half, :].astype(f32)
            all_rows[half : 2 * half, :] = other_ref[0:half, :].astype(f32)

        @pl.when(core_ref[0] != 0)
        def _():
            all_rows[0:half, :] = other_ref[0:half, :].astype(f32)
            all_rows[half : 2 * half, :] = mine_ref[0:half, :].astype(f32)

        for c in range(3):
            out_ref[c] = all_rows[c * cols : (c + 1) * cols, :].T

    return pl.pallas_call(
        body,
        grid_spec=pltpu.PrefetchScalarGridSpec(
            num_scalar_prefetch=1,
            grid=(1,),
            in_specs=[whole(mine.shape)] * 2,
            out_specs=whole((3, width, cols)),
            scratch_shapes=[pltpu.VMEM((2 * half, width), f32)],
        ),
        out_shape=jax.ShapeDtypeStruct((3, width, cols), f32),
        compiler_params=params(),
        name="turn_weights",
    )(core, mine, other)


class Links:
    def __init__(self, head_axes, row_axes, nh, nr):
        self.head_axes, self.row_axes, self.nh, self.nr = head_axes, row_axes, nh, nr
        self.axes = head_axes + row_axes
        self.factored = len(row_axes) == 2

    def swap(self, value, head_bits=0, row_bits=0):
        mask = head_bits * self.nr + row_bits
        return lax.ppermute(value, self.axes, [(i, i ^ mask) for i in range(self.nh * self.nr)])

    def sum_rows(self, value):
        bit = 1
        while bit < self.nr:
            value = value + self.swap(value, 0, bit)
            bit *= 2
        return value

    def sum_heads(self, value):
        bit = 1
        while bit < self.nh:
            value = value + self.swap(value, bit, 0)
            bit *= 2
        return value

    def sum_all(self, value):
        return self.sum_heads(self.sum_rows(value))


def after(value, *others):
    return lax.optimization_barrier((value, *others))[0]


def gather_tokens(links, tokens, chunks, small, early):
    own = [tokens[low : low + size] for low, size in chunks]
    if links.nh != 4:
        return [[(0, 0, t)] + [(k, 0, links.swap(t, k)) for k in range(1, links.nh)] for t in own], None
    result, others, gate = [], None, ()
    for mine in own:
        mine = after(mine, *gate)
        half = mine.shape[1] // 2
        beside, across = links.swap(mine, 1), links.swap(mine, 2)
        if others is None:
            others = exchange(links, small)
            beside, across = hold((beside, across), *early)
        else:
            beside, across = hold((beside, across), *far)
        far = links.swap(across[:, :half], 1), links.swap(beside[:, half:], 2)
        gate = (beside, across)
        result.append([(0, 0, mine), (1, 0, beside), (2, 0, across), (3, 0, far[0]), (3, half, far[1])])
    return result, others


def exchange_first(links, mine):
    return mine, links.swap(mine, 1), links.swap(mine, 2)


def exchange_second(links, mine, beside, across):
    half = mine.shape[0] // 2
    return mine, beside, across, links.swap(across[:half], 1), links.swap(beside[half:], 2)


def exchange(links, mine):
    return exchange_second(links, *exchange_first(links, mine))


def hold(values, *others):
    flat, tree = jax.tree.flatten(values)
    return jax.tree.unflatten(tree, lax.optimization_barrier((*flat, *others))[: len(flat)])


def all_weights(links, in_all, column, beside, across, low, high):
    mine = [in_all, column, beside, across, low, high]
    arrays = mine + [links.swap(a, 0, 1) for a in mine]
    plan = []
    for k in range(4):
        for base in (0, 6):
            copies = [(base, z * 4 + k, 1, 0, z) for z in range(4)]
            if k < 3:
                copies.append((base + 1 + k, 0, 4, 1, 0))
            else:
                copies += [(base + 4, 0, 2, 1, 0), (base + 5, 0, 2, 1, 2)]
            plan.append(copies)
    return arrays, plan


def by_core(first, second, core):
    return jnp.where(core == 0, first, second)


def add_low(a, b):
    return (a.astype(f32) + b.astype(f32)).astype(bf16)


def scatter_first(links, own, beside, across, far):
    half = far.shape[0] // 2
    return own, beside, across, links.swap(far[:half], 1), links.swap(far[half:], 2)


def scatter_second(links, own, beside, across, for_across, for_beside):
    half = for_across.shape[0]
    across = jnp.concatenate([add_low(across[:half], for_across), across[half:]])
    beside = jnp.concatenate([beside[:half], add_low(beside[half:], for_beside)])
    return own, links.swap(beside, 1), links.swap(across, 2)


def scatter_sum(own, beside, across):
    return own.astype(f32) + beside.astype(f32) + across.astype(f32)


def scatter_places(links, total):
    here = lax.axis_index("z")
    pieces = [lax.dynamic_index_in_dim(total, here ^ k, keepdims=False) for k in range(4)]
    return [pieces[0]] + [links.swap(pieces[k], 0, 2 * k) for k in range(1, 4)]


def sum_of(pieces):
    total = pieces[0].astype(f32)
    for piece in pieces[1:]:
        total = total + piece.astype(f32)
    return total


def core_half(links, value, axis):
    core = lax.axis_index("core")
    size = value.shape[axis] // 2
    keep = lax.dynamic_slice_in_dim(value, core * size, size, axis)
    give = lax.dynamic_slice_in_dim(value, (1 - core) * size, size, axis)
    return keep.astype(f32) + links.swap(give.astype(bf16), 0, 1).astype(f32)


def per_device(
    links,
    tokens,
    prev_logits,
    segment_ids,
    w_qkv,
    b_qv,
    w_out,
    b_out,
    ln1_gain,
    ln1_shift,
    w_in,
    b_in,
    w_down,
    b_down,
    ln2_gain,
    ln2_shift,
    out_grad,
    logit_grad,
):
    rows, part, width = tokens.shape
    heads = prev_logits.shape[1]
    cols = heads * head_dim
    shard = w_in.shape[1]
    count = rows * part
    nh, nr = links.nh, links.nr
    me = lax.axis_index(links.head_axes).astype(jnp.int32).reshape(1)
    place = lax.axis_index(links.axes)
    chunks = [(0, rows // 2), (rows // 2, rows - rows // 2)]

    bias_qv = b_qv.astype(f32)
    bias_row = jnp.concatenate([bias_qv[0], jnp.zeros_like(bias_qv[0]), bias_qv[1]])[None]
    w_flat = w_qkv.transpose(1, 0, 2)
    seg_row = segment_ids[:, None, :]
    shards = nh * nr
    blocks = shards * shard // hidden_block
    core = lax.axis_index("core") if links.factored else 0
    if links.factored:
        here_h = lax.axis_index(links.head_axes)
        bias_blocks = None
        bias_row_in = jnp.pad(b_in[None], ((0, bias_rows - 1), (0, width - shard)))
        column = lax.all_gather(jnp.concatenate([w_down, bias_row_in])[None], "z", axis=0, tiled=True)
        out_half = lax.dynamic_slice_in_dim(w_out, core * (cols // 2), cols // 2)
        small = jnp.concatenate([w_in.T, out_half])
    else:
        mine = lax.broadcasted_iota(jnp.int32, (shards, 1), 0) == place
        bias_all = links.sum_all(jnp.where(mine, b_in.astype(f32)[None], 0.0))
        bias_blocks = bias_all.reshape(-1, 1, hidden_block)
        small = None
    vectors = jnp.stack(
        [
            b_out.astype(f32),
            ln1_gain,
            ln1_shift,
            b_down.astype(f32),
            ln2_gain,
            ln2_shift,
            jnp.zeros_like(ln1_gain),
            jnp.zeros_like(ln1_gain),
        ]
    )

    early = (bias_row, vectors)
    tok_pieces, others = gather_tokens(links, tokens, chunks, small, early)
    if links.factored:
        rows_in = [others[0][:shard], others[1][:shard], others[2][:shard], others[3]]
        in_all = lax.all_gather(
            after(jnp.stack(rows_in), column, *(p for _, _, p in tok_pieces[0][1:3])), "z", axis=0, tiled=True
        )
        arrived = [p for _, _, p in tok_pieces[1][1:3]]
        tok_pieces[0] = hold(tok_pieces[0], *arrived)
        tok_pieces[0] = [(k, off, p) for (k, off, _), (_, _, p) in zip(tok_pieces[1], tok_pieces[0])]
        tok_pieces[1] = [(k, off, after(p, others[4]) if k in (1, 2) else p) for k, off, p in tok_pieces[1]]
        weight_pieces = exchange_first(links, after(column, *arrived, others[4]))

    raw_logits, saved, ctx_pieces = None, [], [[] for _ in range(nh)]
    for c, ((low, size), pieces) in enumerate(zip(chunks, tok_pieces)):
        if c and links.factored:
            weight_pieces = hold(weight_pieces, raw_logits_gate)
            weight_pieces = exchange_second(links, *weight_pieces)
            near = weight_pieces[1:3]
            pieces = [(k, off, after(p, *near) if k == 3 else p) for k, off, p in pieces]
        qkv, raw_logits, tok_all, lse, *ctx = attend(
            me, low, pieces, w_flat, bias_row, seg_row, prev_logits, raw_logits
        )
        raw_logits_gate = ctx[0]
        saved.append((qkv, tok_all, lse))
        if c and links.factored:
            ctx = hold(ctx, *(p[0] for p in ctx_pieces), *weight_pieces[3:])
        for k in range(nh):
            piece = links.swap(ctx[k], k) if k else ctx[k]
            ctx_pieces[k].append(piece.reshape(size * part, cols))
    if links.factored:
        weights, plan = all_weights(links, *hold([in_all, *weight_pieces], raw_logits_gate, *(p[0] for p in ctx_pieces)))
        rows_out = jnp.stack([others[0][shard:], others[1][shard:], others[2][shard:], others[4]])
        rows_out = after(rows_out, raw_logits_gate, *(p[0] for p in ctx_pieces))
        theirs = links.swap(rows_out, 0, 1)
        w_out_all = jnp.stack([by_core(rows_out, theirs, core), by_core(theirs, rows_out, core)], axis=1)
        w_out_all = w_out_all.reshape(nh * cols, width)
    else:
        weights = [lax.all_gather(a[None], links.axes, axis=0, tiled=True) for a in (w_in.T, w_down)]
        per_block = hidden_block // shard
        plan = [[(side, t * per_block, per_block, side, 0) for side in range(2)] for t in range(blocks)]
        w_out_all = jnp.concatenate([w_out] + [links.swap(w_out, k) for k in range(1, nh)])
    layer_out, x_low, grad_ffn, grad_res, grad_low, active, grad_hidden, gb_in, norm_sums, *rest = feed(
        ctx_pieces,
        w_out_all,
        tokens.reshape(count, width),
        vectors,
        bias_blocks,
        weights,
        plan,
        out_grad.reshape(count, width),
    )
    ctx_grad, gwo = rest[:-1], rest[-1]
    nc = len(chunks)

    def send_ctx(c, *others):
        pieces = hold([ctx_grad[k * nc + c] for k in range(nh)], *others)
        return [(links.swap(p, k) if k else p).reshape(chunks[c][1], part, cols) for k, p in enumerate(pieces)]

    gb_in = gb_in.reshape(shards, shard)
    if links.factored:
        seq = jnp.arange(shards)
        gb_in = gb_in[((seq // nr) ^ here_h) * 8 + ((seq % 2) ^ core) * 4 + (seq % nr) // 2]
    sums = jnp.concatenate([norm_sums[:6], gb_in.reshape(-1, width)])
    ctx_grads = [send_ctx(0)]
    sums = jnp.pad(sums, ((1, bias_rows - 1 - sums.shape[0]), (0, 0)))
    if links.factored:

        def core_swap(g):
            return links.swap(g.reshape(-1, shard, width), 0, 1).reshape(g.shape)

        half = (blocks // 2, 2)
        down_theirs = weight_grad(active, grad_ffn, *half, 1, shard, False, None)
        sums = sums + links.swap(sums, 1)
        down_swapped = core_swap(after(down_theirs, sums, *ctx_grads[0]))
        ctx_grads.append(send_ctx(1, *ctx_grads[0]))
        in_theirs = weight_grad(after(grad_hidden, down_theirs, sums, *ctx_grads[0]), x_low, *half, 1, shard, True, None)
        gwo = core_half(links, after(gwo, down_theirs), 1).astype(bf16)
        in_swapped = core_swap(in_theirs)
        sums = after(sums, down_theirs)
        sums = sums + links.swap(sums, 2)
        gwo_parts = [gwo[0]] + [links.swap(gwo[k], k) for k in range(1, nh)]
        down_own = weight_grad(after(active, in_swapped, sums, gwo, *ctx_grads[1]), grad_ffn, *half, 0, shard, False, down_swapped)
        down_state = scatter_first(links, *(down_own[k] for k in range(4)))
        in_own = weight_grad(after(grad_hidden, down_own, *gwo_parts), x_low, *half, 0, shard, True, in_swapped)
        in_own = after(in_own, *down_state[3:])
        in_sum = lax.psum_scatter(in_own.reshape(-1, shard, width), "z", scatter_dimension=0, tiled=True)
        ctx_grads[0] = hold(ctx_grads[0], in_own)
        down_state = scatter_second(links, *hold(down_state, in_own))
    else:
        ctx_grads.append(send_ctx(1))
        own = [
            weight_grad(left, right, blocks, 1, 0, shard, False, None)
            for left, right in ((grad_hidden, x_low), (active, grad_ffn))
        ]
        own_in, own_down = (
            lax.psum_scatter(g.reshape(-1, shard, width), links.axes, scatter_dimension=0, tiled=True)[0] for g in own
        )
        own_in = own_in.astype(f32).T
        gwo_parts = [gwo[0]] + [links.swap(gwo[k], k) for k in range(1, nh)]
        sums = links.sum_heads(sums)

    so_far, returned = None, []
    for c, (low, size) in enumerate(chunks):
        qkv, tok_all, lse = saved[c]
        if links.factored and c:
            gwo_total = sum_of(hold(gwo_parts, gw)).astype(bf16)
            ctx_grads[c] = hold(ctx_grads[c], gwo_total, sums)
        prev_grad, gw, *input_part = attend_back(
            me, low, tok_all, ctx_grads[c], qkv, prev_logits, logit_grad, seg_row, lse, w_flat, sums, so_far
        )
        so_far = (prev_grad, gw)
        if links.factored:
            if c:
                gw = core_half(links, after(gw, *returned[0]), 0)[0].astype(bf16)
                gw, in_sum = hold((gw, in_sum))
                input_part = hold(input_part, gw)
            else:
                input_part = hold(input_part, *down_state[1:])
        returned.append([input_part[0]] + [links.swap(input_part[k], k) for k in range(1, nh)])
    if links.factored:
        down_state = hold(down_state, *returned[1][1:3])
        in_sum = after(in_sum, *returned[1])
        down_parts = scatter_places(links, scatter_sum(*down_state).astype(bf16))
        in_state = scatter_first(links, *(in_sum[k] for k in range(4)))
        own_in = add_turned(scatter_second(links, *in_state))
        own_down = sum_of(down_parts)
        gwo_total, gw = lax.psum((gwo_total, gw), "z")
        gwo_other, gw_other = links.swap(gwo_total, 0, 1), links.swap(gw, 0, 1)
        grad_w_out = jnp.concatenate([by_core(gwo_total, gwo_other, core), by_core(gwo_other, gwo_total, core)])
        grad_w_qkv = turn_weights(gw, gw_other, core.astype(jnp.int32).reshape(1)).transpose(1, 0, 2)
        low_rows = gw[-bias_rows:].astype(f32)
        returned[0] = hold(returned[0], *returned[1])
    else:
        grad_w_out, gw = lax.psum((sum_of(gwo_parts).astype(bf16), gw.astype(bf16)), links.row_axes)
        grad_w_qkv = gw[:, :-bias_rows].astype(f32).reshape(3 * cols, width).T.reshape(width, 3, cols)
        low_rows = gw[0, -bias_rows:].astype(f32)
    parts = []
    for (low, size), pieces in zip(chunks, returned):
        total = grad_res.reshape(rows, part, width)[low : low + size]
        for piece in pieces:
            total = total + piece.astype(f32)
        parts.append(total)
    tokens_grad = jnp.concatenate(parts)
    grad_b_qv = jnp.stack([low_rows[0, :cols], low_rows[0, 2 * cols : 3 * cols]])
    totals = low_rows[1:]
    grad_b_in = lax.dynamic_slice_in_dim(totals[6 : 6 + shards * shard // width].reshape(-1), place * shard, shard)
    return (
        layer_out.reshape(rows, part, width),
        raw_logits,
        tokens_grad,
        prev_grad,
        grad_w_qkv,
        grad_b_qv,
        grad_w_out.astype(f32),
        totals[5],
        totals[3],
        totals[4],
        own_in,
        grad_b_in,
        own_down.astype(f32),
        totals[2],
        totals[0],
        totals[1],
    )


def solution(mesh):
    nh, nr = mesh.shape["head"], mesh.shape["row"]
    if (nh, nr) == (4, 8):
        head, row = ("y", "x"), ("z", "core")
        mesh = Mesh(mesh.devices.reshape(2, 2, 4, 2), head + row)
    else:
        head, row = ("head",), ("row",)
    every = head + row
    placed = (
        P(row, head, None),
        P(row, head, None, None),
        P(row, None),
        P(None, None, head),
        P(None, head),
        P(head, None),
        P(),
        P(),
        P(),
        P(None, every),
        P(every),
        P(every, None),
        P(),
        P(),
        P(),
        P(row, head, None),
        P(row, head, None, None),
    )
    return jax.shard_map(
        functools.partial(per_device, Links(head, row, nh, nr)),
        mesh=mesh,
        in_specs=placed,
        out_specs=(
            P(row, head, None),
            P(row, head, None, None),
            P(row, head, None),
            P(row, head, None, None),
            P(None, None, head),
            P(None, head),
            P(head, None),
            P(),
            P(),
            P(),
            P(None, every),
            P(every),
            P(every, None),
            P(),
            P(),
            P(),
        ),
        check_vma=False,
    )
```
